32 devices in a mesh: slides: 2 (over y), rows: 8 (over z, x), cols: 2 (over core).
Axes of the slice: x: 2, y: 2, z: 4, core: 2. Of those that a mesh axis runs over, the one named last changes fastest.
Arguments:
- tokens: bfloat16 [512, 32, 512], P(('slides', 'cols'), 'rows'), parts along dimension 0, may hold values from -6 to 6
- norm_gain: float32 [512], replicated, may hold values from 0.5 to 1.5
- w_in: bfloat16 [512, 2048], replicated, may hold values from -0.25 to 0.25
- w_bc: bfloat16 [512, 64], replicated, may hold values from -0.046875 to 0.046875
- rate_row: float32 [16, 1024], replicated, may hold values from 0.002 to 0.08
- rate_col: float32 [16, 1024], replicated, may hold values from 0.002 to 0.08
- skip_gain: float32 [1024], replicated, may hold values from 0.5 to 1.5
- w_out: bfloat16 [1024, 512], replicated, may hold values from -0.1875 to 0.1875
Outputs:
- mixed: bfloat16 [512, 32, 512], P(('slides', 'cols'), 'rows'), parts along dimension 0
The draws below stay inside these ranges and needn't reach their ends.
There are 2 independent parts, one for each index of `slides`. The reference program is written for one: setup_inputs(seed, part) draws one part's arguments, and reference() takes and returns one part's arrays. A program takes and returns all parts, laid end to end along the dimension named above; an argument that names none is the same for every part. Nothing has to cross between parts.
All inputs are finite; a program needn't handle non-finite values.
Results may differ from the reference program's by a relative error of at most 0.013.
Values may be sent and summed in bfloat16 or wider, within the bound.
A program may use at most 64 MiB of HBM per device.

```python
import math
import jax
import jax.numpy as jnp
from jax import lax

D = 512
E = 1024
N = 16
H = 256
W = 32


def block_levels(stream_key, extent, split, least, top_value):
    factor_of = 1.0
    for position, parts in split:
        draws = jax.random.uniform(jax.random.fold_in(jax.random.fold_in(stream_key, 6), position), (parts,), jnp.float32, least / len(split), top_value / len(split))
        factor_of = factor_of * jnp.repeat(jnp.exp(draws), extent[position] // parts).reshape((-1,) + (1,) * (len(extent) - 1 - position))
    return factor_of


def centred(own_key, dims, deviation, limit, cuts=(), dtype=jnp.bfloat16):
    entries = jax.random.normal(own_key, dims, jnp.float32) * deviation
    if len(cuts) > 0:
        entries = block_levels(own_key, dims, cuts, -0.22, 0.18) * entries
    return jnp.clip(entries, min=-limit, max=limit).astype(dtype)


def setup_inputs(seed: int = 0, part: int = 0) -> dict:
    arg_keys = jax.random.split(jax.random.key(seed), 9)
    own_keys = jax.random.split(jax.random.fold_in(arg_keys[8], part), 9)
    tokens = centred(own_keys[0], (H, W, D), 1.0, 6.0, ((0, 2), (1, 8)))
    norm_gain = jnp.clip(1.0 + 0.1 * jax.random.normal(arg_keys[1], (D,), jnp.float32), 0.5, 1.5)
    w_in = centred(arg_keys[2], (D, 2 * E), D ** -0.5, 0.25)
    w_bc = centred(arg_keys[3], (D, 4 * N), (32 * D) ** -0.5, 0.046875)
    rate_row = jnp.clip(jnp.exp(jax.random.uniform(arg_keys[4], (N, E), jnp.float32, math.log(0.002), math.log(0.08))), 0.002, 0.08)
    rate_col = jnp.clip(jnp.exp(jax.random.uniform(arg_keys[5], (N, E), jnp.float32, math.log(0.002), math.log(0.08))), 0.002, 0.08)
    skip_gain = jnp.clip(jax.random.uniform(arg_keys[6], (E,), jnp.float32, 0.5, 1.5), 0.5, 1.5)
    w_out = centred(arg_keys[7], (E, D), E ** -0.5, 0.1875)
    return {"tokens": tokens, "norm_gain": norm_gain, "w_in": w_in, "w_bc": w_bc, "rate_row": rate_row, "rate_col": rate_col, "skip_gain": skip_gain, "w_out": w_out}


def run_scan(series, inject, readout, rate, skip_weight):
    decay_factor = jnp.exp(-rate)

    def advance(carried, inputs):
        value_now, inject_now, read_now = inputs
        carried = decay_factor[None] * carried + inject_now[:, :, None] * value_now[:, None, :]
        result = jnp.einsum('ine,in->ie', carried, read_now, precision=lax.Precision.HIGHEST) + skip_weight * value_now
        return (carried, result)
    start_state = jnp.zeros((series.shape[1], rate.shape[0], rate.shape[1]), jnp.float32)
    _, results = lax.scan(advance, start_state, (series, inject, readout))
    return results

def reference(tokens, norm_gain, w_in, w_bc, rate_row, rate_col, skip_gain, w_out):
    inner_width = w_out.shape[0]
    state_width = rate_row.shape[0]
    as_float = tokens.astype(jnp.float32)
    scale_now = lax.rsqrt(lax.optimization_barrier(jnp.mean(as_float * as_float, axis=-1, keepdims=True)) + 1e-05)
    normed = (as_float * scale_now * norm_gain).astype(jnp.bfloat16)
    project = jnp.dot(normed, w_in, preferred_element_type=jnp.float32)
    inputs_u = lax.optimization_barrier(project[..., :inner_width].astype(jnp.bfloat16)).astype(jnp.float32)
    gate_z = lax.optimization_barrier(project[..., inner_width:].astype(jnp.bfloat16)).astype(jnp.float32)
    mixers = lax.optimization_barrier(jnp.dot(normed, w_bc, preferred_element_type=jnp.float32).astype(jnp.bfloat16)).astype(jnp.float32)
    b_row = mixers[..., :state_width]
    c_row = mixers[..., state_width:2 * state_width]
    b_col = mixers[..., 2 * state_width:3 * state_width]
    c_col = mixers[..., 3 * state_width:]
    along_rows = run_scan(inputs_u.transpose(1, 0, 2), b_row.transpose(1, 0, 2), c_row.transpose(1, 0, 2), rate_row, skip_gain)
    along_rows = along_rows.transpose(1, 0, 2)
    row_mixed = lax.optimization_barrier(along_rows.astype(jnp.bfloat16)).astype(jnp.float32)
    col_mixed = run_scan(row_mixed, b_col, c_col, rate_col, 1.0)
    gated = (col_mixed * jax.nn.silu(gate_z)).astype(jnp.bfloat16)
    return jnp.dot(gated, w_out, preferred_element_type=jnp.float32).astype(jnp.bfloat16)
```

```python
import functools

import jax
import jax.numpy as jnp
from jax import lax
from jax.experimental import pallas as pl
from jax.experimental.pallas import tpu as pltpu
from jax.sharding import PartitionSpec as P

LANES = 128
VMEM_LIMIT = 60 * 1024 * 1024
MESH = pl.DeviceIdType.MESH


def normalise(tokens, gain):
    as_float = tokens.astype(jnp.float32)
    scale_now = lax.rsqrt(jnp.mean(as_float * as_float, axis=-1, keepdims=True) + 1e-05)
    return (as_float * scale_now * gain).astype(jnp.bfloat16)


def transposed_dot(a, b):
    return lax.dot_general(a, b, (((1,), (1,)), ((), ())), preferred_element_type=jnp.float32)


def spread_channels(ref, value, tiles):
    rows = value.shape[0]
    for t in range(tiles):
        ref[pl.ds(t, rows, stride=tiles), :] = value[:, t * LANES : (t + 1) * LANES]


def spread_vectors(ref, value, first, states, base):
    rows = value.shape[0]
    for n in range(states):
        ref[n, pl.ds(base, rows), :] = jnp.broadcast_to(
            value[:, first + n : first + n + 1], (rows, LANES)
        )


def scan_step(carried, decay, value, inject_ref, readout_ref, patch, start, tiles):
    new = []
    totals = [start, None]
    for n, state in enumerate(carried):
        inject = inject_ref[n, pl.ds(patch, tiles, stride=0), :]
        readout = readout_ref[n, pl.ds(patch, tiles, stride=0), :]
        state = decay[n] * state + inject * value
        term = readout * state
        totals[n % 2] = term if totals[n % 2] is None else totals[n % 2] + term
        new.append(state)
    return tuple(new), totals[0] + totals[1]


def layer_kernel(
    states, rows_n, cols_n, share, per_core,
    tok_ref, gain_in, win_in, wbc_in, rrate_in, crate_in, skip_in, wout_in,
    out_ref,
    gain_ref, win_ref, wbc_ref, rrate_ref, crate_ref, skip_ref, wout_ref, tcol, tin, rsend, rrecv, u_ref, rb_ref, rc_ref, cb_ref, cc_ref, z_ref, y_ref, gated_ref,
    rdecay, cdecay, skip_tile, stage, land, state_ref,
    tsend_sem, tin_sem, csend_sem, crecv_sem, rsend_sem, rrecv_sem, osend_sem, orecv_sem, fetch_sem,
):
    group_n = rows_n * cols_n
    pieces = tok_ref.shape[0] // share
    chunks = tin.shape[0]
    columns, width = tok_ref.shape[1:]
    inner = wout_ref.shape[0]
    tiles = inner // LANES
    piece_len = share * per_core
    chunk_len = group_n * piece_len
    blocks = stage.shape[0]
    blocks_home = blocks // cols_n
    block_len = stage.shape[1]
    r, c = lax.axis_index("rows"), lax.axis_index("cols")
    me = r * cols_n + c

    def spot(g):
        return {"rows": g // cols_n, "cols": g % cols_n}

    barrier = pltpu.get_barrier_semaphore()

    def greet(g, _):
        @pl.when(g != me)
        def _():
            pl.semaphore_signal(barrier, inc=1, device_id=spot(g), device_id_type=MESH)
        return 0

    lax.fori_loop(0, group_n, greet, 0)
    fetches = [
        pltpu.make_async_copy(src, dst, fetch_sem.at[k])
        for k, (src, dst) in enumerate((
            (rrate_in, rrate_ref), (crate_in, crate_ref), (skip_in, skip_ref), (gain_in, gain_ref),
            (wbc_in, wbc_ref), (tok_ref, tcol.at[c]), (win_in, win_ref), (wout_in, wout_ref),
        ))
    ]
    for fetch in fetches:
        fetch.start()
    pl.semaphore_wait(barrier, group_n - 1)

    local_chunks = max(1, chunks // cols_n)
    per_chunk = pieces // local_chunks

    def piece_of(k):
        piece = k // per_chunk * per_chunk + (k % per_chunk + me) % per_chunk
        place = c * pieces + piece
        return piece, place // group_n, place % group_n

    def token_copy(k):
        piece, q, g = piece_of(k)
        return g, pltpu.make_async_remote_copy(
            src_ref=tok_ref.at[pl.ds(piece * share, share)], dst_ref=tin.at[q, r],
            send_sem=tsend_sem.at[piece], recv_sem=tin_sem.at[q],
            device_id=spot(g), device_id_type=MESH,
        )

    def send_tokens(k, _):
        piece, q, g = piece_of(k)

        @pl.when(g == me)
        def _():
            pltpu.make_async_copy(tok_ref.at[pl.ds(piece * share, share)], tin.at[q, r], tin_sem.at[q]).start()

        @pl.when(g != me)
        def _():
            token_copy(k)[1].start()
        return 0

    lax.fori_loop(0, pieces, send_tokens, 0)

    def column_copy(step):
        other = (c + step) % cols_n
        return pltpu.make_async_remote_copy(
            src_ref=tok_ref, dst_ref=tcol.at[c],
            send_sem=csend_sem.at[step], recv_sem=crecv_sem.at[step],
            device_id={"cols": other}, device_id_type=MESH,
        )

    for step in range(1, cols_n):
        column_copy(step).start()

    def gate_part(tokens, core):
        tokens = tokens.astype(jnp.float32)
        own = tokens[:, :per_core]
        for k in range(1, cols_n):
            own = jnp.where(c == k, tokens[:, k * per_core : (k + 1) * per_core], own)
        normed = normalise(own.reshape(-1, width), gain_ref[...])
        count = normed.shape[0]
        base = pl.multiple_of(core * count, count)
        mixers = transposed_dot(normed, wbc_ref[...])
        mixers = mixers.astype(jnp.bfloat16).astype(jnp.float32)
        spread_vectors(cb_ref, mixers, 2 * states, states, base)
        spread_vectors(cc_ref, mixers, 3 * states, states, base)
        for k in range(0, inner, 2 * LANES):
            z_ref[pl.ds(base, count), k : k + 2 * LANES] = jnp.dot(
                normed, win_ref[:, inner + k : inner + k + 2 * LANES],
                preferred_element_type=jnp.float32,
            ).astype(jnp.bfloat16)

    for fetch in fetches:
        fetch.wait()
    spread_channels(rdecay, jnp.exp(-rrate_ref[...]), tiles)
    spread_channels(cdecay, jnp.exp(-crate_ref[...]), tiles)
    spread_channels(skip_tile, skip_ref[...], tiles)
    gate_part(tcol[c], c)

    zero = jnp.zeros((tiles, LANES), jnp.float32)
    lanes = 2 if share % 2 == 0 else 1

    def result_copy(q, k):
        g = (me + k) % group_n
        return pltpu.make_async_remote_copy(
            src_ref=rsend.at[q, pl.ds(g * piece_len, piece_len)],
            dst_ref=rrecv.at[q, pl.ds(me * piece_len, piece_len)],
            send_sem=rsend_sem.at[q, k], recv_sem=rrecv_sem.at[q],
            device_id=spot(g), device_id_type=MESH,
        )

    def row_chunk(q, _):
        pltpu.make_async_copy(tin.at[q], tin.at[q], tin_sem.at[q]).wait()
        normed = normalise(tin[q].astype(jnp.float32).reshape(chunk_len, width), gain_ref[...])
        mixers = transposed_dot(normed, wbc_ref[...])
        mixers = mixers.astype(jnp.bfloat16).astype(jnp.float32)
        spread_vectors(rb_ref, mixers, 0, states, 0)
        spread_vectors(rc_ref, mixers, states, states, 0)
        for k in range(0, tiles, 2):
            part = jnp.dot(normed, win_ref[:, k * LANES : (k + 2) * LANES],
                           preferred_element_type=jnp.float32)
            part = part.astype(jnp.bfloat16).astype(jnp.float32)
            for h in range(2):
                u_ref[pl.ds(k + h, chunk_len, stride=tiles), :] = part[:, h * LANES : (h + 1) * LANES]
        decay = [rdecay[n * tiles : (n + 1) * tiles, :] for n in range(states)]
        skip = skip_tile[...]

        def one_group(first, _):
            def one_step(j, carry):
                carry = list(carry)
                for w in range(columns):
                    for b in range(lanes):
                        row = first * lanes + b
                        patch = (j * share + row) * columns + w
                        owner = j * cols_n + w // per_core
                        value = u_ref[pl.ds(pl.multiple_of(patch * tiles, tiles), tiles), :]
                        carry[b], total = scan_step(carry[b], decay, value, rb_ref, rc_ref,
                                                    patch, skip * value, tiles)
                        rsend[q, (owner * share + row) * per_core + w % per_core] = total.astype(jnp.bfloat16)
                return tuple(carry)

            lax.fori_loop(0, rows_n, one_step, tuple((zero,) * states for _ in range(lanes)))
            return 0

        lax.fori_loop(0, share // lanes, one_group, 0)

        def send_result(k, _):
            result_copy(q, k).start()
            return 0

        pltpu.make_async_copy(
            rsend.at[q, pl.ds(me * piece_len, piece_len)],
            rrecv.at[q, pl.ds(me * piece_len, piece_len)], rrecv_sem.at[q],
        ).start()
        lax.fori_loop(1, group_n, send_result, 0)
        return 0

    lax.fori_loop(0, chunks, row_chunk, 0)

    for step in range(1, cols_n):
        column_copy(step).wait_recv()
        source = (c + cols_n - step) % cols_n
        gate_part(tcol[source], source)

    for g in range(per_core):
        for n in range(states):
            state_ref[g, n] = zero

    def out_copy(o):
        return pltpu.make_async_remote_copy(
            src_ref=stage.at[o], dst_ref=land.at[c, o % blocks_home],
            send_sem=osend_sem.at[o], recv_sem=orecv_sem.at[c, o % blocks_home],
            device_id={"cols": o // blocks_home}, device_id_type=MESH,
        )

    def col_chunk(q, _):
        pltpu.make_async_copy(rrecv.at[q], rrecv.at[q], rrecv_sem.at[q]).wait()
        decay = [cdecay[n * tiles : (n + 1) * tiles, :] for n in range(states)]
        base = q * chunk_len

        def one_step(s, carry):
            result = []
            for g in range(per_core):
                patch = s * per_core + g
                value = rrecv[q, patch].astype(jnp.float32)
                state, total = scan_step(carry[g], decay, value, cb_ref, cc_ref,
                                         base + patch, value, tiles)
                y_ref[pl.ds(pl.multiple_of(patch * tiles, tiles), tiles), :] = total
                result.append(state)
            return tuple(result)

        carry = tuple(tuple(state_ref[g, n] for n in range(states)) for g in range(per_core))
        carry = lax.fori_loop(0, chunk_len // per_core, one_step, carry)
        for g in range(per_core):
            for n in range(states):
                state_ref[g, n] = carry[g][n]
        start = pl.multiple_of(base, chunk_len)
        for t in range(tiles):
            gate = z_ref[pl.ds(start, chunk_len), t * LANES : (t + 1) * LANES].astype(jnp.float32)
            mixed = y_ref[pl.ds(t, chunk_len, stride=tiles), :]
            gated_ref[:, t * LANES : (t + 1) * LANES] = (
                mixed * (gate / (1.0 + jnp.exp(-gate)))
            ).astype(jnp.bfloat16)
        result = jnp.dot(gated_ref[...], wout_ref[...], preferred_element_type=jnp.float32)
        result = result.astype(jnp.bfloat16)
        for k in range(blocks // chunks):
            o = q * (blocks // chunks) + k
            block = result[k * block_len : (k + 1) * block_len]
            stage[o] = block

            @pl.when(o // blocks_home == c)
            def _():
                land[c, o % blocks_home] = block

            @pl.when(o // blocks_home != c)
            def _():
                out_copy(o).start()
        return 0

    lax.fori_loop(0, chunks, col_chunk, 0)

    def drain_tokens(k, _):
        g, copy = token_copy(k)

        @pl.when(g != me)
        def _():
            copy.wait_send()
        return 0

    lax.fori_loop(0, pieces, drain_tokens, 0)
    for step in range(1, cols_n):
        column_copy(step).wait_send()

    def drain_results(q, _):
        def one(k, _):
            result_copy(q, k).wait_send()
            return 0
        return lax.fori_loop(1, group_n, one, 0)

    lax.fori_loop(0, chunks, drain_results, 0)

    def drain_out(o, _):
        @pl.when(o // blocks_home != c)
        def _():
            out_copy(o).wait_send()
        return 0

    lax.fori_loop(0, blocks, drain_out, 0)
    for source in range(cols_n):
        @pl.when(source != c)
        def _():
            for i in range(blocks_home):
                pltpu.make_async_copy(
                    land.at[source, i], land.at[source, i], orecv_sem.at[source, i]
                ).wait()
    for i in range(blocks_home):
        parts = [
            land[s, i].astype(jnp.float32).reshape(block_len // per_core, per_core, -1)
            for s in range(cols_n)
        ]
        rows = block_len // per_core
        out_ref[i * rows : (i + 1) * rows] = jnp.concatenate(parts, axis=1).astype(jnp.bfloat16)


def per_device_uniform(tokens, norm_gain, w_in, w_bc, rate_row, rate_col, skip_gain, w_out):
    inner, width_out = w_out.shape
    states = rate_row.shape[0]
    height, columns, width = tokens.shape
    rows_n, cols_n = lax.axis_size("rows"), lax.axis_size("cols")
    group_n = rows_n * cols_n
    per_core = columns // cols_n
    total = height * cols_n
    share = min(4, total // group_n)
    chunks = total // (group_n * share)
    pieces = height // share
    piece_len = share * per_core
    chunk_len = group_n * piece_len
    tiles = inner // LANES
    blocks = max(chunks, cols_n)
    block_len = total * per_core // blocks
    patches = total * per_core
    f32, bf16 = jnp.float32, jnp.bfloat16
    dma = pltpu.SemaphoreType.DMA
    out = pl.pallas_call(
        functools.partial(layer_kernel, states, rows_n, cols_n, share, per_core),
        in_specs=[pl.BlockSpec(memory_space=pl.ANY)] * 8,
        out_specs=pl.BlockSpec(memory_space=pltpu.VMEM),
        out_shape=jax.ShapeDtypeStruct((height, columns, width_out), bf16),
        scratch_shapes=[
            pltpu.VMEM((1, width), f32),
            pltpu.VMEM(w_in.shape, bf16),
            pltpu.VMEM(w_bc.shape[::-1], bf16),
            pltpu.VMEM(rate_row.shape, f32),
            pltpu.VMEM(rate_col.shape, f32),
            pltpu.VMEM((1, inner), f32),
            pltpu.VMEM(w_out.shape, bf16),
            pltpu.VMEM((cols_n, height, columns, width), bf16),
            pltpu.VMEM((chunks, rows_n, share, columns, width), bf16),
            pltpu.VMEM((chunks, chunk_len, tiles, LANES), bf16),
            pltpu.VMEM((chunks, chunk_len, tiles, LANES), bf16),
            pltpu.VMEM((chunk_len * tiles, LANES), f32),
            pltpu.VMEM((states, chunk_len + 8, LANES), f32),
            pltpu.VMEM((states, chunk_len + 8, LANES), f32),
            pltpu.VMEM((states, patches + 8, LANES), f32),
            pltpu.VMEM((states, patches + 8, LANES), f32),
            pltpu.VMEM((patches, inner), bf16),
            pltpu.VMEM((chunk_len * tiles, LANES), f32),
            pltpu.VMEM((chunk_len, inner), bf16),
            pltpu.VMEM((states * tiles, LANES), f32),
            pltpu.VMEM((states * tiles, LANES), f32),
            pltpu.VMEM((tiles, LANES), f32),
            pltpu.VMEM((blocks, block_len, width_out), bf16),
            pltpu.VMEM((cols_n, blocks // cols_n, block_len, width_out), bf16),
            pltpu.VMEM((per_core, states, tiles, LANES), f32),
            dma((pieces,)), dma((chunks,)), dma((cols_n,)), dma((cols_n,)),
            dma((chunks, group_n)), dma((chunks,)), dma((blocks,)),
            dma((cols_n, blocks // cols_n)), dma((8,)),
        ],
        compiler_params=pltpu.CompilerParams(
            vmem_limit_bytes=VMEM_LIMIT, collective_id=0, has_side_effects=True
        ),
        name="layer",
    )(tokens, norm_gain[None], w_in, w_bc.T, rate_row, rate_col, skip_gain[None], w_out)
    return out


LANE_PAIR = 2 * LANES


def grouped_kernel(
    states, rows_n, cols_n, chunks, per_core,
    tok_ref, gain_in, win_in, wbc_in, rrate_in, crate_in, skip_in, wout_in,
    out_ref,
    gain_ref, win_ref, wbc_ref, rrate_ref, crate_ref, skip_ref, wout_ref,
    tcol, tin_a, tin_b, tin_c, table, order_ref, normed_ref, u_ref, b_ref, c_ref, lag_ref, ys_ref,
    rsend, rrecv, cb_ref, cc_ref, z_ref, y_ref, gated_ref, cdecay, stage, land, state_ref,
    tsend_sem, own_sem, early_sem, relay_sem, csend_sem, crecv_sem, rsend_sem, rrecv_sem,
    osend_sem, orecv_sem, fetch_sem,
):
    height, columns, width = tok_ref.shape
    inner = wout_ref.shape[0]
    tiles = inner // LANES
    pairs = inner // LANE_PAIR
    quarter = rows_n // 4
    chunk_rows = height * cols_n // chunks
    chunk_len = chunk_rows * per_core
    local_chunks = chunks // cols_n
    blocks = stage.shape[0]
    blocks_home = blocks // cols_n
    block_len = stage.shape[1]
    r, c = lax.axis_index("rows"), lax.axis_index("cols")
    lines = quarter * cols_n
    long_rows = chunk_rows // lines
    short_rows = long_rows // 2

    groups = ((0, quarter, long_rows), (quarter, quarter, long_rows), (2 * quarter, 2 * quarter, short_rows))
    inside = (r < quarter, (r >= quarter) & (r < 2 * quarter), r >= 2 * quarter)

    def line_of(group, k):
        first, chips, _ = groups[group]
        chip, core = k // cols_n, k % cols_n
        return (chip % quarter) * cols_n + core, chip // quarter, first + chip, core

    def row_offset(group, k):
        line, half, _, _ = line_of(group, k)
        return line * long_rows + half * short_rows

    barrier = pltpu.get_barrier_semaphore()

    def greet(chip, core):
        pl.semaphore_signal(barrier, inc=1, device_id={"rows": chip, "cols": core}, device_id_type=MESH)

    for group, (first, chips, _) in enumerate(groups):
        @pl.when(inside[group])
        def _():
            me = (r - first) * cols_n + c

            def one(k, _):
                @pl.when(k != me)
                def _():
                    greet(first + k // cols_n, k % cols_n)
                return 0

            lax.fori_loop(0, chips * cols_n, one, 0)
            if group == 1:
                greet(r - quarter, c)
            if group == 2:
                greet(quarter + (r - first) % quarter, c)

    fetches = [
        pltpu.make_async_copy(src, dst, fetch_sem.at[k])
        for k, (src, dst) in enumerate((
            (rrate_in, rrate_ref), (crate_in, crate_ref), (skip_in, skip_ref), (gain_in, gain_ref),
            (wbc_in, wbc_ref), (tok_ref, tcol.at[c]), (win_in, win_ref), (wout_in, wout_ref),
        ))
    ]
    for fetch in fetches:
        fetch.start()

    for group, (first, chips, _) in enumerate(groups):
        @pl.when(inside[group])
        def _():
            pl.semaphore_wait(barrier, chips * cols_n - 1 + (1, 2, 0)[group])

    tins = (tin_a, tin_b, tin_c)
    early = (0, quarter, 2 * quarter)

    def own_copy(group, n):
        first, chips, rows = groups[group]
        part, k = n // (chips * cols_n), n % (chips * cols_n)
        me = (r - first) * cols_n + c
        k = (k + me) % (chips * cols_n)
        _, _, chip, core = line_of(group, k)
        q = c * local_chunks + part
        src = tok_ref.at[pl.ds(part * chunk_rows + row_offset(group, k), rows)]
        dst = tins[group].at[q, early[group] + r - first]
        remote = pltpu.make_async_remote_copy(
            src_ref=src, dst_ref=dst, send_sem=tsend_sem.at[n], recv_sem=own_sem.at[q],
            device_id={"rows": chip, "cols": core}, device_id_type=MESH,
        )
        return k != me, remote, lambda: pltpu.make_async_copy(src, dst, own_sem.at[q])

    for group, (first, chips, _) in enumerate(groups):
        @pl.when(inside[group])
        def _():
            def one(n, _):
                away, remote, local = own_copy(group, n)

                @pl.when(away)
                def _():
                    remote.start()

                @pl.when(jnp.logical_not(away))
                def _():
                    local().start()
                return 0

            lax.fori_loop(0, local_chunks * chips * cols_n, one, 0)

    def column_copy(step):
        other = (c + step) % cols_n
        return pltpu.make_async_remote_copy(
            src_ref=tok_ref, dst_ref=tcol.at[c],
            send_sem=csend_sem.at[step], recv_sem=crecv_sem.at[step],
            device_id={"cols": other}, device_id_type=MESH,
        )

    for step in range(1, cols_n):
        column_copy(step).start()

    def gate_part(tokens, core):
        tokens = tokens.astype(jnp.float32)
        own = tokens[:, :per_core]
        for k in range(1, cols_n):
            own = jnp.where(c == k, tokens[:, k * per_core : (k + 1) * per_core], own)
        normed = normalise(own.reshape(-1, width), gain_ref[...])
        count = normed.shape[0]
        base = pl.multiple_of(core * count, count)
        mixers = transposed_dot(normed, wbc_ref[...])
        mixers = mixers.astype(jnp.bfloat16).astype(jnp.float32)
        spread_vectors(cb_ref, mixers, 2 * states, states, base)
        spread_vectors(cc_ref, mixers, 3 * states, states, base)
        for k in range(0, inner, LANE_PAIR):
            z_ref[pl.ds(base, count), k : k + LANE_PAIR] = jnp.dot(
                normed, win_ref[:, inner + k : inner + k + LANE_PAIR],
                preferred_element_type=jnp.float32,
            ).astype(jnp.bfloat16)

    for fetch in fetches:
        fetch.wait()

    for group, (first, chips, _) in enumerate(groups):
        @pl.when(inside[group])
        def _():
            rate = [rrate_ref[:, k * LANE_PAIR : (k + 1) * LANE_PAIR] for k in range(pairs)]
            for k in range(pairs):
                def fill(d, _):
                    table[k, d] = jnp.exp(-rate[k] * d.astype(jnp.float32)).astype(jnp.bfloat16)
                    return 0

                lax.fori_loop(0, (early[group] + chips) * columns, fill, 0)

    spread_channels(cdecay, jnp.exp(-crate_ref[...]), tiles)
    zero = jnp.zeros((tiles, LANES), jnp.float32)
    for g in range(per_core):
        for n in range(states):
            state_ref[g, n] = zero
    gate_part(tcol[c], c)
    for step in range(1, cols_n):
        column_copy(step).wait_recv()
        source = (c + cols_n - step) % cols_n
        gate_part(tcol[source], source)

    def relay_copy(group, q, half):
        if group == 0:
            src, dst = tin_a.at[q], tin_b.at[q, pl.ds(0, quarter)]
            chip = r + quarter
        else:
            src = tin_b.at[q, :, pl.ds(half * short_rows, short_rows)]
            dst = tin_c.at[q, pl.ds(0, 2 * quarter)]
            chip = r + quarter + half * quarter
        return pltpu.make_async_remote_copy(
            src_ref=src, dst_ref=dst, send_sem=relay_sem.at[q, half], recv_sem=early_sem.at[q],
            device_id={"rows": chip}, device_id_type=MESH,
        )

    def result_copy(group, q, k):
        first, chips, rows = groups[group]
        count = chips * cols_n
        me = (r - first) * cols_n + c
        g = (me + k) % count
        patches = rows * per_core
        src = rsend.at[q, pl.ds(g * patches, patches)]
        dst = rrecv.at[q, pl.ds(row_offset(group, me) * per_core, patches)]
        remote = pltpu.make_async_remote_copy(
            src_ref=src, dst_ref=dst, send_sem=rsend_sem.at[q, k], recv_sem=rrecv_sem.at[q],
            device_id={"rows": first + g // cols_n, "cols": g % cols_n}, device_id_type=MESH,
        )
        return remote, lambda: pltpu.make_async_copy(src, dst, rrecv_sem.at[q])

    def row_chunk(group, q):
        first, chips, rows = groups[group]
        tin = tins[group]
        before = early[group]
        if before:
            part = tin.at[q, pl.ds(0, before)]
            pltpu.make_async_copy(part, part, early_sem.at[q]).wait()
        part = tin.at[q, pl.ds(before, chips)]
        pltpu.make_async_copy(part, part, own_sem.at[q]).wait()
        for half in range((1, 2, 0)[group]):
            relay_copy(group, q, half).start()
        sources = before + chips
        out_cols, pre_cols = chips * columns, before * columns
        all_cols = out_cols + pre_cols
        block = columns * rows
        for s in range(sources):
            arrived = tin[q, s].astype(jnp.float32).reshape(block, width)
            for t in range(width // LANES):
                order_ref[t, s * block : (s + 1) * block] = arrived[:, t * LANES : (t + 1) * LANES]
        for s in range(sources):
            ordered = jnp.concatenate([
                jnp.concatenate(
                    [order_ref[t, pl.ds(s * block + w, rows, stride=columns), :] for w in range(columns)], axis=0
                )
                for t in range(width // LANES)
            ], axis=1)
            normed_ref[s * block : (s + 1) * block] = normalise(ordered, gain_ref[...])
        normed = normed_ref[: all_cols * rows]
        b_ref[: all_cols * rows] = transposed_dot(normed, wbc_ref[:states]).astype(jnp.bfloat16).astype(jnp.float32)
        c_ref[: out_cols * rows] = transposed_dot(
            normed_ref[pre_cols * rows : all_cols * rows], wbc_ref[states : 2 * states]
        ).astype(jnp.bfloat16).astype(jnp.float32)
        for k in range(pairs):
            u_ref[k, : all_cols * rows] = jnp.dot(
                normed, win_ref[:, k * LANE_PAIR : (k + 1) * LANE_PAIR], preferred_element_type=jnp.float32
            ).astype(jnp.bfloat16).astype(jnp.float32)

        def span(d):
            low = max(0, d - pre_cols)
            return low, out_cols - low, pre_cols + low - d

        for d in range(all_cols):
            low, count, source = span(d)
            lag_ref[d, : count * rows] = (
                c_ref[low * rows : out_cols * rows] * b_ref[source * rows : (source + count) * rows]
            ).astype(jnp.bfloat16)

        def one_pair(k, _):
            skip = skip_ref[k]
            total = [
                skip * u_ref[k, (pre_cols + o) * rows : (pre_cols + o + 1) * rows] for o in range(out_cols)
            ]
            for d in range(all_cols):
                low, count, source = span(d)
                weight = jnp.dot(lag_ref[d, : count * rows], table[k, d], preferred_element_type=jnp.float32)
                for i in range(count):
                    total[low + i] += weight[i * rows : (i + 1) * rows] * u_ref[
                        k, (source + i) * rows : (source + i + 1) * rows
                    ]
            for o in range(out_cols):
                for h in range(2):
                    ys_ref[pl.ds(o * rows * tiles + 2 * k + h, rows, stride=tiles), :] = (
                        total[o][:, h * LANES : (h + 1) * LANES]
                    )
            return 0

        lax.fori_loop(0, pairs, one_pair, 0)

        def pack(i, _):
            for w in range(per_core):
                for v in range(rows):
                    at = ((i * per_core + w) * rows + v) * tiles
                    rsend[q, (i * rows + v) * per_core + w] = (
                        ys_ref[pl.ds(pl.multiple_of(at, tiles), tiles), :].astype(jnp.bfloat16)
                    )
            return 0

        lax.fori_loop(0, out_cols // per_core, pack, 0)
        result_copy(group, q, 0)[1]().start()

        def send_result(k, _):
            result_copy(group, q, k)[0].start()
            return 0

        lax.fori_loop(1, chips * cols_n, send_result, 0)

    def out_copy(o):
        return pltpu.make_async_remote_copy(
            src_ref=stage.at[o], dst_ref=land.at[c, o % blocks_home],
            send_sem=osend_sem.at[o], recv_sem=orecv_sem.at[c, o % blocks_home],
            device_id={"cols": o // blocks_home}, device_id_type=MESH,
        )

    def col_chunk(q):
        pltpu.make_async_copy(rrecv.at[q], rrecv.at[q], rrecv_sem.at[q]).wait()
        decay = [cdecay[n * tiles : (n + 1) * tiles, :] for n in range(states)]
        base = q * chunk_len

        def one_step(s, carry):
            result = []
            for g in range(per_core):
                patch = s * per_core + g
                value = rrecv[q, patch].astype(jnp.float32)
                state, total = scan_step(carry[g], decay, value, cb_ref, cc_ref,
                                         base + patch, value, tiles)
                y_ref[pl.ds(pl.multiple_of(patch * tiles, tiles), tiles), :] = total
                result.append(state)
            return tuple(result)

        carry = tuple(tuple(state_ref[g, n] for n in range(states)) for g in range(per_core))
        carry = lax.fori_loop(0, chunk_len // per_core, one_step, carry)
        for g in range(per_core):
            for n in range(states):
                state_ref[g, n] = carry[g][n]
        start = pl.multiple_of(base, chunk_len)
        for t in range(tiles):
            gate = z_ref[pl.ds(start, chunk_len), t * LANES : (t + 1) * LANES].astype(jnp.float32)
            mixed = y_ref[pl.ds(t, chunk_len, stride=tiles), :]
            gated_ref[:, t * LANES : (t + 1) * LANES] = (
                mixed * (gate / (1.0 + jnp.exp(-gate)))
            ).astype(jnp.bfloat16)
        result = jnp.dot(gated_ref[...], wout_ref[...], preferred_element_type=jnp.float32)
        result = result.astype(jnp.bfloat16)
        for k in range(blocks // chunks):
            o = q * (blocks // chunks) + k
            block = result[k * block_len : (k + 1) * block_len]
            stage[o] = block

            @pl.when(o // blocks_home == c)
            def _():
                land[c, o % blocks_home] = block

            @pl.when(o // blocks_home != c)
            def _():
                out_copy(o).start()

    def one_chunk(q, _):
        @pl.when(q < chunks)
        def _():
            for group in range(3):
                @pl.when(inside[group])
                def _():
                    row_chunk(group, q)

        @pl.when(q > 0)
        def _():
            col_chunk(q - 1)
        return 0

    lax.fori_loop(0, chunks + 1, one_chunk, 0)

    for group, (first, chips, _) in enumerate(groups):
        @pl.when(inside[group])
        def _():
            def drain_tokens(n, _):
                away, remote, _ = own_copy(group, n)

                @pl.when(away)
                def _():
                    remote.wait_send()
                return 0

            lax.fori_loop(0, local_chunks * chips * cols_n, drain_tokens, 0)

            def drain_chunk(q, _):
                for half in range((1, 2, 0)[group]):
                    relay_copy(group, q, half).wait_send()

                def one(k, _):
                    result_copy(group, q, k)[0].wait_send()
                    return 0
                return lax.fori_loop(1, chips * cols_n, one, 0)

            lax.fori_loop(0, chunks, drain_chunk, 0)

    for step in range(1, cols_n):
        column_copy(step).wait_send()

    def drain_out(o, _):
        @pl.when(o // blocks_home != c)
        def _():
            out_copy(o).wait_send()
        return 0

    lax.fori_loop(0, blocks, drain_out, 0)
    for source in range(cols_n):
        @pl.when(source != c)
        def _():
            for i in range(blocks_home):
                pltpu.make_async_copy(
                    land.at[source, i], land.at[source, i], orecv_sem.at[source, i]
                ).wait()
    for i in range(blocks_home):
        parts = [
            land[s, i].astype(jnp.float32).reshape(block_len // per_core, per_core, -1)
            for s in range(cols_n)
        ]
        rows = block_len // per_core
        out_ref[i * rows : (i + 1) * rows] = jnp.concatenate(parts, axis=1).astype(jnp.bfloat16)


def per_device_grouped(chunks, tokens, norm_gain, w_in, w_bc, rate_row, rate_col, skip_gain, w_out):
    inner, width_out = w_out.shape
    states = rate_row.shape[0]
    height, columns, width = tokens.shape
    rows_n, cols_n = lax.axis_size("rows"), lax.axis_size("cols")
    quarter = rows_n // 4
    per_core = columns // cols_n
    total = height * cols_n
    chunk_rows = total // chunks
    chunk_len = chunk_rows * per_core
    long_rows = chunk_rows // (quarter * cols_n)
    short_rows = long_rows // 2
    tiles = inner // LANES
    pairs = inner // LANE_PAIR
    blocks = max(chunks, cols_n)
    block_len = total * per_core // blocks
    patches = total * per_core
    lags = rows_n * columns
    held = lags * short_rows
    outs = 2 * quarter * columns * short_rows
    f32, bf16 = jnp.float32, jnp.bfloat16
    dma = pltpu.SemaphoreType.DMA
    return pl.pallas_call(
        functools.partial(grouped_kernel, states, rows_n, cols_n, chunks, per_core),
        in_specs=[pl.BlockSpec(memory_space=pl.ANY)] * 8,
        out_specs=pl.BlockSpec(memory_space=pltpu.VMEM),
        out_shape=jax.ShapeDtypeStruct((height, columns, width_out), bf16),
        scratch_shapes=[
            pltpu.VMEM((1, width), f32),
            pltpu.VMEM(w_in.shape, bf16),
            pltpu.VMEM(w_bc.shape[::-1], bf16),
            pltpu.VMEM(rate_row.shape, f32),
            pltpu.VMEM(rate_col.shape, f32),
            pltpu.VMEM((pairs, 1, LANE_PAIR), f32),
            pltpu.VMEM(w_out.shape, bf16),
            pltpu.VMEM((cols_n, height, columns, width), bf16),
            pltpu.VMEM((chunks, quarter, long_rows, columns, width), bf16),
            pltpu.VMEM((chunks, 2 * quarter, long_rows, columns, width), bf16),
            pltpu.VMEM((chunks, 4 * quarter, short_rows, columns, width), bf16),
            pltpu.VMEM((pairs, lags, states, LANE_PAIR), bf16),
            pltpu.VMEM((width // LANES, held, LANES), f32),
            pltpu.VMEM((held, width), bf16),
            pltpu.VMEM((pairs, held, LANE_PAIR), f32),
            pltpu.VMEM((held, states), f32),
            pltpu.VMEM((outs, states), f32),
            pltpu.VMEM((lags, outs, states), bf16),
            pltpu.VMEM((outs * tiles, LANES), f32),
            pltpu.VMEM((chunks, chunk_len, tiles, LANES), bf16),
            pltpu.VMEM((chunks, chunk_len, tiles, LANES), bf16),
            pltpu.VMEM((states, patches + 8, LANES), f32),
            pltpu.VMEM((states, patches + 8, LANES), f32),
            pltpu.VMEM((patches, inner), bf16),
            pltpu.VMEM((chunk_len * tiles, LANES), f32),
            pltpu.VMEM((chunk_len, inner), bf16),
            pltpu.VMEM((states * tiles, LANES), f32),
            pltpu.VMEM((blocks, block_len, width_out), bf16),
            pltpu.VMEM((cols_n, blocks // cols_n, block_len, width_out), bf16),
            pltpu.VMEM((per_core, states, tiles, LANES), f32),
            dma((chunks // cols_n * 2 * quarter * cols_n,)), dma((chunks,)), dma((chunks,)), dma((chunks, 2)),
            dma((cols_n,)), dma((cols_n,)),
            dma((chunks, 2 * quarter * cols_n)), dma((chunks,)), dma((blocks,)),
            dma((cols_n, blocks // cols_n)), dma((8,)),
        ],
        compiler_params=pltpu.CompilerParams(
            vmem_limit_bytes=VMEM_LIMIT, collective_id=0, has_side_effects=True
        ),
        name="layer",
    )(
        tokens, norm_gain[None], w_in, w_bc.T, rate_row, rate_col,
        skip_gain.reshape(pairs, 1, LANE_PAIR), w_out,
    )


def chunk_count(tokens, inner):
    height, columns, _ = tokens.shape
    rows_n, cols_n = lax.axis_size("rows"), lax.axis_size("cols")
    total = height * cols_n
    if rows_n % 4 or columns % cols_n or inner % LANE_PAIR:
        return 0
    step = rows_n // 2 * cols_n * 8
    if total % step or total // step % cols_n:
        return 0
    return total // step


def per_device(tokens, norm_gain, w_in, w_bc, rate_row, rate_col, skip_gain, w_out):
    args = (tokens, norm_gain, w_in, w_bc, rate_row, rate_col, skip_gain, w_out)
    chunks = chunk_count(tokens, w_out.shape[0])
    if chunks:
        return per_device_grouped(chunks, *args)
    return per_device_uniform(*args)


def solution(mesh):
    placed = (P(("slides", "cols"), "rows", None), P(), P(), P(), P(), P(), P(), P())
    return jax.shard_map(
        per_device,
        mesh=mesh,
        in_specs=placed,
        out_specs=P(("slides", "cols"), "rows", None),
        check_vma=False,
    )
```

```python
import functools

import jax
import jax.numpy as jnp
from jax import lax
from jax.experimental import pallas as pl
from jax.experimental.pallas import tpu as pltpu
from jax.sharding import PartitionSpec as P

LANES = 128
VMEM_LIMIT = 60 * 1024 * 1024
MESH = pl.DeviceIdType.MESH


def normalise(tokens, gain):
    as_float = tokens.astype(jnp.float32)
    scale_now = lax.rsqrt(jnp.mean(as_float * as_float, axis=-1, keepdims=True) + 1e-05)
    return (as_float * scale_now * gain).astype(jnp.bfloat16)


def transposed_dot(a, b):
    return lax.dot_general(a, b, (((1,), (1,)), ((), ())), preferred_element_type=jnp.float32)


def spread_channels(ref, value, tiles):
    rows = value.shape[0]
    for t in range(tiles):
        ref[pl.ds(t, rows, stride=tiles), :] = value[:, t * LANES : (t + 1) * LANES]


def spread_vectors(ref, value, first, states, base):
    rows = value.shape[0]
    for n in range(states):
        ref[n, pl.ds(base, rows), :] = jnp.broadcast_to(
            value[:, first + n : first + n + 1], (rows, LANES)
        )


def scan_step(carried, decay, value, inject_ref, readout_ref, patch, start, tiles):
    new = []
    totals = [start, None]
    for n, state in enumerate(carried):
        inject = inject_ref[n, pl.ds(patch, tiles, stride=0), :]
        readout = readout_ref[n, pl.ds(patch, tiles, stride=0), :]
        state = decay[n] * state + inject * value
        term = readout * state
        totals[n % 2] = term if totals[n % 2] is None else totals[n % 2] + term
        new.append(state)
    return tuple(new), totals[0] + totals[1]


def layer_kernel(
    states, rows_n, cols_n, share, per_core,
    tok_ref, gain_in, win_in, wbc_in, rrate_in, crate_in, skip_in, wout_in,
    out_ref,
    gain_ref, win_ref, wbc_ref, rrate_ref, crate_ref, skip_ref, wout_ref, tcol, tin, rsend, rrecv, u_ref, rb_ref, rc_ref, cb_ref, cc_ref, z_ref, y_ref, gated_ref,
    rdecay, cdecay, skip_tile, stage, land, state_ref,
    tsend_sem, tin_sem, csend_sem, crecv_sem, rsend_sem, rrecv_sem, osend_sem, orecv_sem, fetch_sem,
):
    group_n = rows_n * cols_n
    pieces = tok_ref.shape[0] // share
    chunks = tin.shape[0]
    columns, width = tok_ref.shape[1:]
    inner = wout_ref.shape[0]
    tiles = inner // LANES
    piece_len = share * per_core
    chunk_len = group_n * piece_len
    blocks = stage.shape[0]
    blocks_home = blocks // cols_n
    block_len = stage.shape[1]
    r, c = lax.axis_index("rows"), lax.axis_index("cols")
    me = r * cols_n + c

    def spot(g):
        return {"rows": g // cols_n, "cols": g % cols_n}

    barrier = pltpu.get_barrier_semaphore()

    def greet(g, _):
        @pl.when(g != me)
        def _():
            pl.semaphore_signal(barrier, inc=1, device_id=spot(g), device_id_type=MESH)
        return 0

    lax.fori_loop(0, group_n, greet, 0)
    fetches = [
        pltpu.make_async_copy(src, dst, fetch_sem.at[k])
        for k, (src, dst) in enumerate((
            (rrate_in, rrate_ref), (crate_in, crate_ref), (skip_in, skip_ref), (gain_in, gain_ref),
            (wbc_in, wbc_ref), (tok_ref, tcol.at[c]), (win_in, win_ref), (wout_in, wout_ref),
        ))
    ]
    for fetch in fetches:
        fetch.start()
    pl.semaphore_wait(barrier, group_n - 1)

    local_chunks = max(1, chunks // cols_n)
    per_chunk = pieces // local_chunks

    def piece_of(k):
        piece = k // per_chunk * per_chunk + (k % per_chunk + me) % per_chunk
        place = c * pieces + piece
        return piece, place // group_n, place % group_n

    def token_copy(k):
        piece, q, g = piece_of(k)
        return g, pltpu.make_async_remote_copy(
            src_ref=tok_ref.at[pl.ds(piece * share, share)], dst_ref=tin.at[q, r],
            send_sem=tsend_sem.at[piece], recv_sem=tin_sem.at[q],
            device_id=spot(g), device_id_type=MESH,
        )

    def send_tokens(k, _):
        piece, q, g = piece_of(k)

        @pl.when(g == me)
        def _():
            pltpu.make_async_copy(tok_ref.at[pl.ds(piece * share, share)], tin.at[q, r], tin_sem.at[q]).start()

        @pl.when(g != me)
        def _():
            token_copy(k)[1].start()
        return 0

    lax.fori_loop(0, pieces, send_tokens, 0)

    def column_copy(step):
        other = (c + step) % cols_n
        return pltpu.make_async_remote_copy(
            src_ref=tok_ref, dst_ref=tcol.at[c],
            send_sem=csend_sem.at[step], recv_sem=crecv_sem.at[step],
            device_id={"cols": other}, device_id_type=MESH,
        )

    for step in range(1, cols_n):
        column_copy(step).start()

    def gate_part(tokens, core):
        tokens = tokens.astype(jnp.float32)
        own = tokens[:, :per_core]
        for k in range(1, cols_n):
            own = jnp.where(c == k, tokens[:, k * per_core : (k + 1) * per_core], own)
        normed = normalise(own.reshape(-1, width), gain_ref[...])
        count = normed.shape[0]
        base = pl.multiple_of(core * count, count)
        mixers = transposed_dot(normed, wbc_ref[...])
        mixers = mixers.astype(jnp.bfloat16).astype(jnp.float32)
        spread_vectors(cb_ref, mixers, 2 * states, states, base)
        spread_vectors(cc_ref, mixers, 3 * states, states, base)
        for k in range(0, inner, 2 * LANES):
            z_ref[pl.ds(base, count), k : k + 2 * LANES] = jnp.dot(
                normed, win_ref[:, inner + k : inner + k + 2 * LANES],
                preferred_element_type=jnp.float32,
            ).astype(jnp.bfloat16)

    for fetch in fetches:
        fetch.wait()
    spread_channels(rdecay, jnp.exp(-rrate_ref[...]), tiles)
    spread_channels(cdecay, jnp.exp(-crate_ref[...]), tiles)
    spread_channels(skip_tile, skip_ref[...], tiles)
    gate_part(tcol[c], c)

    zero = jnp.zeros((tiles, LANES), jnp.float32)
    lanes = 2 if share % 2 == 0 else 1

    def result_copy(q, k):
        g = (me + k) % group_n
        return pltpu.make_async_remote_copy(
            src_ref=rsend.at[q, pl.ds(g * piece_len, piece_len)],
            dst_ref=rrecv.at[q, pl.ds(me * piece_len, piece_len)],
            send_sem=rsend_sem.at[q, k], recv_sem=rrecv_sem.at[q],
            device_id=spot(g), device_id_type=MESH,
        )

    def row_chunk(q, _):
        pltpu.make_async_copy(tin.at[q], tin.at[q], tin_sem.at[q]).wait()
        normed = normalise(tin[q].astype(jnp.float32).reshape(chunk_len, width), gain_ref[...])
        mixers = transposed_dot(normed, wbc_ref[...])
        mixers = mixers.astype(jnp.bfloat16).astype(jnp.float32)
        spread_vectors(rb_ref, mixers, 0, states, 0)
        spread_vectors(rc_ref, mixers, states, states, 0)
        for k in range(0, tiles, 2):
            part = jnp.dot(normed, win_ref[:, k * LANES : (k + 2) * LANES],
                           preferred_element_type=jnp.float32)
            part = part.astype(jnp.bfloat16).astype(jnp.float32)
            for h in range(2):
                u_ref[pl.ds(k + h, chunk_len, stride=tiles), :] = part[:, h * LANES : (h + 1) * LANES]
        decay = [rdecay[n * tiles : (n + 1) * tiles, :] for n in range(states)]
        skip = skip_tile[...]

        def one_group(first, _):
            def one_step(j, carry):
                carry = list(carry)
                for w in range(columns):
                    for b in range(lanes):
                        row = first * lanes + b
                        patch = (j * share + row) * columns + w
                        owner = j * cols_n + w // per_core
                        value = u_ref[pl.ds(pl.multiple_of(patch * tiles, tiles), tiles), :]
                        carry[b], total = scan_step(carry[b], decay, value, rb_ref, rc_ref,
                                                    patch, skip * value, tiles)
                        rsend[q, (owner * share + row) * per_core + w % per_core] = total.astype(jnp.bfloat16)
                return tuple(carry)

            lax.fori_loop(0, rows_n, one_step, tuple((zero,) * states for _ in range(lanes)))
            return 0

        lax.fori_loop(0, share // lanes, one_group, 0)

        def send_result(k, _):
            result_copy(q, k).start()
            return 0

        pltpu.make_async_copy(
            rsend.at[q, pl.ds(me * piece_len, piece_len)],
            rrecv.at[q, pl.ds(me * piece_len, piece_len)], rrecv_sem.at[q],
        ).start()
        lax.fori_loop(1, group_n, send_result, 0)
        return 0

    lax.fori_loop(0, chunks, row_chunk, 0)

    for step in range(1, cols_n):
        column_copy(step).wait_recv()
        source = (c + cols_n - step) % cols_n
        gate_part(tcol[source], source)

    for g in range(per_core):
        for n in range(states):
            state_ref[g, n] = zero

    def out_copy(o):
        return pltpu.make_async_remote_copy(
            src_ref=stage.at[o], dst_ref=land.at[c, o % blocks_home],
            send_sem=osend_sem.at[o], recv_sem=orecv_sem.at[c, o % blocks_home],
            device_id={"cols": o // blocks_home}, device_id_type=MESH,
        )

    def col_chunk(q, _):
        pltpu.make_async_copy(rrecv.at[q], rrecv.at[q], rrecv_sem.at[q]).wait()
        decay = [cdecay[n * tiles : (n + 1) * tiles, :] for n in range(states)]
        base = q * chunk_len

        def one_step(s, carry):
            result = []
            for g in range(per_core):
                patch = s * per_core + g
                value = rrecv[q, patch].astype(jnp.float32)
                state, total = scan_step(carry[g], decay, value, cb_ref, cc_ref,
                                         base + patch, value, tiles)
                y_ref[pl.ds(pl.multiple_of(patch * tiles, tiles), tiles), :] = total
                result.append(state)
            return tuple(result)

        carry = tuple(tuple(state_ref[g, n] for n in range(states)) for g in range(per_core))
        carry = lax.fori_loop(0, chunk_len // per_core, one_step, carry)
        for g in range(per_core):
            for n in range(states):
                state_ref[g, n] = carry[g][n]
        start = pl.multiple_of(base, chunk_len)
        for t in range(tiles):
            gate = z_ref[pl.ds(start, chunk_len), t * LANES : (t + 1) * LANES].astype(jnp.float32)
            mixed = y_ref[pl.ds(t, chunk_len, stride=tiles), :]
            gated_ref[:, t * LANES : (t + 1) * LANES] = (
                mixed * (gate / (1.0 + jnp.exp(-gate)))
            ).astype(jnp.bfloat16)
        result = jnp.dot(gated_ref[...], wout_ref[...], preferred_element_type=jnp.float32)
        result = result.astype(jnp.bfloat16)
        for k in range(blocks // chunks):
            o = q * (blocks // chunks) + k
            block = result[k * block_len : (k + 1) * block_len]
            stage[o] = block

            @pl.when(o // blocks_home == c)
            def _():
                land[c, o % blocks_home] = block

            @pl.when(o // blocks_home != c)
            def _():
                out_copy(o).start()
        return 0

    lax.fori_loop(0, chunks, col_chunk, 0)

    def drain_tokens(k, _):
        g, copy = token_copy(k)

        @pl.when(g != me)
        def _():
            copy.wait_send()
        return 0

    lax.fori_loop(0, pieces, drain_tokens, 0)
    for step in range(1, cols_n):
        column_copy(step).wait_send()

    def drain_results(q, _):
        def one(k, _):
            result_copy(q, k).wait_send()
            return 0
        return lax.fori_loop(1, group_n, one, 0)

    lax.fori_loop(0, chunks, drain_results, 0)

    def drain_out(o, _):
        @pl.when(o // blocks_home != c)
        def _():
            out_copy(o).wait_send()
        return 0

    lax.fori_loop(0, blocks, drain_out, 0)
    for source in range(cols_n):
        @pl.when(source != c)
        def _():
            for i in range(blocks_home):
                pltpu.make_async_copy(
                    land.at[source, i], land.at[source, i], orecv_sem.at[source, i]
                ).wait()
    for i in range(blocks_home):
        parts = [
            land[s, i].astype(jnp.float32).reshape(block_len // per_core, per_core, -1)
            for s in range(cols_n)
        ]
        rows = block_len // per_core
        out_ref[i * rows : (i + 1) * rows] = jnp.concatenate(parts, axis=1).astype(jnp.bfloat16)


def per_device_uniform(tokens, norm_gain, w_in, w_bc, rate_row, rate_col, skip_gain, w_out):
    inner, width_out = w_out.shape
    states = rate_row.shape[0]
    height, columns, width = tokens.shape
    rows_n, cols_n = lax.axis_size("rows"), lax.axis_size("cols")
    group_n = rows_n * cols_n
    per_core = columns // cols_n
    total = height * cols_n
    share = min(4, total // group_n)
    chunks = total // (group_n * share)
    pieces = height // share
    piece_len = share * per_core
    chunk_len = group_n * piece_len
    tiles = inner // LANES
    blocks = max(chunks, cols_n)
    block_len = total * per_core // blocks
    patches = total * per_core
    f32, bf16 = jnp.float32, jnp.bfloat16
    dma = pltpu.SemaphoreType.DMA
    out = pl.pallas_call(
        functools.partial(layer_kernel, states, rows_n, cols_n, share, per_core),
        in_specs=[pl.BlockSpec(memory_space=pl.ANY)] * 8,
        out_specs=pl.BlockSpec(memory_space=pltpu.VMEM),
        out_shape=jax.ShapeDtypeStruct((height, columns, width_out), bf16),
        scratch_shapes=[
            pltpu.VMEM((1, width), f32),
            pltpu.VMEM(w_in.shape, bf16),
            pltpu.VMEM(w_bc.shape[::-1], bf16),
            pltpu.VMEM(rate_row.shape, f32),
            pltpu.VMEM(rate_col.shape, f32),
            pltpu.VMEM((1, inner), f32),
            pltpu.VMEM(w_out.shape, bf16),
            pltpu.VMEM((cols_n, height, columns, width), bf16),
            pltpu.VMEM((chunks, rows_n, share, columns, width), bf16),
            pltpu.VMEM((chunks, chunk_len, tiles, LANES), bf16),
            pltpu.VMEM((chunks, chunk_len, tiles, LANES), bf16),
            pltpu.VMEM((chunk_len * tiles, LANES), f32),
            pltpu.VMEM((states, chunk_len + 8, LANES), f32),
            pltpu.VMEM((states, chunk_len + 8, LANES), f32),
            pltpu.VMEM((states, patches + 8, LANES), f32),
            pltpu.VMEM((states, patches + 8, LANES), f32),
            pltpu.VMEM((patches, inner), bf16),
            pltpu.VMEM((chunk_len * tiles, LANES), f32),
            pltpu.VMEM((chunk_len, inner), bf16),
            pltpu.VMEM((states * tiles, LANES), f32),
            pltpu.VMEM((states * tiles, LANES), f32),
            pltpu.VMEM((tiles, LANES), f32),
            pltpu.VMEM((blocks, block_len, width_out), bf16),
            pltpu.VMEM((cols_n, blocks // cols_n, block_len, width_out), bf16),
            pltpu.VMEM((per_core, states, tiles, LANES), f32),
            dma((pieces,)), dma((chunks,)), dma((cols_n,)), dma((cols_n,)),
            dma((chunks, group_n)), dma((chunks,)), dma((blocks,)),
            dma((cols_n, blocks // cols_n)), dma((8,)),
        ],
        compiler_params=pltpu.CompilerParams(
            vmem_limit_bytes=VMEM_LIMIT, collective_id=0, has_side_effects=True
        ),
        name="layer",
    )(tokens, norm_gain[None], w_in, w_bc.T, rate_row, rate_col, skip_gain[None], w_out)
    return out


LANE_PAIR = 2 * LANES
SUBLANES = 8


def grouped_kernel(
    states, rows_n, cols_n, chunks, per_core,
    tok_ref, gain_in, win_in, wbc_in, rrate_in, crate_in, skip_in, wout_in,
    out_ref,
    gain_ref, win_ref, wbc_ref, rrate_ref, crate_ref, skip_ref, wout_ref,
    tcol, tin_a, tin_b, tin_c, table, order_ref, normed_ref, u_ref, b_ref, c_ref, lag_ref,
    rsend, rrecv, vcol, inject_ref, spread_ref, read_ref, hist, z_ref, gated_ref, stage, land, state_ref,
    own_send_sem, next_send_sem, own_sem, early_sem, relay_sem, csend_sem, crecv_sem, rsend_sem, rrecv_sem,
    osend_sem, orecv_sem, fetch_sem,
):
    height, columns, width = tok_ref.shape
    inner = wout_ref.shape[0]
    tiles = inner // LANES
    pairs = inner // LANE_PAIR
    quarter = rows_n // 4
    total = height * cols_n
    chunk_rows = total // chunks
    local_chunks = chunks // cols_n
    lines = quarter * cols_n
    rows = chunk_rows // lines
    run = LANE_PAIR // states
    r, c = lax.axis_index("rows"), lax.axis_index("cols")

    groups = ((0, quarter), (quarter, quarter), (2 * quarter, 2 * quarter))
    inside = (r < quarter, (r >= quarter) & (r < 2 * quarter), r >= 2 * quarter)
    tins = (tin_a, tin_b, tin_c)
    early = (0, quarter, 2 * quarter)
    line = r % quarter * cols_n + c

    def chip_of(group, q, p):
        chip = groups[group][0] + p // cols_n
        return chip + q % 2 * quarter if group == 2 else chip

    def slot(group, q):
        return q // 2 if group == 2 else q

    barrier = pltpu.get_barrier_semaphore()

    def greet(chip, core):
        pl.semaphore_signal(barrier, inc=1, device_id={"rows": chip, "cols": core}, device_id_type=MESH)

    for group, (first, chips) in enumerate(groups):
        @pl.when(inside[group])
        def _():
            me = (r - first) * cols_n + c

            def one(k, _):
                @pl.when(k != me)
                def _():
                    greet(first + k // cols_n, k % cols_n)
                return 0

            lax.fori_loop(0, chips * cols_n, one, 0)
            if group:
                def back(k, _):
                    greet(first - quarter + k // cols_n, k % cols_n)
                    return 0

                lax.fori_loop(0, lines, back, 0)

    fetches = [
        pltpu.make_async_copy(src, dst, fetch_sem.at[k])
        for k, (src, dst) in enumerate((
            (rrate_in, rrate_ref), (crate_in, crate_ref), (skip_in, skip_ref), (gain_in, gain_ref),
            (wbc_in, wbc_ref), (tok_ref, tcol.at[c]), (win_in, win_ref), (wout_in, wout_ref),
        ))
    ]
    for fetch in fetches:
        fetch.start()

    for group, (first, chips) in enumerate(groups):
        @pl.when(inside[group])
        def _():
            waited = chips * cols_n - 1
            if group < 2:
                waited += groups[group + 1][1] * cols_n
            pl.semaphore_wait(barrier, waited)

    def token_copy(group, target, n):
        part, p = n // lines, (n + line) % lines
        q = c * local_chunks + part
        chip, core = chip_of(target, q, p), p % cols_n
        src = tok_ref.at[pl.ds(part * chunk_rows + p * rows, rows)]
        dst = tins[target].at[slot(target, q), r]
        if target == group:
            dst = tins[target].at[slot(target, q), early[group] + r - groups[group][0]]
        send = own_send_sem if target == group else next_send_sem
        recv = own_sem if target == group else early_sem
        remote = pltpu.make_async_remote_copy(
            src_ref=src, dst_ref=dst, send_sem=send.at[n], recv_sem=recv.at[q],
            device_id={"rows": chip, "cols": core}, device_id_type=MESH,
        )
        away = (chip != r) | (core != c)
        return away, remote, lambda: pltpu.make_async_copy(src, dst, recv.at[q])

    def send_own(group, n):
        away, remote, local = token_copy(group, group, n)

        @pl.when(away)
        def _():
            remote.start()

        @pl.when(jnp.logical_not(away))
        def _():
            local().start()

    def send_next(group, part):
        def one(p, _):
            token_copy(group, group + 1, part * lines + p)[1].start()
            return 0

        lax.fori_loop(0, lines, one, 0)

    ahead = 2
    for group in range(3):
        @pl.when(inside[group])
        def _():
            def one_part(part, _):
                def one(p, _):
                    send_own(group, part * lines + p)
                    return 0

                lax.fori_loop(0, lines, one, 0)
                if group == 0:
                    send_next(group, part)
                if group == 1:
                    @pl.when(c * local_chunks + part < ahead)
                    def _():
                        send_next(group, part)
                return 0

            lax.fori_loop(0, local_chunks, one_part, 0)

    def column_copy(step):
        other = (c + step) % cols_n
        return pltpu.make_async_remote_copy(
            src_ref=tok_ref, dst_ref=tcol.at[c],
            send_sem=csend_sem.at[step], recv_sem=crecv_sem.at[step],
            device_id={"cols": other}, device_id_type=MESH,
        )

    for step in range(1, cols_n):
        column_copy(step).start()

    def in_order(base, first, count):
        return jnp.concatenate([
            order_ref[t, pl.ds(base + first, count, stride=columns), :] for t in range(width // LANES)
        ], axis=1)

    def keep_order(base, tokens):
        flat = tokens.astype(jnp.float32).reshape(-1, width)
        for t in range(width // LANES):
            order_ref[t, base : base + flat.shape[0]] = flat[:, t * LANES : (t + 1) * LANES]

    def gate_part(core):
        keep_order(0, tcol[core])
        for w in range(per_core):
            normed = normalise(in_order(0, c * per_core + w, height), gain_ref[...])
            base = pl.multiple_of(w * total + core * height, height)
            inject = transposed_dot(normed, wbc_ref[2 * states : 3 * states])
            inject = inject.astype(jnp.bfloat16).astype(jnp.float32)
            for n in range(states):
                inject_ref[pl.ds(base * states + n, height, stride=states), :] = jnp.broadcast_to(
                    inject[:, n : n + 1], (height, LANES)
                )
            read = transposed_dot(normed, spread_ref[...])
            owner = lax.broadcasted_iota(jnp.int32, read.shape, 1) // states
            here = lax.broadcasted_iota(jnp.int32, read.shape, 0) % run
            read_ref[pl.ds(base, height), :] = jnp.where(owner == here, read, 0.0).astype(jnp.bfloat16)
            for k in range(0, inner, LANE_PAIR):
                z_ref[pl.ds(base, height), k : k + LANE_PAIR] = jnp.dot(
                    normed, win_ref[:, inner + k : inner + k + LANE_PAIR],
                    preferred_element_type=jnp.float32,
                ).astype(jnp.bfloat16)

    for fetch in fetches:
        fetch.wait()

    for group, (first, chips) in enumerate(groups):
        @pl.when(inside[group])
        def _():
            def fill(d, _):
                for k in range(pairs):
                    rate = rrate_ref[:, k * LANE_PAIR : (k + 1) * LANE_PAIR]
                    table[k, d] = jnp.exp(-rate * d.astype(jnp.float32)).astype(jnp.bfloat16)
                return 0

            lax.fori_loop(0, (early[group] + chips) * columns, fill, 0)

    for i in range(run):
        spread_ref[i * states : (i + 1) * states] = wbc_ref[3 * states : 4 * states]
    crate_ref[...] = jnp.exp(-crate_ref[...])
    state_ref[...] = jnp.zeros(state_ref.shape, jnp.float32)
    gate_part(c)
    for step in range(1, cols_n):
        column_copy(step).wait_recv()
        gate_part((c + cols_n - step) % cols_n)

    def relay_copy(q):
        return pltpu.make_async_remote_copy(
            src_ref=tin_b.at[q, pl.ds(0, quarter)], dst_ref=tin_c.at[q // 2, pl.ds(0, quarter)],
            send_sem=relay_sem.at[q], recv_sem=early_sem.at[q],
            device_id={"rows": r + quarter + q % 2 * quarter}, device_id_type=MESH,
        )

    def result_copy(group, q, k):
        first, chips = groups[group]
        g = ((r - first) * cols_n + c + k) % (chips * cols_n)
        src, dst = rsend.at[slot(group, q), g], rrecv.at[q, line]
        remote = pltpu.make_async_remote_copy(
            src_ref=src, dst_ref=dst, send_sem=rsend_sem.at[slot(group, q), k], recv_sem=rrecv_sem.at[q],
            device_id={"rows": first + g // cols_n, "cols": g % cols_n}, device_id_type=MESH,
        )
        return remote, lambda: pltpu.make_async_copy(src, dst, rrecv_sem.at[q])

    def row_chunk(group, q):
        chips = groups[group][1]
        before = early[group]
        at = slot(group, q)
        tin = tins[group]
        if before:
            part = tin.at[at, pl.ds(0, before)]
            pltpu.make_async_copy(part, part, early_sem.at[q]).wait()
        if group == 1:
            relay_copy(q).start()
            later = q + ahead

            @pl.when((later < chunks) & (later // local_chunks == c))
            def _():
                send_next(group, later % local_chunks)
        part = tin.at[at, pl.ds(before, chips)]
        pltpu.make_async_copy(part, part, own_sem.at[q]).wait()
        out_cols, pre_cols = chips * columns, before * columns
        all_cols = out_cols + pre_cols
        block = columns * rows
        for s in range(before + chips):
            keep_order(s * block, tin[at, s])
        for s in range(before + chips):
            ordered = jnp.concatenate([in_order(s * block, w, rows) for w in range(columns)], axis=0)
            normed_ref[s * block : (s + 1) * block] = normalise(ordered, gain_ref[...])
        normed = normed_ref[: all_cols * rows]
        b_ref[: all_cols * rows] = transposed_dot(normed, wbc_ref[:states]).astype(jnp.bfloat16).astype(jnp.float32)
        c_ref[: out_cols * rows] = transposed_dot(
            normed_ref[pre_cols * rows : all_cols * rows], wbc_ref[states : 2 * states]
        ).astype(jnp.bfloat16).astype(jnp.float32)
        for k in range(pairs):
            u_ref[k, : all_cols * rows] = jnp.dot(
                normed, win_ref[:, k * LANE_PAIR : (k + 1) * LANE_PAIR], preferred_element_type=jnp.float32
            ).astype(jnp.bfloat16).astype(jnp.float32)

        def span(d):
            low = max(0, d - pre_cols)
            return low, out_cols - low, pre_cols + low - d

        for d in range(all_cols):
            low, count, source = span(d)
            lag_ref[d, : count * rows] = (
                c_ref[low * rows : out_cols * rows] * b_ref[source * rows : (source + count) * rows]
            ).astype(jnp.bfloat16)

        def one_pair(k, _):
            skip = skip_ref[k]
            sums = [
                skip * u_ref[k, (pre_cols + o) * rows : (pre_cols + o + 1) * rows] for o in range(out_cols)
            ]
            for d in range(all_cols):
                low, count, source = span(d)
                weight = jnp.dot(lag_ref[d, : count * rows], table[k, d], preferred_element_type=jnp.float32)
                for i in range(count):
                    sums[low + i] += weight[i * rows : (i + 1) * rows] * u_ref[
                        k, (source + i) * rows : (source + i + 1) * rows
                    ]
            for o in range(out_cols):
                rsend[at, o // per_core, o % per_core, :, pl.ds(pl.multiple_of(k * LANE_PAIR, LANE_PAIR), LANE_PAIR)] = (
                    sums[o].astype(jnp.bfloat16)
                )
            return 0

        lax.fori_loop(0, pairs, one_pair, 0)
        result_copy(group, q, 0)[1]().start()

        def send_result(k, _):
            result_copy(group, q, k)[0].start()
            return 0

        lax.fori_loop(1, chips * cols_n, send_result, 0)

    def out_copy(q):
        return pltpu.make_async_remote_copy(
            src_ref=stage.at[q], dst_ref=land.at[c, q % local_chunks],
            send_sem=osend_sem.at[q], recv_sem=orecv_sem.at[c, q % local_chunks],
            device_id={"cols": q // local_chunks}, device_id_type=MESH,
        )

    def col_chunk(q):
        pltpu.make_async_copy(rrecv.at[q], rrecv.at[q], rrecv_sem.at[q]).wait()
        for p in range(lines):
            for w in range(per_core):
                value = rrecv[q, p, w].astype(jnp.float32)
                for t in range(tiles):
                    vcol[t, w * chunk_rows + p * rows : w * chunk_rows + (p + 1) * rows] = (
                        value[:, t * LANES : (t + 1) * LANES]
                    )
        halves = range(0, states, SUBLANES)

        def one_run(i, _):
            for w in range(per_core):
                here = pl.multiple_of(w * chunk_rows + i * run, run)
                patch = pl.multiple_of(w * total + q * chunk_rows + i * run, run)
                decay = [[crate_ref[h : h + SUBLANES, t * LANES : (t + 1) * LANES] for t in range(tiles)] for h in halves]
                state = [[state_ref[w, h : h + SUBLANES, t * LANES : (t + 1) * LANES] for t in range(tiles)] for h in halves]
                for s in range(run):
                    inject = [
                        inject_ref[pl.ds(pl.multiple_of((patch + s) * states + h, SUBLANES), SUBLANES), :] for h in halves
                    ]
                    for t in range(tiles):
                        value = vcol[t, pl.ds(here + s, SUBLANES, stride=0), :]
                        for j in range(len(inject)):
                            state[j][t] = decay[j][t] * state[j][t] + inject[j] * value
                        hist[w, s * states : (s + 1) * states, t * LANES : (t + 1) * LANES] = jnp.concatenate(
                            [state[j][t] for j in range(len(inject))], axis=0
                        ).astype(jnp.bfloat16)
                for j, h in enumerate(halves):
                    for t in range(tiles):
                        state_ref[w, h : h + SUBLANES, t * LANES : (t + 1) * LANES] = state[j][t]
                mixed = jnp.dot(read_ref[pl.ds(patch, run), :], hist[w], preferred_element_type=jnp.float32)
                for t in range(tiles):
                    gate = z_ref[pl.ds(patch, run), t * LANES : (t + 1) * LANES].astype(jnp.float32)
                    both = mixed[:, t * LANES : (t + 1) * LANES] + vcol[t, pl.ds(here, run), :]
                    gated_ref[pl.ds(here, run), t * LANES : (t + 1) * LANES] = (
                        both * (gate / (1.0 + jnp.exp(-gate)))
                    ).astype(jnp.bfloat16)
            return 0

        lax.fori_loop(0, chunk_rows // run, one_run, 0)
        result = jnp.dot(gated_ref[...], wout_ref[...], preferred_element_type=jnp.float32).astype(jnp.bfloat16)
        home = q // local_chunks

        @pl.when(home == c)
        def _():
            land[c, q % local_chunks] = result

        @pl.when(home != c)
        def _():
            stage[q] = result
            out_copy(q).start()

    def one_chunk(q, _):
        for group in range(3):
            mine = inside[group] & (q < chunks)
            if group == 2:
                mine = mine & (q % 2 == (r - 2 * quarter) // quarter)

            @pl.when(mine)
            def _():
                row_chunk(group, q)

        @pl.when(q > 0)
        def _():
            col_chunk(q - 1)
        return 0

    lax.fori_loop(0, chunks + 1, one_chunk, 0)

    for group, (first, chips) in enumerate(groups):
        @pl.when(inside[group])
        def _():
            def drain_tokens(n, _):
                away, remote, _ = token_copy(group, group, n)

                @pl.when(away)
                def _():
                    remote.wait_send()
                if group < 2:
                    token_copy(group, group + 1, n)[1].wait_send()
                return 0

            lax.fori_loop(0, local_chunks * lines, drain_tokens, 0)

            def drain_chunk(q, _):
                if group == 1:
                    relay_copy(q).wait_send()

                def one(k, _):
                    result_copy(group, q, k)[0].wait_send()
                    return 0

                if group == 2:
                    @pl.when(q % 2 == (r - 2 * quarter) // quarter)
                    def _():
                        lax.fori_loop(1, chips * cols_n, one, 0)
                else:
                    lax.fori_loop(1, chips * cols_n, one, 0)
                return 0

            lax.fori_loop(0, chunks, drain_chunk, 0)

    for step in range(1, cols_n):
        column_copy(step).wait_send()

    def drain_out(q, _):
        @pl.when(q // local_chunks != c)
        def _():
            out_copy(q).wait_send()
        return 0

    lax.fori_loop(0, chunks, drain_out, 0)
    for source in range(cols_n):
        @pl.when(source != c)
        def _():
            for i in range(local_chunks):
                pltpu.make_async_copy(
                    land.at[source, i], land.at[source, i], orecv_sem.at[source, i]
                ).wait()
    for source in range(cols_n):
        for i in range(local_chunks):
            for w in range(per_core):
                out_ref[source * per_core + w, i * chunk_rows : (i + 1) * chunk_rows] = (
                    land[source, i, w * chunk_rows : (w + 1) * chunk_rows]
                )


def per_device_grouped(chunks, tokens, norm_gain, w_in, w_bc, rate_row, rate_col, skip_gain, w_out):
    inner, width_out = w_out.shape
    states = rate_row.shape[0]
    height, columns, width = tokens.shape
    rows_n, cols_n = lax.axis_size("rows"), lax.axis_size("cols")
    quarter = rows_n // 4
    per_core = columns // cols_n
    total = height * cols_n
    chunk_rows = total // chunks
    lines = quarter * cols_n
    rows = chunk_rows // lines
    tiles = inner // LANES
    pairs = inner // LANE_PAIR
    patches = total * per_core
    local_chunks = chunks // cols_n
    lags = rows_n * columns
    held = lags * rows
    outs = 2 * quarter * columns * rows
    f32, bf16 = jnp.float32, jnp.bfloat16
    dma = pltpu.SemaphoreType.DMA
    out = pl.pallas_call(
        functools.partial(grouped_kernel, states, rows_n, cols_n, chunks, per_core),
        in_specs=[pl.BlockSpec(memory_space=pl.ANY)] * 8,
        out_specs=pl.BlockSpec(memory_space=pltpu.VMEM),
        out_shape=jax.ShapeDtypeStruct((columns, height, width_out), bf16),
        scratch_shapes=[
            pltpu.VMEM((1, width), f32),
            pltpu.VMEM(w_in.shape, bf16),
            pltpu.VMEM(w_bc.shape[::-1], bf16),
            pltpu.VMEM(rate_row.shape, f32),
            pltpu.VMEM(rate_col.shape, f32),
            pltpu.VMEM((pairs, 1, LANE_PAIR), f32),
            pltpu.VMEM(w_out.shape, bf16),
            pltpu.VMEM((cols_n, height, columns, width), bf16),
            pltpu.VMEM((chunks, quarter, rows, columns, width), bf16),
            pltpu.VMEM((chunks, 2 * quarter, rows, columns, width), bf16),
            pltpu.VMEM((chunks // 2, 4 * quarter, rows, columns, width), bf16),
            pltpu.VMEM((pairs, lags, states, LANE_PAIR), bf16),
            pltpu.VMEM((width // LANES, max(held, height * columns), LANES), f32),
            pltpu.VMEM((held, width), bf16),
            pltpu.VMEM((pairs, held, LANE_PAIR), f32),
            pltpu.VMEM((held, states), f32),
            pltpu.VMEM((outs, states), f32),
            pltpu.VMEM((lags, outs, states), bf16),
            pltpu.VMEM((chunks, 2 * lines, per_core, rows, inner), bf16),
            pltpu.VMEM((chunks, lines, per_core, rows, inner), bf16),
            pltpu.VMEM((tiles, per_core * chunk_rows + SUBLANES, LANES), f32),
            pltpu.VMEM((patches * states, LANES), f32),
            pltpu.VMEM((LANE_PAIR, width), bf16),
            pltpu.VMEM((patches, LANE_PAIR), bf16),
            pltpu.VMEM((per_core, LANE_PAIR, inner), bf16),
            pltpu.VMEM((patches, inner), bf16),
            pltpu.VMEM((per_core * chunk_rows, inner), bf16),
            pltpu.VMEM((chunks, per_core * chunk_rows, width_out), bf16),
            pltpu.VMEM((cols_n, local_chunks, per_core * chunk_rows, width_out), bf16),
            pltpu.VMEM((per_core, states, inner), f32),
            dma((local_chunks * lines,)), dma((local_chunks * lines,)), dma((chunks,)), dma((chunks,)), dma((chunks,)),
            dma((cols_n,)), dma((cols_n,)),
            dma((chunks, 2 * lines)), dma((chunks,)), dma((chunks,)),
            dma((cols_n, local_chunks)), dma((8,)),
        ],
        compiler_params=pltpu.CompilerParams(
            vmem_limit_bytes=VMEM_LIMIT, collective_id=0, has_side_effects=True
        ),
        name="layer",
    )(
        tokens, norm_gain[None], w_in, w_bc.T, rate_row, rate_col,
        skip_gain.reshape(pairs, 1, LANE_PAIR), w_out,
    )
    return out.transpose(1, 0, 2)


def chunk_count(tokens, rate_row, inner):
    height, columns, _ = tokens.shape
    states = rate_row.shape[0]
    rows_n, cols_n = lax.axis_size("rows"), lax.axis_size("cols")
    total = height * cols_n
    if rows_n % 4 or columns % cols_n or inner % LANE_PAIR or states % SUBLANES or LANE_PAIR % states:
        return 0
    step = rows_n // 4 * cols_n * SUBLANES
    run = LANE_PAIR // states
    if total % step or step % run or total // step % (2 * cols_n):
        return 0
    return total // step


def per_device(tokens, norm_gain, w_in, w_bc, rate_row, rate_col, skip_gain, w_out):
    args = (tokens, norm_gain, w_in, w_bc, rate_row, rate_col, skip_gain, w_out)
    chunks = chunk_count(tokens, rate_row, w_out.shape[0])
    if chunks:
        return per_device_grouped(chunks, *args)
    return per_device_uniform(*args)


def solution(mesh):
    placed = (P(("slides", "cols"), "rows", None), P(), P(), P(), P(), P(), P(), P())
    return jax.shard_map(
        per_device,
        mesh=mesh,
        in_specs=placed,
        out_specs=P(("slides", "cols"), "rows", None),
        check_vma=False,
    )
```

```python
import functools

import jax
import jax.numpy as jnp
from jax import lax
from jax.experimental import pallas as pl
from jax.experimental.pallas import tpu as pltpu
from jax.sharding import PartitionSpec as P

LANES = 128
VMEM_LIMIT = 60 * 1024 * 1024
MESH = pl.DeviceIdType.MESH


def normalise(tokens, gain):
    as_float = tokens.astype(jnp.float32)
    scale_now = lax.rsqrt(jnp.mean(as_float * as_float, axis=-1, keepdims=True) + 1e-05)
    return (as_float * scale_now * gain).astype(jnp.bfloat16)


def transposed_dot(a, b):
    return lax.dot_general(a, b, (((1,), (1,)), ((), ())), preferred_element_type=jnp.float32)


def spread_channels(ref, value, tiles):
    rows = value.shape[0]
    for t in range(tiles):
        ref[pl.ds(t, rows, stride=tiles), :] = value[:, t * LANES : (t + 1) * LANES]


def spread_vectors(ref, value, first, states, base):
    rows = value.shape[0]
    for n in range(states):
        ref[n, pl.ds(base, rows), :] = jnp.broadcast_to(
            value[:, first + n : first + n + 1], (rows, LANES)
        )


def scan_step(carried, decay, value, inject_ref, readout_ref, patch, start, tiles):
    new = []
    totals = [start, None]
    for n, state in enumerate(carried):
        inject = inject_ref[n, pl.ds(patch, tiles, stride=0), :]
        readout = readout_ref[n, pl.ds(patch, tiles, stride=0), :]
        state = decay[n] * state + inject * value
        term = readout * state
        totals[n % 2] = term if totals[n % 2] is None else totals[n % 2] + term
        new.append(state)
    return tuple(new), totals[0] + totals[1]


def layer_kernel(
    states, rows_n, cols_n, share, per_core,
    tok_ref, gain_in, win_in, wbc_in, rrate_in, crate_in, skip_in, wout_in,
    out_ref,
    gain_ref, win_ref, wbc_ref, rrate_ref, crate_ref, skip_ref, wout_ref, tcol, tin, rsend, rrecv, u_ref, rb_ref, rc_ref, cb_ref, cc_ref, z_ref, y_ref, gated_ref,
    rdecay, cdecay, skip_tile, stage, land, state_ref,
    tsend_sem, tin_sem, csend_sem, crecv_sem, rsend_sem, rrecv_sem, osend_sem, orecv_sem, fetch_sem,
):
    group_n = rows_n * cols_n
    pieces = tok_ref.shape[0] // share
    chunks = tin.shape[0]
    columns, width = tok_ref.shape[1:]
    inner = wout_ref.shape[0]
    tiles = inner // LANES
    piece_len = share * per_core
    chunk_len = group_n * piece_len
    blocks = stage.shape[0]
    blocks_home = blocks // cols_n
    block_len = stage.shape[1]
    r, c = lax.axis_index("rows"), lax.axis_index("cols")
    me = r * cols_n + c

    def spot(g):
        return {"rows": g // cols_n, "cols": g % cols_n}

    barrier = pltpu.get_barrier_semaphore()

    def greet(g, _):
        @pl.when(g != me)
        def _():
            pl.semaphore_signal(barrier, inc=1, device_id=spot(g), device_id_type=MESH)
        return 0

    lax.fori_loop(0, group_n, greet, 0)
    fetches = [
        pltpu.make_async_copy(src, dst, fetch_sem.at[k])
        for k, (src, dst) in enumerate((
            (rrate_in, rrate_ref), (crate_in, crate_ref), (skip_in, skip_ref), (gain_in, gain_ref),
            (wbc_in, wbc_ref), (tok_ref, tcol.at[c]), (win_in, win_ref), (wout_in, wout_ref),
        ))
    ]
    for fetch in fetches:
        fetch.start()
    pl.semaphore_wait(barrier, group_n - 1)

    local_chunks = max(1, chunks // cols_n)
    per_chunk = pieces // local_chunks

    def piece_of(k):
        piece = k // per_chunk * per_chunk + (k % per_chunk + me) % per_chunk
        place = c * pieces + piece
        return piece, place // group_n, place % group_n

    def token_copy(k):
        piece, q, g = piece_of(k)
        return g, pltpu.make_async_remote_copy(
            src_ref=tok_ref.at[pl.ds(piece * share, share)], dst_ref=tin.at[q, r],
            send_sem=tsend_sem.at[piece], recv_sem=tin_sem.at[q],
            device_id=spot(g), device_id_type=MESH,
        )

    def send_tokens(k, _):
        piece, q, g = piece_of(k)

        @pl.when(g == me)
        def _():
            pltpu.make_async_copy(tok_ref.at[pl.ds(piece * share, share)], tin.at[q, r], tin_sem.at[q]).start()

        @pl.when(g != me)
        def _():
            token_copy(k)[1].start()
        return 0

    lax.fori_loop(0, pieces, send_tokens, 0)

    def column_copy(step):
        other = (c + step) % cols_n
        return pltpu.make_async_remote_copy(
            src_ref=tok_ref, dst_ref=tcol.at[c],
            send_sem=csend_sem.at[step], recv_sem=crecv_sem.at[step],
            device_id={"cols": other}, device_id_type=MESH,
        )

    for step in range(1, cols_n):
        column_copy(step).start()

    def gate_part(tokens, core):
        tokens = tokens.astype(jnp.float32)
        own = tokens[:, :per_core]
        for k in range(1, cols_n):
            own = jnp.where(c == k, tokens[:, k * per_core : (k + 1) * per_core], own)
        normed = normalise(own.reshape(-1, width), gain_ref[...])
        count = normed.shape[0]
        base = pl.multiple_of(core * count, count)
        mixers = transposed_dot(normed, wbc_ref[...])
        mixers = mixers.astype(jnp.bfloat16).astype(jnp.float32)
        spread_vectors(cb_ref, mixers, 2 * states, states, base)
        spread_vectors(cc_ref, mixers, 3 * states, states, base)
        for k in range(0, inner, 2 * LANES):
            z_ref[pl.ds(base, count), k : k + 2 * LANES] = jnp.dot(
                normed, win_ref[:, inner + k : inner + k + 2 * LANES],
                preferred_element_type=jnp.float32,
            ).astype(jnp.bfloat16)

    for fetch in fetches:
        fetch.wait()
    spread_channels(rdecay, jnp.exp(-rrate_ref[...]), tiles)
    spread_channels(cdecay, jnp.exp(-crate_ref[...]), tiles)
    spread_channels(skip_tile, skip_ref[...], tiles)
    gate_part(tcol[c], c)

    zero = jnp.zeros((tiles, LANES), jnp.float32)
    lanes = 2 if share % 2 == 0 else 1

    def result_copy(q, k):
        g = (me + k) % group_n
        return pltpu.make_async_remote_copy(
            src_ref=rsend.at[q, pl.ds(g * piece_len, piece_len)],
            dst_ref=rrecv.at[q, pl.ds(me * piece_len, piece_len)],
            send_sem=rsend_sem.at[q, k], recv_sem=rrecv_sem.at[q],
            device_id=spot(g), device_id_type=MESH,
        )

    def row_chunk(q, _):
        pltpu.make_async_copy(tin.at[q], tin.at[q], tin_sem.at[q]).wait()
        normed = normalise(tin[q].astype(jnp.float32).reshape(chunk_len, width), gain_ref[...])
        mixers = transposed_dot(normed, wbc_ref[...])
        mixers = mixers.astype(jnp.bfloat16).astype(jnp.float32)
        spread_vectors(rb_ref, mixers, 0, states, 0)
        spread_vectors(rc_ref, mixers, states, states, 0)
        for k in range(0, tiles, 2):
            part = jnp.dot(normed, win_ref[:, k * LANES : (k + 2) * LANES],
                           preferred_element_type=jnp.float32)
            part = part.astype(jnp.bfloat16).astype(jnp.float32)
            for h in range(2):
                u_ref[pl.ds(k + h, chunk_len, stride=tiles), :] = part[:, h * LANES : (h + 1) * LANES]
        decay = [rdecay[n * tiles : (n + 1) * tiles, :] for n in range(states)]
        skip = skip_tile[...]

        def one_group(first, _):
            def one_step(j, carry):
                carry = list(carry)
                for w in range(columns):
                    for b in range(lanes):
                        row = first * lanes + b
                        patch = (j * share + row) * columns + w
                        owner = j * cols_n + w // per_core
                        value = u_ref[pl.ds(pl.multiple_of(patch * tiles, tiles), tiles), :]
                        carry[b], total = scan_step(carry[b], decay, value, rb_ref, rc_ref,
                                                    patch, skip * value, tiles)
                        rsend[q, (owner * share + row) * per_core + w % per_core] = total.astype(jnp.bfloat16)
                return tuple(carry)

            lax.fori_loop(0, rows_n, one_step, tuple((zero,) * states for _ in range(lanes)))
            return 0

        lax.fori_loop(0, share // lanes, one_group, 0)

        def send_result(k, _):
            result_copy(q, k).start()
            return 0

        pltpu.make_async_copy(
            rsend.at[q, pl.ds(me * piece_len, piece_len)],
            rrecv.at[q, pl.ds(me * piece_len, piece_len)], rrecv_sem.at[q],
        ).start()
        lax.fori_loop(1, group_n, send_result, 0)
        return 0

    lax.fori_loop(0, chunks, row_chunk, 0)

    for step in range(1, cols_n):
        column_copy(step).wait_recv()
        source = (c + cols_n - step) % cols_n
        gate_part(tcol[source], source)

    for g in range(per_core):
        for n in range(states):
            state_ref[g, n] = zero

    def out_copy(o):
        return pltpu.make_async_remote_copy(
            src_ref=stage.at[o], dst_ref=land.at[c, o % blocks_home],
            send_sem=osend_sem.at[o], recv_sem=orecv_sem.at[c, o % blocks_home],
            device_id={"cols": o // blocks_home}, device_id_type=MESH,
        )

    def col_chunk(q, _):
        pltpu.make_async_copy(rrecv.at[q], rrecv.at[q], rrecv_sem.at[q]).wait()
        decay = [cdecay[n * tiles : (n + 1) * tiles, :] for n in range(states)]
        base = q * chunk_len

        def one_step(s, carry):
            result = []
            for g in range(per_core):
                patch = s * per_core + g
                value = rrecv[q, patch].astype(jnp.float32)
                state, total = scan_step(carry[g], decay, value, cb_ref, cc_ref,
                                         base + patch, value, tiles)
                y_ref[pl.ds(pl.multiple_of(patch * tiles, tiles), tiles), :] = total
                result.append(state)
            return tuple(result)

        carry = tuple(tuple(state_ref[g, n] for n in range(states)) for g in range(per_core))
        carry = lax.fori_loop(0, chunk_len // per_core, one_step, carry)
        for g in range(per_core):
            for n in range(states):
                state_ref[g, n] = carry[g][n]
        start = pl.multiple_of(base, chunk_len)
        for t in range(tiles):
            gate = z_ref[pl.ds(start, chunk_len), t * LANES : (t + 1) * LANES].astype(jnp.float32)
            mixed = y_ref[pl.ds(t, chunk_len, stride=tiles), :]
            gated_ref[:, t * LANES : (t + 1) * LANES] = (
                mixed * (gate / (1.0 + jnp.exp(-gate)))
            ).astype(jnp.bfloat16)
        result = jnp.dot(gated_ref[...], wout_ref[...], preferred_element_type=jnp.float32)
        result = result.astype(jnp.bfloat16)
        for k in range(blocks // chunks):
            o = q * (blocks // chunks) + k
            block = result[k * block_len : (k + 1) * block_len]
            stage[o] = block

            @pl.when(o // blocks_home == c)
            def _():
                land[c, o % blocks_home] = block

            @pl.when(o // blocks_home != c)
            def _():
                out_copy(o).start()
        return 0

    lax.fori_loop(0, chunks, col_chunk, 0)

    def drain_tokens(k, _):
        g, copy = token_copy(k)

        @pl.when(g != me)
        def _():
            copy.wait_send()
        return 0

    lax.fori_loop(0, pieces, drain_tokens, 0)
    for step in range(1, cols_n):
        column_copy(step).wait_send()

    def drain_results(q, _):
        def one(k, _):
            result_copy(q, k).wait_send()
            return 0
        return lax.fori_loop(1, group_n, one, 0)

    lax.fori_loop(0, chunks, drain_results, 0)

    def drain_out(o, _):
        @pl.when(o // blocks_home != c)
        def _():
            out_copy(o).wait_send()
        return 0

    lax.fori_loop(0, blocks, drain_out, 0)
    for source in range(cols_n):
        @pl.when(source != c)
        def _():
            for i in range(blocks_home):
                pltpu.make_async_copy(
                    land.at[source, i], land.at[source, i], orecv_sem.at[source, i]
                ).wait()
    for i in range(blocks_home):
        parts = [
            land[s, i].astype(jnp.float32).reshape(block_len // per_core, per_core, -1)
            for s in range(cols_n)
        ]
        rows = block_len // per_core
        out_ref[i * rows : (i + 1) * rows] = jnp.concatenate(parts, axis=1).astype(jnp.bfloat16)


def per_device_uniform(tokens, norm_gain, w_in, w_bc, rate_row, rate_col, skip_gain, w_out):
    inner, width_out = w_out.shape
    states = rate_row.shape[0]
    height, columns, width = tokens.shape
    rows_n, cols_n = lax.axis_size("rows"), lax.axis_size("cols")
    group_n = rows_n * cols_n
    per_core = columns // cols_n
    total = height * cols_n
    share = min(4, total // group_n)
    chunks = total // (group_n * share)
    pieces = height // share
    piece_len = share * per_core
    chunk_len = group_n * piece_len
    tiles = inner // LANES
    blocks = max(chunks, cols_n)
    block_len = total * per_core // blocks
    patches = total * per_core
    f32, bf16 = jnp.float32, jnp.bfloat16
    dma = pltpu.SemaphoreType.DMA
    out = pl.pallas_call(
        functools.partial(layer_kernel, states, rows_n, cols_n, share, per_core),
        in_specs=[pl.BlockSpec(memory_space=pl.ANY)] * 8,
        out_specs=pl.BlockSpec(memory_space=pltpu.VMEM),
        out_shape=jax.ShapeDtypeStruct((height, columns, width_out), bf16),
        scratch_shapes=[
            pltpu.VMEM((1, width), f32),
            pltpu.VMEM(w_in.shape, bf16),
            pltpu.VMEM(w_bc.shape[::-1], bf16),
            pltpu.VMEM(rate_row.shape, f32),
            pltpu.VMEM(rate_col.shape, f32),
            pltpu.VMEM((1, inner), f32),
            pltpu.VMEM(w_out.shape, bf16),
            pltpu.VMEM((cols_n, height, columns, width), bf16),
            pltpu.VMEM((chunks, rows_n, share, columns, width), bf16),
            pltpu.VMEM((chunks, chunk_len, tiles, LANES), bf16),
            pltpu.VMEM((chunks, chunk_len, tiles, LANES), bf16),
            pltpu.VMEM((chunk_len * tiles, LANES), f32),
            pltpu.VMEM((states, chunk_len + 8, LANES), f32),
            pltpu.VMEM((states, chunk_len + 8, LANES), f32),
            pltpu.VMEM((states, patches + 8, LANES), f32),
            pltpu.VMEM((states, patches + 8, LANES), f32),
            pltpu.VMEM((patches, inner), bf16),
            pltpu.VMEM((chunk_len * tiles, LANES), f32),
            pltpu.VMEM((chunk_len, inner), bf16),
            pltpu.VMEM((states * tiles, LANES), f32),
            pltpu.VMEM((states * tiles, LANES), f32),
            pltpu.VMEM((tiles, LANES), f32),
            pltpu.VMEM((blocks, block_len, width_out), bf16),
            pltpu.VMEM((cols_n, blocks // cols_n, block_len, width_out), bf16),
            pltpu.VMEM((per_core, states, tiles, LANES), f32),
            dma((pieces,)), dma((chunks,)), dma((cols_n,)), dma((cols_n,)),
            dma((chunks, group_n)), dma((chunks,)), dma((blocks,)),
            dma((cols_n, blocks // cols_n)), dma((8,)),
        ],
        compiler_params=pltpu.CompilerParams(
            vmem_limit_bytes=VMEM_LIMIT, collective_id=0, has_side_effects=True
        ),
        name="layer",
    )(tokens, norm_gain[None], w_in, w_bc.T, rate_row, rate_col, skip_gain[None], w_out)
    return out


LANE_PAIR = 2 * LANES
SUBLANES = 8


def grouped_kernel(
    states, rows_n, cols_n, chunks, per_core,
    tok_ref, gain_in, win_in, wbc_in, rrate_in, crate_in, skip_in, wout_in,
    out_ref,
    gain_ref, win_ref, wbc_ref, rrate_ref, crate_ref, skip_ref, wout_ref,
    tokv, nown, ncol, tin_a, tin_b, tin_c, table, order_ref, u_ref, b_ref, c_ref, lag_ref,
    rsend, rrecv, vcol, inject_ref, spread_ref, read_ref, hist, z_ref, gated_ref, stage, land, state_ref,
    own_send_sem, own_sem, early_sem, relay_sem, csend_sem, crecv_sem, rsend_sem, rrecv_sem,
    osend_sem, orecv_sem, fetch_sem,
):
    height, columns, width = tok_ref.shape
    inner = wout_ref.shape[0]
    tiles = inner // LANES
    pairs = inner // LANE_PAIR
    quarter = rows_n // 4
    total = height * cols_n
    chunk_rows = total // chunks
    local_chunks = chunks // cols_n
    lines = quarter * cols_n
    rows = chunk_rows // lines
    run = LANE_PAIR // states
    parts = rsend_sem.shape[1]
    share = inner // parts
    r, c = lax.axis_index("rows"), lax.axis_index("cols")

    groups = ((0, quarter), (quarter, quarter), (2 * quarter, 2 * quarter))
    inside = (r < quarter, (r >= quarter) & (r < 2 * quarter), r >= 2 * quarter)
    tins = (tin_a, tin_b, tin_c)
    early = (0, quarter, 2 * quarter)
    line = r % quarter * cols_n + c

    def chip_of(group, q, p):
        chip = groups[group][0] + p // cols_n
        return chip + q % 2 * quarter if group == 2 else chip

    def slot(group, q):
        return q // 2 if group == 2 else q

    barrier = pltpu.get_barrier_semaphore()

    def greet(chip, core):
        pl.semaphore_signal(barrier, inc=1, device_id={"rows": chip, "cols": core}, device_id_type=MESH)

    for group, (first, chips) in enumerate(groups):
        @pl.when(inside[group])
        def _():
            me = (r - first) * cols_n + c

            def one(k, _):
                @pl.when(k != me)
                def _():
                    greet(first + k // cols_n, k % cols_n)
                return 0

            lax.fori_loop(0, chips * cols_n, one, 0)
            if group:
                greet(first - quarter + (r - first) % quarter, c)

    fetches = [
        pltpu.make_async_copy(src, dst, fetch_sem.at[k])
        for k, (src, dst) in enumerate((
            (tok_ref, tokv), (gain_in, gain_ref), (rrate_in, rrate_ref), (crate_in, crate_ref),
            (skip_in, skip_ref), (wbc_in, wbc_ref), (win_in, win_ref), (wout_in, wout_ref),
        ))
    ]
    for fetch in fetches:
        fetch.start()
    for fetch in fetches[:2]:
        fetch.wait()
    for first in range(0, height, chunk_rows):
        flat = normalise(tokv[first : first + chunk_rows].astype(jnp.float32).reshape(-1, width), gain_ref[...])
        flat = flat.astype(jnp.float32)
        for t in range(width // LANES):
            order_ref[t, first * columns : (first + chunk_rows) * columns] = flat[:, t * LANES : (t + 1) * LANES]
        for w in range(columns):
            nown[w, first : first + chunk_rows] = jnp.concatenate([
                order_ref[t, pl.ds(first * columns + w, chunk_rows, stride=columns), :] for t in range(width // LANES)
            ], axis=1).astype(jnp.bfloat16)

    for group, (first, chips) in enumerate(groups):
        @pl.when(inside[group])
        def _():
            pl.semaphore_wait(barrier, chips * cols_n - 1 + (1, 2, 0)[group])

    def token_copy(group, n):
        part, p = n // lines, (n + line) % lines
        q = c * local_chunks + part
        chip, core = chip_of(group, q, p), p % cols_n
        src = nown.at[:, pl.ds(pl.multiple_of(part * chunk_rows + p * rows, rows), rows)]
        dst = tins[group].at[slot(group, q), early[group] + r - groups[group][0]]
        remote = pltpu.make_async_remote_copy(
            src_ref=src, dst_ref=dst, send_sem=own_send_sem.at[n], recv_sem=own_sem.at[q],
            device_id={"rows": chip, "cols": core}, device_id_type=MESH,
        )
        away = (chip != r) | (core != c)
        return away, remote, lambda: pltpu.make_async_copy(src, dst, own_sem.at[q])

    def send_own(low, high):
        for group in range(3):
            @pl.when(inside[group])
            def _():
                def one(n, _):
                    away, remote, local = token_copy(group, n)

                    @pl.when(away)
                    def _():
                        remote.start()

                    @pl.when(jnp.logical_not(away))
                    def _():
                        local().start()
                    return 0

                lax.fori_loop(low * lines, high * lines, one, 0)

    @pl.when(c == 0)
    def _():
        send_own(0, 1)

    def column_copy(step):
        other = (c + step) % cols_n
        return pltpu.make_async_remote_copy(
            src_ref=nown.at[pl.ds(other * per_core, per_core)], dst_ref=ncol.at[c],
            send_sem=csend_sem.at[step], recv_sem=crecv_sem.at[step],
            device_id={"cols": other}, device_id_type=MESH,
        )

    for step in range(1, cols_n):
        column_copy(step).start()

    def own_wait(group, q):
        part = tins[group].at[slot(group, q), pl.ds(early[group], groups[group][1])]
        pltpu.make_async_copy(part, part, own_sem.at[q]).wait()

    def early_wait(group, q):
        part = tins[group].at[slot(group, q), pl.ds(0, early[group])]
        pltpu.make_async_copy(part, part, early_sem.at[q]).wait()

    def relay_copy(group, q, which):
        if group == 0:
            src, dst, chip = tin_a.at[q], tin_b.at[q, pl.ds(0, quarter)], r + quarter
        else:
            src = tin_b.at[q, pl.ds(which * quarter, quarter)]
            dst = tin_c.at[q // 2, pl.ds(which * quarter, quarter)]
            chip = r + quarter + q % 2 * quarter
        return pltpu.make_async_remote_copy(
            src_ref=src, dst_ref=dst, send_sem=relay_sem.at[q, which], recv_sem=early_sem.at[q],
            device_id={"rows": chip}, device_id_type=MESH,
        )

    def relay_own(group, q):
        own_wait(group, q)
        relay_copy(group, q, 1).start()

    def relay_early(group, q):
        early_wait(group, q)
        relay_copy(group, q, 0).start()

    def gate_part(core, normed_of):
        for w in range(per_core):
            normed = normed_of(w)
            base = pl.multiple_of(w * total + core * height, height)
            inject = transposed_dot(normed, wbc_ref[2 * states : 3 * states])
            inject = inject.astype(jnp.bfloat16).astype(jnp.float32)
            for n in range(states):
                inject_ref[pl.ds(base * states + n, height, stride=states), :] = jnp.broadcast_to(
                    inject[:, n : n + 1], (height, LANES)
                )
            read = transposed_dot(normed, spread_ref[...])
            owner = lax.broadcasted_iota(jnp.int32, read.shape, 1) // states
            here = lax.broadcasted_iota(jnp.int32, read.shape, 0) % run
            read_ref[pl.ds(base, height), :] = jnp.where(owner == here, read, 0.0).astype(jnp.bfloat16)
            for k in range(0, inner, LANE_PAIR):
                z_ref[pl.ds(base, height), k : k + LANE_PAIR] = jnp.dot(
                    normed, win_ref[:, inner + k : inner + k + LANE_PAIR],
                    preferred_element_type=jnp.float32,
                ).astype(jnp.bfloat16)

    for fetch in fetches[2:]:
        fetch.wait()

    for group, (first, chips) in enumerate(groups):
        @pl.when(inside[group])
        def _():
            def fill(d, _):
                for k in range(pairs):
                    rate = rrate_ref[:, k * LANE_PAIR : (k + 1) * LANE_PAIR]
                    table[k, d] = jnp.exp(-rate * d.astype(jnp.float32)).astype(jnp.bfloat16)
                return 0

            lax.fori_loop(0, (early[group] + chips) * columns, fill, 0)

    for i in range(run):
        spread_ref[i * states : (i + 1) * states] = wbc_ref[3 * states : 4 * states]
    crate_ref[...] = jnp.exp(-crate_ref[...])
    state_ref[...] = jnp.zeros(state_ref.shape, jnp.float32)
    @pl.when(c == 0)
    def _():
        send_own(1, 2)

    @pl.when(inside[0])
    def _():
        relay_own(0, 0)

    gate_part(c, lambda w: nown[c * per_core + w])

    @pl.when(c == 0)
    def _():
        send_own(2, local_chunks)

    @pl.when(inside[0])
    def _():
        relay_own(0, 1)

    @pl.when(inside[1])
    def _():
        relay_own(1, 0)

    for step in range(1, cols_n):
        column_copy(step).wait_recv()
        source = (c + cols_n - step) % cols_n
        gate_part(source, lambda w: ncol[source, w])

    @pl.when(c > 0)
    def _():
        send_own(0, local_chunks)

    @pl.when(inside[0])
    def _():
        def one(q, _):
            relay_own(0, q)
            return 0

        lax.fori_loop(2, local_chunks, one, 0)

    @pl.when(inside[1])
    def _():
        relay_early(1, 0)
        relay_own(1, 1)

    def result_copy(group, q, part, k):
        first, chips = groups[group]
        g = ((r - first) * cols_n + c + k) % (chips * cols_n)
        some = pl.ds(pl.multiple_of(part * share, share), share)
        src, dst = rsend.at[slot(group, q), g, :, :, some], rrecv.at[q, line, :, :, some]
        remote = pltpu.make_async_remote_copy(
            src_ref=src, dst_ref=dst, send_sem=rsend_sem.at[slot(group, q), part, k], recv_sem=rrecv_sem.at[q],
            device_id={"rows": first + g // cols_n, "cols": g % cols_n}, device_id_type=MESH,
        )
        return remote, lambda: pltpu.make_async_copy(src, dst, rrecv_sem.at[q])

    def row_chunk(group, q):
        chips = groups[group][1]
        before = early[group]
        at = slot(group, q)
        tin = tins[group]
        if group == 2:
            early_wait(group, q)
            own_wait(group, q)
        out_cols, pre_cols = chips * columns, before * columns
        all_cols = out_cols + pre_cols
        normed = tin[at].reshape(all_cols * rows, width)
        b_ref[: all_cols * rows] = transposed_dot(normed, wbc_ref[:states]).astype(jnp.bfloat16).astype(jnp.float32)
        c_ref[: out_cols * rows] = transposed_dot(
            normed[pre_cols * rows :], wbc_ref[states : 2 * states]
        ).astype(jnp.bfloat16).astype(jnp.float32)
        for k in range(pairs):
            u_ref[k, : all_cols * rows] = jnp.dot(
                normed, win_ref[:, k * LANE_PAIR : (k + 1) * LANE_PAIR], preferred_element_type=jnp.float32
            ).astype(jnp.bfloat16).astype(jnp.float32)

        def span(d):
            low = max(0, d - pre_cols)
            return low, out_cols - low, pre_cols + low - d

        for d in range(all_cols):
            low, count, source = span(d)
            lag_ref[d, : count * rows] = (
                c_ref[low * rows : out_cols * rows] * b_ref[source * rows : (source + count) * rows]
            ).astype(jnp.bfloat16)

        def one_pair(k):
            skip = skip_ref[k]
            sums = [
                skip * u_ref[k, (pre_cols + o) * rows : (pre_cols + o + 1) * rows] for o in range(out_cols)
            ]
            for d in range(all_cols):
                low, count, source = span(d)
                weight = jnp.dot(lag_ref[d, : count * rows], table[k, d], preferred_element_type=jnp.float32)
                for i in range(count):
                    sums[low + i] += weight[i * rows : (i + 1) * rows] * u_ref[
                        k, (source + i) * rows : (source + i + 1) * rows
                    ]
            some = pl.ds(pl.multiple_of(k * LANE_PAIR, LANE_PAIR), LANE_PAIR)
            for o in range(out_cols):
                rsend[at, o // per_core, o % per_core, :, some] = sums[o].astype(jnp.bfloat16)

        def one_part(part, _):
            for k in range(pairs // parts):
                one_pair(part * (pairs // parts) + k)
            result_copy(group, q, part, 0)[1]().start()

            def send_result(k, _):
                result_copy(group, q, part, k)[0].start()
                return 0

            lax.fori_loop(1, chips * cols_n, send_result, 0)
            return 0

        lax.fori_loop(0, parts, one_part, 0)

    def out_copy(q):
        return pltpu.make_async_remote_copy(
            src_ref=stage.at[q], dst_ref=land.at[c, q % local_chunks],
            send_sem=osend_sem.at[q], recv_sem=orecv_sem.at[c, q % local_chunks],
            device_id={"cols": q // local_chunks}, device_id_type=MESH,
        )

    def col_chunk(q):
        pltpu.make_async_copy(rrecv.at[q], rrecv.at[q], rrecv_sem.at[q]).wait()
        for p in range(lines):
            for w in range(per_core):
                value = rrecv[q, p, w].astype(jnp.float32)
                for t in range(tiles):
                    vcol[t, w * chunk_rows + p * rows : w * chunk_rows + (p + 1) * rows] = (
                        value[:, t * LANES : (t + 1) * LANES]
                    )
        halves = range(0, states, SUBLANES)

        def one_run(i):
            for w in range(per_core):
                here = w * chunk_rows + i * run
                patch = pl.multiple_of(w * total + q * chunk_rows + i * run, run)
                decay = [[crate_ref[h : h + SUBLANES, t * LANES : (t + 1) * LANES] for t in range(tiles)] for h in halves]
                state = [[state_ref[w, h : h + SUBLANES, t * LANES : (t + 1) * LANES] for t in range(tiles)] for h in halves]
                for s in range(run):
                    inject = [
                        inject_ref[pl.ds(pl.multiple_of((patch + s) * states + h, SUBLANES), SUBLANES), :] for h in halves
                    ]
                    for t in range(tiles):
                        value = vcol[t, pl.ds(here + s, SUBLANES, stride=0), :]
                        for j in range(len(inject)):
                            state[j][t] = decay[j][t] * state[j][t] + inject[j] * value
                        hist[i * per_core + w, t, s * states : (s + 1) * states, :] = jnp.concatenate(
                            [state[j][t] for j in range(len(inject))], axis=0
                        ).astype(jnp.bfloat16)
                for j, h in enumerate(halves):
                    for t in range(tiles):
                        state_ref[w, h : h + SUBLANES, t * LANES : (t + 1) * LANES] = state[j][t]
                for t in range(tiles):
                    if t % 2 == 0:
                        both_tiles = jnp.concatenate([hist[i * per_core + w, t], hist[i * per_core + w, t + 1]], axis=1)
                        mixed = jnp.dot(
                            read_ref[pl.ds(patch, run), :], both_tiles, preferred_element_type=jnp.float32
                        )
                    gate = z_ref[pl.ds(patch, run), t * LANES : (t + 1) * LANES].astype(jnp.float32)
                    both = mixed[:, t % 2 * LANES : (t % 2 + 1) * LANES] + vcol[t, pl.ds(here, run), :]
                    gated_ref[pl.ds(here, run), t * LANES : (t + 1) * LANES] = (
                        both * (gate / (1.0 + jnp.exp(-gate)))
                    ).astype(jnp.bfloat16)

        for i in range(chunk_rows // run):
            one_run(i)
        result = jnp.dot(gated_ref[...], wout_ref[...], preferred_element_type=jnp.float32).astype(jnp.bfloat16)
        home = q // local_chunks

        @pl.when(home == c)
        def _():
            land[c, q % local_chunks] = result

        @pl.when(home != c)
        def _():
            stage[q] = result
            out_copy(q).start()

    def one_chunk(q, _):
        for group in range(3):
            mine = inside[group] & (q < chunks)
            if group == 2:
                mine = mine & (q % 2 == (r - 2 * quarter) // quarter)

            @pl.when(mine)
            def _():
                row_chunk(group, q)

            if group == 0:
                @pl.when(inside[group] & (q + local_chunks < chunks))
                def _():
                    relay_own(group, q + local_chunks)
            if group == 1:
                @pl.when(inside[group] & (q + 1 < chunks))
                def _():
                    relay_early(group, q + 1)

                @pl.when(inside[group] & (q + 2 < chunks))
                def _():
                    relay_own(group, q + 2)

        @pl.when(q >= lag)
        def _():
            col_chunk(q - lag)
        return 0

    lag = 2
    lax.fori_loop(0, chunks + lag, one_chunk, 0)

    for group, (first, chips) in enumerate(groups):
        @pl.when(inside[group])
        def _():
            def drain_tokens(n, _):
                away, remote, _ = token_copy(group, n)

                @pl.when(away)
                def _():
                    remote.wait_send()
                return 0

            lax.fori_loop(0, local_chunks * lines, drain_tokens, 0)

            def drain_chunk(q, _):
                if group < 2:
                    relay_copy(group, q, 1).wait_send()
                if group == 1:
                    relay_copy(group, q, 0).wait_send()

                def one(k, _):
                    for part in range(parts):
                        result_copy(group, q, part, k)[0].wait_send()
                    return 0

                if group == 2:
                    @pl.when(q % 2 == (r - 2 * quarter) // quarter)
                    def _():
                        lax.fori_loop(1, chips * cols_n, one, 0)
                else:
                    lax.fori_loop(1, chips * cols_n, one, 0)
                return 0

            lax.fori_loop(0, chunks, drain_chunk, 0)

    for step in range(1, cols_n):
        column_copy(step).wait_send()

    def drain_out(q, _):
        @pl.when(q // local_chunks != c)
        def _():
            out_copy(q).wait_send()
        return 0

    lax.fori_loop(0, chunks, drain_out, 0)
    for source in range(cols_n):
        @pl.when(source != c)
        def _():
            for i in range(local_chunks):
                pltpu.make_async_copy(
                    land.at[source, i], land.at[source, i], orecv_sem.at[source, i]
                ).wait()
    for source in range(cols_n):
        for i in range(local_chunks):
            for w in range(per_core):
                out_ref[source * per_core + w, i * chunk_rows : (i + 1) * chunk_rows] = (
                    land[source, i, w * chunk_rows : (w + 1) * chunk_rows]
                )


def per_device_grouped(chunks, tokens, norm_gain, w_in, w_bc, rate_row, rate_col, skip_gain, w_out):
    inner, width_out = w_out.shape
    states = rate_row.shape[0]
    height, columns, width = tokens.shape
    rows_n, cols_n = lax.axis_size("rows"), lax.axis_size("cols")
    quarter = rows_n // 4
    per_core = columns // cols_n
    total = height * cols_n
    chunk_rows = total // chunks
    lines = quarter * cols_n
    rows = chunk_rows // lines
    tiles = inner // LANES
    pairs = inner // LANE_PAIR
    patches = total * per_core
    local_chunks = chunks // cols_n
    lags = rows_n * columns
    held = lags * rows
    outs = 2 * quarter * columns * rows
    f32, bf16 = jnp.float32, jnp.bfloat16
    dma = pltpu.SemaphoreType.DMA
    out = pl.pallas_call(
        functools.partial(grouped_kernel, states, rows_n, cols_n, chunks, per_core),
        in_specs=[pl.BlockSpec(memory_space=pl.ANY)] * 8,
        out_specs=pl.BlockSpec(memory_space=pltpu.VMEM),
        out_shape=jax.ShapeDtypeStruct((columns, height, width_out), bf16),
        scratch_shapes=[
            pltpu.VMEM((1, width), f32),
            pltpu.VMEM(w_in.shape, bf16),
            pltpu.VMEM(w_bc.shape[::-1], bf16),
            pltpu.VMEM(rate_row.shape, f32),
            pltpu.VMEM(rate_col.shape, f32),
            pltpu.VMEM((pairs, 1, LANE_PAIR), f32),
            pltpu.VMEM(w_out.shape, bf16),
            pltpu.VMEM((height, columns, width), bf16),
            pltpu.VMEM((columns, height, width), bf16),
            pltpu.VMEM((cols_n, per_core, height, width), bf16),
            pltpu.VMEM((chunks, quarter, columns, rows, width), bf16),
            pltpu.VMEM((chunks, 2 * quarter, columns, rows, width), bf16),
            pltpu.VMEM((chunks // 2, 4 * quarter, columns, rows, width), bf16),
            pltpu.VMEM((pairs, lags, states, LANE_PAIR), bf16),
            pltpu.VMEM((width // LANES, height * columns, LANES), f32),
            pltpu.VMEM((pairs, held, LANE_PAIR), f32),
            pltpu.VMEM((held, states), f32),
            pltpu.VMEM((outs, states), f32),
            pltpu.VMEM((lags, outs, states), bf16),
            pltpu.VMEM((chunks, 2 * lines, per_core, rows, inner), bf16),
            pltpu.VMEM((chunks, lines, per_core, rows, inner), bf16),
            pltpu.VMEM((tiles, per_core * chunk_rows + SUBLANES, LANES), f32),
            pltpu.VMEM((patches * states, LANES), f32),
            pltpu.VMEM((LANE_PAIR, width), bf16),
            pltpu.VMEM((patches, LANE_PAIR), bf16),
            pltpu.VMEM((per_core * chunk_rows * states // LANE_PAIR, tiles, LANE_PAIR, LANES), bf16),
            pltpu.VMEM((patches, inner), bf16),
            pltpu.VMEM((per_core * chunk_rows, inner), bf16),
            pltpu.VMEM((chunks, per_core * chunk_rows, width_out), bf16),
            pltpu.VMEM((cols_n, local_chunks, per_core * chunk_rows, width_out), bf16),
            pltpu.VMEM((per_core, states, inner), f32),
            dma((local_chunks * lines,)), dma((chunks,)), dma((chunks,)), dma((chunks, 2)),
            dma((cols_n,)), dma((cols_n,)),
            dma((chunks, 2, 2 * lines)), dma((chunks,)), dma((chunks,)),
            dma((cols_n, local_chunks)), dma((8,)),
        ],
        compiler_params=pltpu.CompilerParams(
            vmem_limit_bytes=VMEM_LIMIT, collective_id=0, has_side_effects=True
        ),
        name="layer",
    )(
        tokens, norm_gain[None], w_in, w_bc.T, rate_row, rate_col,
        skip_gain.reshape(pairs, 1, LANE_PAIR), w_out,
    )
    return out.transpose(1, 0, 2)


def chunk_count(tokens, rate_row, inner):
    height, columns, _ = tokens.shape
    states = rate_row.shape[0]
    rows_n, cols_n = lax.axis_size("rows"), lax.axis_size("cols")
    total = height * cols_n
    if rows_n % 4 or columns % cols_n or inner % LANE_PAIR or states % SUBLANES or LANE_PAIR % states:
        return 0
    step = rows_n // 4 * cols_n * SUBLANES
    run = LANE_PAIR // states
    if total % step or step % run or total // step % (2 * cols_n):
        return 0
    return total // step


def per_device(tokens, norm_gain, w_in, w_bc, rate_row, rate_col, skip_gain, w_out):
    args = (tokens, norm_gain, w_in, w_bc, rate_row, rate_col, skip_gain, w_out)
    chunks = chunk_count(tokens, rate_row, w_out.shape[0])
    if chunks:
        return per_device_grouped(chunks, *args)
    return per_device_uniform(*args)


def solution(mesh):
    placed = (P(("slides", "cols"), "rows", None), P(), P(), P(), P(), P(), P(), P())
    return jax.shard_map(
        per_device,
        mesh=mesh,
        in_specs=placed,
        out_specs=P(("slides", "cols"), "rows", None),
        check_vma=False,
    )
```

```python
import functools

import jax
import jax.numpy as jnp
from jax import lax
from jax.experimental import pallas as pl
from jax.experimental.pallas import tpu as pltpu
from jax.sharding import PartitionSpec as P

LANES = 128
VMEM_LIMIT = 60 * 1024 * 1024
MESH = pl.DeviceIdType.MESH


def normalise(tokens, gain):
    as_float = tokens.astype(jnp.float32)
    scale_now = lax.rsqrt(jnp.mean(as_float * as_float, axis=-1, keepdims=True) + 1e-05)
    return (as_float * scale_now * gain).astype(jnp.bfloat16)


def transposed_dot(a, b):
    return lax.dot_general(a, b, (((1,), (1,)), ((), ())), preferred_element_type=jnp.float32)


def spread_channels(ref, value, tiles):
    rows = value.shape[0]
    for t in range(tiles):
        ref[pl.ds(t, rows, stride=tiles), :] = value[:, t * LANES : (t + 1) * LANES]


def spread_vectors(ref, value, first, states, base):
    rows = value.shape[0]
    for n in range(states):
        ref[n, pl.ds(base, rows), :] = jnp.broadcast_to(
            value[:, first + n : first + n + 1], (rows, LANES)
        )


def scan_step(carried, decay, value, inject_ref, readout_ref, patch, start, tiles):
    new = []
    totals = [start, None]
    for n, state in enumerate(carried):
        inject = inject_ref[n, pl.ds(patch, tiles, stride=0), :]
        readout = readout_ref[n, pl.ds(patch, tiles, stride=0), :]
        state = decay[n] * state + inject * value
        term = readout * state
        totals[n % 2] = term if totals[n % 2] is None else totals[n % 2] + term
        new.append(state)
    return tuple(new), totals[0] + totals[1]


def layer_kernel(
    states, rows_n, cols_n, share, per_core,
    tok_ref, gain_in, win_in, wbc_in, rrate_in, crate_in, skip_in, wout_in,
    out_ref,
    gain_ref, win_ref, wbc_ref, rrate_ref, crate_ref, skip_ref, wout_ref, tcol, tin, rsend, rrecv, u_ref, rb_ref, rc_ref, cb_ref, cc_ref, z_ref, y_ref, gated_ref,
    rdecay, cdecay, skip_tile, stage, land, state_ref,
    tsend_sem, tin_sem, csend_sem, crecv_sem, rsend_sem, rrecv_sem, osend_sem, orecv_sem, fetch_sem,
):
    group_n = rows_n * cols_n
    pieces = tok_ref.shape[0] // share
    chunks = tin.shape[0]
    columns, width = tok_ref.shape[1:]
    inner = wout_ref.shape[0]
    tiles = inner // LANES
    piece_len = share * per_core
    chunk_len = group_n * piece_len
    blocks = stage.shape[0]
    blocks_home = blocks // cols_n
    block_len = stage.shape[1]
    r, c = lax.axis_index("rows"), lax.axis_index("cols")
    me = r * cols_n + c

    def spot(g):
        return {"rows": g // cols_n, "cols": g % cols_n}

    barrier = pltpu.get_barrier_semaphore()

    def greet(g, _):
        @pl.when(g != me)
        def _():
            pl.semaphore_signal(barrier, inc=1, device_id=spot(g), device_id_type=MESH)
        return 0

    lax.fori_loop(0, group_n, greet, 0)
    fetches = [
        pltpu.make_async_copy(src, dst, fetch_sem.at[k])
        for k, (src, dst) in enumerate((
            (rrate_in, rrate_ref), (crate_in, crate_ref), (skip_in, skip_ref), (gain_in, gain_ref),
            (wbc_in, wbc_ref), (tok_ref, tcol.at[c]), (win_in, win_ref), (wout_in, wout_ref),
        ))
    ]
    for fetch in fetches:
        fetch.start()
    pl.semaphore_wait(barrier, group_n - 1)

    local_chunks = max(1, chunks // cols_n)
    per_chunk = pieces // local_chunks

    def piece_of(k):
        piece = k // per_chunk * per_chunk + (k % per_chunk + me) % per_chunk
        place = c * pieces + piece
        return piece, place // group_n, place % group_n

    def token_copy(k):
        piece, q, g = piece_of(k)
        return g, pltpu.make_async_remote_copy(
            src_ref=tok_ref.at[pl.ds(piece * share, share)], dst_ref=tin.at[q, r],
            send_sem=tsend_sem.at[piece], recv_sem=tin_sem.at[q],
            device_id=spot(g), device_id_type=MESH,
        )

    def send_tokens(k, _):
        piece, q, g = piece_of(k)

        @pl.when(g == me)
        def _():
            pltpu.make_async_copy(tok_ref.at[pl.ds(piece * share, share)], tin.at[q, r], tin_sem.at[q]).start()

        @pl.when(g != me)
        def _():
            token_copy(k)[1].start()
        return 0

    lax.fori_loop(0, pieces, send_tokens, 0)

    def column_copy(step):
        other = (c + step) % cols_n
        return pltpu.make_async_remote_copy(
            src_ref=tok_ref, dst_ref=tcol.at[c],
            send_sem=csend_sem.at[step], recv_sem=crecv_sem.at[step],
            device_id={"cols": other}, device_id_type=MESH,
        )

    for step in range(1, cols_n):
        column_copy(step).start()

    def gate_part(tokens, core):
        tokens = tokens.astype(jnp.float32)
        own = tokens[:, :per_core]
        for k in range(1, cols_n):
            own = jnp.where(c == k, tokens[:, k * per_core : (k + 1) * per_core], own)
        normed = normalise(own.reshape(-1, width), gain_ref[...])
        count = normed.shape[0]
        base = pl.multiple_of(core * count, count)
        mixers = transposed_dot(normed, wbc_ref[...])
        mixers = mixers.astype(jnp.bfloat16).astype(jnp.float32)
        spread_vectors(cb_ref, mixers, 2 * states, states, base)
        spread_vectors(cc_ref, mixers, 3 * states, states, base)
        for k in range(0, inner, 2 * LANES):
            z_ref[pl.ds(base, count), k : k + 2 * LANES] = jnp.dot(
                normed, win_ref[:, inner + k : inner + k + 2 * LANES],
                preferred_element_type=jnp.float32,
            ).astype(jnp.bfloat16)

    for fetch in fetches:
        fetch.wait()
    spread_channels(rdecay, jnp.exp(-rrate_ref[...]), tiles)
    spread_channels(cdecay, jnp.exp(-crate_ref[...]), tiles)
    spread_channels(skip_tile, skip_ref[...], tiles)
    gate_part(tcol[c], c)

    zero = jnp.zeros((tiles, LANES), jnp.float32)
    lanes = 2 if share % 2 == 0 else 1

    def result_copy(q, k):
        g = (me + k) % group_n
        return pltpu.make_async_remote_copy(
            src_ref=rsend.at[q, pl.ds(g * piece_len, piece_len)],
            dst_ref=rrecv.at[q, pl.ds(me * piece_len, piece_len)],
            send_sem=rsend_sem.at[q, k], recv_sem=rrecv_sem.at[q],
            device_id=spot(g), device_id_type=MESH,
        )

    def row_chunk(q, _):
        pltpu.make_async_copy(tin.at[q], tin.at[q], tin_sem.at[q]).wait()
        normed = normalise(tin[q].astype(jnp.float32).reshape(chunk_len, width), gain_ref[...])
        mixers = transposed_dot(normed, wbc_ref[...])
        mixers = mixers.astype(jnp.bfloat16).astype(jnp.float32)
        spread_vectors(rb_ref, mixers, 0, states, 0)
        spread_vectors(rc_ref, mixers, states, states, 0)
        for k in range(0, tiles, 2):
            part = jnp.dot(normed, win_ref[:, k * LANES : (k + 2) * LANES],
                           preferred_element_type=jnp.float32)
            part = part.astype(jnp.bfloat16).astype(jnp.float32)
            for h in range(2):
                u_ref[pl.ds(k + h, chunk_len, stride=tiles), :] = part[:, h * LANES : (h + 1) * LANES]
        decay = [rdecay[n * tiles : (n + 1) * tiles, :] for n in range(states)]
        skip = skip_tile[...]

        def one_group(first, _):
            def one_step(j, carry):
                carry = list(carry)
                for w in range(columns):
                    for b in range(lanes):
                        row = first * lanes + b
                        patch = (j * share + row) * columns + w
                        owner = j * cols_n + w // per_core
                        value = u_ref[pl.ds(pl.multiple_of(patch * tiles, tiles), tiles), :]
                        carry[b], total = scan_step(carry[b], decay, value, rb_ref, rc_ref,
                                                    patch, skip * value, tiles)
                        rsend[q, (owner * share + row) * per_core + w % per_core] = total.astype(jnp.bfloat16)
                return tuple(carry)

            lax.fori_loop(0, rows_n, one_step, tuple((zero,) * states for _ in range(lanes)))
            return 0

        lax.fori_loop(0, share // lanes, one_group, 0)

        def send_result(k, _):
            result_copy(q, k).start()
            return 0

        pltpu.make_async_copy(
            rsend.at[q, pl.ds(me * piece_len, piece_len)],
            rrecv.at[q, pl.ds(me * piece_len, piece_len)], rrecv_sem.at[q],
        ).start()
        lax.fori_loop(1, group_n, send_result, 0)
        return 0

    lax.fori_loop(0, chunks, row_chunk, 0)

    for step in range(1, cols_n):
        column_copy(step).wait_recv()
        source = (c + cols_n - step) % cols_n
        gate_part(tcol[source], source)

    for g in range(per_core):
        for n in range(states):
            state_ref[g, n] = zero

    def out_copy(o):
        return pltpu.make_async_remote_copy(
            src_ref=stage.at[o], dst_ref=land.at[c, o % blocks_home],
            send_sem=osend_sem.at[o], recv_sem=orecv_sem.at[c, o % blocks_home],
            device_id={"cols": o // blocks_home}, device_id_type=MESH,
        )

    def col_chunk(q, _):
        pltpu.make_async_copy(rrecv.at[q], rrecv.at[q], rrecv_sem.at[q]).wait()
        decay = [cdecay[n * tiles : (n + 1) * tiles, :] for n in range(states)]
        base = q * chunk_len

        def one_step(s, carry):
            result = []
            for g in range(per_core):
                patch = s * per_core + g
                value = rrecv[q, patch].astype(jnp.float32)
                state, total = scan_step(carry[g], decay, value, cb_ref, cc_ref,
                                         base + patch, value, tiles)
                y_ref[pl.ds(pl.multiple_of(patch * tiles, tiles), tiles), :] = total
                result.append(state)
            return tuple(result)

        carry = tuple(tuple(state_ref[g, n] for n in range(states)) for g in range(per_core))
        carry = lax.fori_loop(0, chunk_len // per_core, one_step, carry)
        for g in range(per_core):
            for n in range(states):
                state_ref[g, n] = carry[g][n]
        start = pl.multiple_of(base, chunk_len)
        for t in range(tiles):
            gate = z_ref[pl.ds(start, chunk_len), t * LANES : (t + 1) * LANES].astype(jnp.float32)
            mixed = y_ref[pl.ds(t, chunk_len, stride=tiles), :]
            gated_ref[:, t * LANES : (t + 1) * LANES] = (
                mixed * (gate / (1.0 + jnp.exp(-gate)))
            ).astype(jnp.bfloat16)
        result = jnp.dot(gated_ref[...], wout_ref[...], preferred_element_type=jnp.float32)
        result = result.astype(jnp.bfloat16)
        for k in range(blocks // chunks):
            o = q * (blocks // chunks) + k
            block = result[k * block_len : (k + 1) * block_len]
            stage[o] = block

            @pl.when(o // blocks_home == c)
            def _():
                land[c, o % blocks_home] = block

            @pl.when(o // blocks_home != c)
            def _():
                out_copy(o).start()
        return 0

    lax.fori_loop(0, chunks, col_chunk, 0)

    def drain_tokens(k, _):
        g, copy = token_copy(k)

        @pl.when(g != me)
        def _():
            copy.wait_send()
        return 0

    lax.fori_loop(0, pieces, drain_tokens, 0)
    for step in range(1, cols_n):
        column_copy(step).wait_send()

    def drain_results(q, _):
        def one(k, _):
            result_copy(q, k).wait_send()
            return 0
        return lax.fori_loop(1, group_n, one, 0)

    lax.fori_loop(0, chunks, drain_results, 0)

    def drain_out(o, _):
        @pl.when(o // blocks_home != c)
        def _():
            out_copy(o).wait_send()
        return 0

    lax.fori_loop(0, blocks, drain_out, 0)
    for source in range(cols_n):
        @pl.when(source != c)
        def _():
            for i in range(blocks_home):
                pltpu.make_async_copy(
                    land.at[source, i], land.at[source, i], orecv_sem.at[source, i]
                ).wait()
    for i in range(blocks_home):
        parts = [
            land[s, i].astype(jnp.float32).reshape(block_len // per_core, per_core, -1)
            for s in range(cols_n)
        ]
        rows = block_len // per_core
        out_ref[i * rows : (i + 1) * rows] = jnp.concatenate(parts, axis=1).astype(jnp.bfloat16)


def per_device_uniform(tokens, norm_gain, w_in, w_bc, rate_row, rate_col, skip_gain, w_out):
    inner, width_out = w_out.shape
    states = rate_row.shape[0]
    height, columns, width = tokens.shape
    rows_n, cols_n = lax.axis_size("rows"), lax.axis_size("cols")
    group_n = rows_n * cols_n
    per_core = columns // cols_n
    total = height * cols_n
    share = min(4, total // group_n)
    chunks = total // (group_n * share)
    pieces = height // share
    piece_len = share * per_core
    chunk_len = group_n * piece_len
    tiles = inner // LANES
    blocks = max(chunks, cols_n)
    block_len = total * per_core // blocks
    patches = total * per_core
    f32, bf16 = jnp.float32, jnp.bfloat16
    dma = pltpu.SemaphoreType.DMA
    out = pl.pallas_call(
        functools.partial(layer_kernel, states, rows_n, cols_n, share, per_core),
        in_specs=[pl.BlockSpec(memory_space=pl.ANY)] * 8,
        out_specs=pl.BlockSpec(memory_space=pltpu.VMEM),
        out_shape=jax.ShapeDtypeStruct((height, columns, width_out), bf16),
        scratch_shapes=[
            pltpu.VMEM((1, width), f32),
            pltpu.VMEM(w_in.shape, bf16),
            pltpu.VMEM(w_bc.shape[::-1], bf16),
            pltpu.VMEM(rate_row.shape, f32),
            pltpu.VMEM(rate_col.shape, f32),
            pltpu.VMEM((1, inner), f32),
            pltpu.VMEM(w_out.shape, bf16),
            pltpu.VMEM((cols_n, height, columns, width), bf16),
            pltpu.VMEM((chunks, rows_n, share, columns, width), bf16),
            pltpu.VMEM((chunks, chunk_len, tiles, LANES), bf16),
            pltpu.VMEM((chunks, chunk_len, tiles, LANES), bf16),
            pltpu.VMEM((chunk_len * tiles, LANES), f32),
            pltpu.VMEM((states, chunk_len + 8, LANES), f32),
            pltpu.VMEM((states, chunk_len + 8, LANES), f32),
            pltpu.VMEM((states, patches + 8, LANES), f32),
            pltpu.VMEM((states, patches + 8, LANES), f32),
            pltpu.VMEM((patches, inner), bf16),
            pltpu.VMEM((chunk_len * tiles, LANES), f32),
            pltpu.VMEM((chunk_len, inner), bf16),
            pltpu.VMEM((states * tiles, LANES), f32),
            pltpu.VMEM((states * tiles, LANES), f32),
            pltpu.VMEM((tiles, LANES), f32),
            pltpu.VMEM((blocks, block_len, width_out), bf16),
            pltpu.VMEM((cols_n, blocks // cols_n, block_len, width_out), bf16),
            pltpu.VMEM((per_core, states, tiles, LANES), f32),
            dma((pieces,)), dma((chunks,)), dma((cols_n,)), dma((cols_n,)),
            dma((chunks, group_n)), dma((chunks,)), dma((blocks,)),
            dma((cols_n, blocks // cols_n)), dma((8,)),
        ],
        compiler_params=pltpu.CompilerParams(
            vmem_limit_bytes=VMEM_LIMIT, collective_id=0, has_side_effects=True
        ),
        name="layer",
    )(tokens, norm_gain[None], w_in, w_bc.T, rate_row, rate_col, skip_gain[None], w_out)
    return out


LANE_PAIR = 2 * LANES
SUBLANES = 8


def grouped_kernel(
    states, rows_n, cols_n, chunks, per_core,
    tok_ref, gain_in, win_in, wbc_in, rrate_in, crate_in, skip_in, wout_in,
    out_ref,
    gain_ref, win_ref, wbc_ref, rrate_ref, crate_ref, skip_ref, wout_ref,
    tokv, nown, ncol, tin_a, tin_b, tin_c, table, order_ref, u_ref, b_ref, c_ref, lag_ref,
    rsend, rrecv, vcol, inject_ref, spread_ref, read_ref, hist, z_ref, gated_ref, stage, land, state_ref,
    own_send_sem, own_sem, early_sem, relay_sem, csend_sem, crecv_sem, rsend_sem, rrecv_sem,
    osend_sem, orecv_sem, fetch_sem, ready_sem,
):
    height, columns, width = tok_ref.shape
    inner = wout_ref.shape[0]
    tiles = inner // LANES
    pairs = inner // LANE_PAIR
    quarter = rows_n // 4
    total = height * cols_n
    chunk_rows = total // chunks
    local_chunks = chunks // cols_n
    lines = quarter * cols_n
    rows = chunk_rows // lines
    run = LANE_PAIR // states
    parts = rsend_sem.shape[1]
    share = inner // parts
    r, c = lax.axis_index("rows"), lax.axis_index("cols")

    groups = ((0, quarter), (quarter, quarter), (2 * quarter, 2 * quarter))
    inside = (r < quarter, (r >= quarter) & (r < 2 * quarter), r >= 2 * quarter)
    tins = (tin_a, tin_b, tin_c)
    early = (0, quarter, 2 * quarter)
    line = r % quarter * cols_n + c

    def chip_of(group, q, p):
        chip = groups[group][0] + p // cols_n
        return chip + q % 2 * quarter if group == 2 else chip

    def slot(group, q):
        return q // 2 if group == 2 else q

    barrier = pltpu.get_barrier_semaphore()

    def greet(chip, core):
        pl.semaphore_signal(barrier, inc=1, device_id={"rows": chip, "cols": core}, device_id_type=MESH)

    for group, (first, chips) in enumerate(groups):
        @pl.when(inside[group])
        def _():
            me = (r - first) * cols_n + c

            def one(k, _):
                @pl.when(k != me)
                def _():
                    greet(first + k // cols_n, k % cols_n)
                return 0

            lax.fori_loop(0, chips * cols_n, one, 0)
            if group < 2:
                for k in range(group + 1):
                    greet(r + (k + 1) * quarter, c)

    head, rest = pl.ds(0, chunk_rows), pl.ds(chunk_rows, height - chunk_rows)
    fetches = [
        pltpu.make_async_copy(src, dst, fetch_sem.at[k])
        for k, (src, dst) in enumerate((
            (tok_ref.at[head], tokv.at[head]), (gain_in, gain_ref), (tok_ref.at[rest], tokv.at[rest]),
            (rrate_in, rrate_ref), (wbc_in, wbc_ref), (win_in, win_ref),
            (crate_in, crate_ref), (skip_in, skip_ref), (wout_in, wout_ref),
        ))
    ]
    for fetch in fetches:
        fetch.start()

    def normalise_part(part):
        first = part * chunk_rows
        flat = normalise(tokv[first : first + chunk_rows].astype(jnp.float32).reshape(-1, width), gain_ref[...])
        flat = flat.astype(jnp.float32)
        for t in range(width // LANES):
            order_ref[t, first * columns : (first + chunk_rows) * columns] = flat[:, t * LANES : (t + 1) * LANES]
        for w in range(columns):
            nown[w, first : first + chunk_rows] = jnp.concatenate([
                order_ref[t, pl.ds(first * columns + w, chunk_rows, stride=columns), :] for t in range(width // LANES)
            ], axis=1).astype(jnp.bfloat16)

    for fetch in fetches[:2]:
        fetch.wait()
    normalise_part(0)

    for group, (first, chips) in enumerate(groups):
        @pl.when(inside[group])
        def _():
            pl.semaphore_wait(barrier, chips * cols_n - 1 + (group > 0))
            if group:
                pl.semaphore_signal(
                    ready_sem, inc=1, device_id={"rows": first - quarter + (r - first) % quarter}, device_id_type=MESH
                )

    def token_copy(group, n):
        part, p = n // lines, (n + line) % lines
        q = c * local_chunks + part
        chip, core = chip_of(group, q, p), p % cols_n
        src = nown.at[:, pl.ds(pl.multiple_of(part * chunk_rows + p * rows, rows), rows)]
        dst = tins[group].at[slot(group, q), early[group] + r - groups[group][0]]
        remote = pltpu.make_async_remote_copy(
            src_ref=src, dst_ref=dst, send_sem=own_send_sem.at[n], recv_sem=own_sem.at[q],
            device_id={"rows": chip, "cols": core}, device_id_type=MESH,
        )
        away = (chip != r) | (core != c)
        return away, remote, lambda: pltpu.make_async_copy(src, dst, own_sem.at[q])

    def send_own(low, high):
        for group in range(3):
            @pl.when(inside[group])
            def _():
                def one(n, _):
                    away, remote, local = token_copy(group, n)

                    @pl.when(away)
                    def _():
                        remote.start()

                    @pl.when(jnp.logical_not(away))
                    def _():
                        local().start()
                    return 0

                lax.fori_loop(low * lines, high * lines, one, 0)

    @pl.when(c == 0)
    def _():
        send_own(0, 1)

    fetches[2].wait()
    for part in range(1, local_chunks):
        normalise_part(part)

    def column_copy(step):
        other = (c + step) % cols_n
        return pltpu.make_async_remote_copy(
            src_ref=nown.at[pl.ds(other * per_core, per_core)], dst_ref=ncol.at[c],
            send_sem=csend_sem.at[step], recv_sem=crecv_sem.at[step],
            device_id={"cols": other}, device_id_type=MESH,
        )

    for step in range(1, cols_n):
        column_copy(step).start()

    def own_wait(group, q):
        part = tins[group].at[slot(group, q), pl.ds(early[group], groups[group][1])]
        pltpu.make_async_copy(part, part, own_sem.at[q]).wait()

    def early_wait(group, q):
        part = tins[group].at[slot(group, q), pl.ds(0, early[group])]
        pltpu.make_async_copy(part, part, early_sem.at[q]).wait()

    def relay_copy(group, q, which):
        if group == 0:
            src, dst, chip = tin_a.at[q], tin_b.at[q, pl.ds(0, quarter)], r + quarter
        else:
            src = tin_b.at[q, pl.ds(which * quarter, quarter)]
            dst = tin_c.at[q // 2, pl.ds(which * quarter, quarter)]
            chip = r + quarter + q % 2 * quarter
        return pltpu.make_async_remote_copy(
            src_ref=src, dst_ref=dst, send_sem=relay_sem.at[q, which], recv_sem=early_sem.at[q],
            device_id={"rows": chip}, device_id_type=MESH,
        )

    def relay_own(group, q):
        own_wait(group, q)
        relay_copy(group, q, 1).start()

    def relay_early(group, q):
        early_wait(group, q)
        relay_copy(group, q, 0).start()

    def gate_part(core, normed_of):
        for w in range(per_core):
            normed = normed_of(w)
            base = pl.multiple_of(w * total + core * height, height)
            inject = transposed_dot(normed, wbc_ref[2 * states : 3 * states])
            inject = inject.astype(jnp.bfloat16).astype(jnp.float32)
            for n in range(states):
                inject_ref[pl.ds(base * states + n, height, stride=states), :] = jnp.broadcast_to(
                    inject[:, n : n + 1], (height, LANES)
                )
            read = transposed_dot(normed, spread_ref[...])
            owner = lax.broadcasted_iota(jnp.int32, read.shape, 1) // states
            here = lax.broadcasted_iota(jnp.int32, read.shape, 0) % run
            read_ref[pl.ds(base, height), :] = jnp.where(owner == here, read, 0.0).astype(jnp.bfloat16)
            for k in range(0, inner, LANE_PAIR):
                z_ref[pl.ds(base, height), k : k + LANE_PAIR] = jnp.dot(
                    normed, win_ref[:, inner + k : inner + k + LANE_PAIR],
                    preferred_element_type=jnp.float32,
                ).astype(jnp.bfloat16)

    for fetch in fetches[3:]:
        fetch.wait()

    for group, (first, chips) in enumerate(groups):
        @pl.when(inside[group])
        def _():
            def fill(d, _):
                for k in range(pairs):
                    rate = rrate_ref[:, k * LANE_PAIR : (k + 1) * LANE_PAIR]
                    table[k, d] = jnp.exp(-rate * d.astype(jnp.float32)).astype(jnp.bfloat16)
                return 0

            lax.fori_loop(0, (early[group] + chips) * columns, fill, 0)

    for i in range(run):
        spread_ref[i * states : (i + 1) * states] = wbc_ref[3 * states : 4 * states]
    crate_ref[...] = jnp.exp(-crate_ref[...])
    state_ref[...] = jnp.zeros(state_ref.shape, jnp.float32)
    @pl.when(c == 0)
    def _():
        send_own(1, 2)

    @pl.when(inside[0])
    def _():
        pl.semaphore_wait(ready_sem, 1)
        relay_own(0, 0)

    gate_part(c, lambda w: nown[c * per_core + w])

    @pl.when(c == 0)
    def _():
        send_own(2, local_chunks)

    @pl.when(inside[0])
    def _():
        relay_own(0, 1)

    @pl.when(inside[1])
    def _():
        pl.semaphore_wait(ready_sem, 2)
        relay_own(1, 0)

    for step in range(1, cols_n):
        column_copy(step).wait_recv()
        source = (c + cols_n - step) % cols_n
        gate_part(source, lambda w: ncol[source, w])

    @pl.when(c > 0)
    def _():
        send_own(0, local_chunks)

    @pl.when(inside[0])
    def _():
        def one(q, _):
            relay_own(0, q)
            return 0

        lax.fori_loop(2, local_chunks, one, 0)

    @pl.when(inside[1])
    def _():
        relay_early(1, 0)
        relay_own(1, 1)

    def result_copy(group, q, part, k):
        first, chips = groups[group]
        g = ((r - first) * cols_n + c + k) % (chips * cols_n)
        some = pl.ds(pl.multiple_of(part * share, share), share)
        src, dst = rsend.at[slot(group, q), g, :, :, some], rrecv.at[q, line, :, :, some]
        remote = pltpu.make_async_remote_copy(
            src_ref=src, dst_ref=dst, send_sem=rsend_sem.at[slot(group, q), part, k], recv_sem=rrecv_sem.at[q],
            device_id={"rows": first + g // cols_n, "cols": g % cols_n}, device_id_type=MESH,
        )
        return remote, lambda: pltpu.make_async_copy(src, dst, rrecv_sem.at[q])

    def row_chunk(group, q):
        chips = groups[group][1]
        before = early[group]
        at = slot(group, q)
        tin = tins[group]
        if group == 2:
            early_wait(group, q)
            own_wait(group, q)
        out_cols, pre_cols = chips * columns, before * columns
        all_cols = out_cols + pre_cols
        normed = tin[at].reshape(all_cols * rows, width)
        b_ref[: all_cols * rows] = transposed_dot(normed, wbc_ref[:states]).astype(jnp.bfloat16).astype(jnp.float32)
        c_ref[: out_cols * rows] = transposed_dot(
            normed[pre_cols * rows :], wbc_ref[states : 2 * states]
        ).astype(jnp.bfloat16).astype(jnp.float32)
        for k in range(pairs):
            u_ref[k, : all_cols * rows] = jnp.dot(
                normed, win_ref[:, k * LANE_PAIR : (k + 1) * LANE_PAIR], preferred_element_type=jnp.float32
            ).astype(jnp.bfloat16).astype(jnp.float32)

        def span(d):
            low = max(0, d - pre_cols)
            return low, out_cols - low, pre_cols + low - d

        for d in range(all_cols):
            low, count, source = span(d)
            lag_ref[d, : count * rows] = (
                c_ref[low * rows : out_cols * rows] * b_ref[source * rows : (source + count) * rows]
            ).astype(jnp.bfloat16)

        def one_pair(k):
            skip = skip_ref[k]
            sums = [
                skip * u_ref[k, (pre_cols + o) * rows : (pre_cols + o + 1) * rows] for o in range(out_cols)
            ]
            for d in range(all_cols):
                low, count, source = span(d)
                weight = jnp.dot(lag_ref[d, : count * rows], table[k, d], preferred_element_type=jnp.float32)
                for i in range(count):
                    sums[low + i] += weight[i * rows : (i + 1) * rows] * u_ref[
                        k, (source + i) * rows : (source + i + 1) * rows
                    ]
            some = pl.ds(pl.multiple_of(k * LANE_PAIR, LANE_PAIR), LANE_PAIR)
            for o in range(out_cols):
                rsend[at, o // per_core, o % per_core, :, some] = sums[o].astype(jnp.bfloat16)

        def one_part(part, _):
            for k in range(pairs // parts):
                one_pair(part * (pairs // parts) + k)
            result_copy(group, q, part, 0)[1]().start()

            def send_result(k, _):
                result_copy(group, q, part, k)[0].start()
                return 0

            lax.fori_loop(1, chips * cols_n, send_result, 0)
            return 0

        lax.fori_loop(0, parts, one_part, 0)

    def out_copy(q):
        return pltpu.make_async_remote_copy(
            src_ref=stage.at[q], dst_ref=land.at[c, q % local_chunks],
            send_sem=osend_sem.at[q], recv_sem=orecv_sem.at[c, q % local_chunks],
            device_id={"cols": q // local_chunks}, device_id_type=MESH,
        )

    def col_chunk(q):
        pltpu.make_async_copy(rrecv.at[q], rrecv.at[q], rrecv_sem.at[q]).wait()
        for p in range(lines):
            for w in range(per_core):
                value = rrecv[q, p, w].astype(jnp.float32)
                for t in range(tiles):
                    vcol[t, w * chunk_rows + p * rows : w * chunk_rows + (p + 1) * rows] = (
                        value[:, t * LANES : (t + 1) * LANES]
                    )
        halves = range(0, states, SUBLANES)

        def one_run(i):
            for w in range(per_core):
                here = w * chunk_rows + i * run
                patch = pl.multiple_of(w * total + q * chunk_rows + i * run, run)
                decay = [[crate_ref[h : h + SUBLANES, t * LANES : (t + 1) * LANES] for t in range(tiles)] for h in halves]
                state = [[state_ref[w, h : h + SUBLANES, t * LANES : (t + 1) * LANES] for t in range(tiles)] for h in halves]
                for s in range(run):
                    inject = [
                        inject_ref[pl.ds(pl.multiple_of((patch + s) * states + h, SUBLANES), SUBLANES), :] for h in halves
                    ]
                    for t in range(tiles):
                        value = vcol[t, pl.ds(here + s, SUBLANES, stride=0), :]
                        for j in range(len(inject)):
                            state[j][t] = decay[j][t] * state[j][t] + inject[j] * value
                        hist[i * per_core + w, t, s * states : (s + 1) * states, :] = jnp.concatenate(
                            [state[j][t] for j in range(len(inject))], axis=0
                        ).astype(jnp.bfloat16)
                for j, h in enumerate(halves):
                    for t in range(tiles):
                        state_ref[w, h : h + SUBLANES, t * LANES : (t + 1) * LANES] = state[j][t]
                for t in range(tiles):
                    if t % 2 == 0:
                        both_tiles = jnp.concatenate([hist[i * per_core + w, t], hist[i * per_core + w, t + 1]], axis=1)
                        mixed = jnp.dot(
                            read_ref[pl.ds(patch, run), :], both_tiles, preferred_element_type=jnp.float32
                        )
                    gate = z_ref[pl.ds(patch, run), t * LANES : (t + 1) * LANES].astype(jnp.float32)
                    both = mixed[:, t % 2 * LANES : (t % 2 + 1) * LANES] + vcol[t, pl.ds(here, run), :]
                    gated_ref[pl.ds(here, run), t * LANES : (t + 1) * LANES] = (
                        both * (gate / (1.0 + jnp.exp(-gate)))
                    ).astype(jnp.bfloat16)

        for i in range(chunk_rows // run):
            one_run(i)
        result = jnp.dot(gated_ref[...], wout_ref[...], preferred_element_type=jnp.float32).astype(jnp.bfloat16)
        home = q // local_chunks

        @pl.when(home == c)
        def _():
            land[c, q % local_chunks] = result

        @pl.when(home != c)
        def _():
            stage[q] = result
            out_copy(q).start()

    def one_chunk(q, _):
        for group in range(3):
            mine = inside[group] & (q < chunks)
            if group == 2:
                mine = mine & (q % 2 == (r - 2 * quarter) // quarter)

            @pl.when(mine)
            def _():
                row_chunk(group, q)

            if group == 0:
                @pl.when(inside[group] & (q + local_chunks < chunks))
                def _():
                    relay_own(group, q + local_chunks)
            if group == 1:
                @pl.when(inside[group] & (q + 1 < chunks))
                def _():
                    relay_early(group, q + 1)

                @pl.when(inside[group] & (q + 2 < chunks))
                def _():
                    relay_own(group, q + 2)

        @pl.when(q >= lag)
        def _():
            col_chunk(q - lag)
        return 0

    lag = 3
    lax.fori_loop(0, chunks + lag, one_chunk, 0)

    for group, (first, chips) in enumerate(groups):
        @pl.when(inside[group])
        def _():
            def drain_tokens(n, _):
                away, remote, _ = token_copy(group, n)

                @pl.when(away)
                def _():
                    remote.wait_send()
                return 0

            lax.fori_loop(0, local_chunks * lines, drain_tokens, 0)

            def drain_chunk(q, _):
                if group < 2:
                    relay_copy(group, q, 1).wait_send()
                if group == 1:
                    relay_copy(group, q, 0).wait_send()

                def one(k, _):
                    for part in range(parts):
                        result_copy(group, q, part, k)[0].wait_send()
                    return 0

                if group == 2:
                    @pl.when(q % 2 == (r - 2 * quarter) // quarter)
                    def _():
                        lax.fori_loop(1, chips * cols_n, one, 0)
                else:
                    lax.fori_loop(1, chips * cols_n, one, 0)
                return 0

            lax.fori_loop(0, chunks, drain_chunk, 0)

    for step in range(1, cols_n):
        column_copy(step).wait_send()

    def drain_out(q, _):
        @pl.when(q // local_chunks != c)
        def _():
            out_copy(q).wait_send()
        return 0

    lax.fori_loop(0, chunks, drain_out, 0)
    for source in range(cols_n):
        @pl.when(source != c)
        def _():
            for i in range(local_chunks):
                pltpu.make_async_copy(
                    land.at[source, i], land.at[source, i], orecv_sem.at[source, i]
                ).wait()
    for source in range(cols_n):
        for i in range(local_chunks):
            for w in range(per_core):
                out_ref[source * per_core + w, i * chunk_rows : (i + 1) * chunk_rows] = (
                    land[source, i, w * chunk_rows : (w + 1) * chunk_rows]
                )


def per_device_grouped(chunks, tokens, norm_gain, w_in, w_bc, rate_row, rate_col, skip_gain, w_out):
    inner, width_out = w_out.shape
    states = rate_row.shape[0]
    height, columns, width = tokens.shape
    rows_n, cols_n = lax.axis_size("rows"), lax.axis_size("cols")
    quarter = rows_n // 4
    per_core = columns // cols_n
    total = height * cols_n
    chunk_rows = total // chunks
    lines = quarter * cols_n
    rows = chunk_rows // lines
    tiles = inner // LANES
    pairs = inner // LANE_PAIR
    patches = total * per_core
    local_chunks = chunks // cols_n
    lags = rows_n * columns
    held = lags * rows
    outs = 2 * quarter * columns * rows
    f32, bf16 = jnp.float32, jnp.bfloat16
    dma = pltpu.SemaphoreType.DMA
    out = pl.pallas_call(
        functools.partial(grouped_kernel, states, rows_n, cols_n, chunks, per_core),
        in_specs=[pl.BlockSpec(memory_space=pl.ANY)] * 8,
        out_specs=pl.BlockSpec(memory_space=pltpu.VMEM),
        out_shape=pltpu.VMEM((columns, height, width_out), bf16),
        scratch_shapes=[
            pltpu.VMEM((1, width), f32),
            pltpu.VMEM(w_in.shape, bf16),
            pltpu.VMEM(w_bc.shape[::-1], bf16),
            pltpu.VMEM(rate_row.shape, f32),
            pltpu.VMEM(rate_col.shape, f32),
            pltpu.VMEM((pairs, 1, LANE_PAIR), f32),
            pltpu.VMEM(w_out.shape, bf16),
            pltpu.VMEM((height, columns, width), bf16),
            pltpu.VMEM((columns, height, width), bf16),
            pltpu.VMEM((cols_n, per_core, height, width), bf16),
            pltpu.VMEM((chunks, quarter, columns, rows, width), bf16),
            pltpu.VMEM((chunks, 2 * quarter, columns, rows, width), bf16),
            pltpu.VMEM((chunks // 2, 4 * quarter, columns, rows, width), bf16),
            pltpu.VMEM((pairs, lags, states, LANE_PAIR), bf16),
            pltpu.VMEM((width // LANES, height * columns, LANES), f32),
            pltpu.VMEM((pairs, held, LANE_PAIR), f32),
            pltpu.VMEM((held, states), f32),
            pltpu.VMEM((outs, states), f32),
            pltpu.VMEM((lags, outs, states), bf16),
            pltpu.VMEM((chunks, 2 * lines, per_core, rows, inner), bf16),
            pltpu.VMEM((chunks, lines, per_core, rows, inner), bf16),
            pltpu.VMEM((tiles, per_core * chunk_rows + SUBLANES, LANES), f32),
            pltpu.VMEM((patches * states, LANES), f32),
            pltpu.VMEM((LANE_PAIR, width), bf16),
            pltpu.VMEM((patches, LANE_PAIR), bf16),
            pltpu.VMEM((per_core * chunk_rows * states // LANE_PAIR, tiles, LANE_PAIR, LANES), bf16),
            pltpu.VMEM((patches, inner), bf16),
            pltpu.VMEM((per_core * chunk_rows, inner), bf16),
            pltpu.VMEM((chunks, per_core * chunk_rows, width_out), bf16),
            pltpu.VMEM((cols_n, local_chunks, per_core * chunk_rows, width_out), bf16),
            pltpu.VMEM((per_core, states, inner), f32),
            dma((local_chunks * lines,)), dma((chunks,)), dma((chunks,)), dma((chunks, 2)),
            dma((cols_n,)), dma((cols_n,)),
            dma((chunks, 2, 2 * lines)), dma((chunks,)), dma((chunks,)),
            dma((cols_n, local_chunks)), dma((9,)), pltpu.SemaphoreType.REGULAR,
        ],
        compiler_params=pltpu.CompilerParams(
            vmem_limit_bytes=VMEM_LIMIT, collective_id=0, has_side_effects=True
        ),
        name="layer",
    )(
        tokens, norm_gain[None], w_in, w_bc.T, rate_row, rate_col,
        skip_gain.reshape(pairs, 1, LANE_PAIR), w_out,
    )
    return out.transpose(1, 0, 2)


def chunk_count(tokens, rate_row, inner):
    height, columns, _ = tokens.shape
    states = rate_row.shape[0]
    rows_n, cols_n = lax.axis_size("rows"), lax.axis_size("cols")
    total = height * cols_n
    if rows_n % 4 or columns % cols_n or inner % LANE_PAIR or states % SUBLANES or LANE_PAIR % states:
        return 0
    step = rows_n // 4 * cols_n * SUBLANES
    run = LANE_PAIR // states
    if total % step or step % run or total // step % (2 * cols_n):
        return 0
    return total // step


def per_device(tokens, norm_gain, w_in, w_bc, rate_row, rate_col, skip_gain, w_out):
    args = (tokens, norm_gain, w_in, w_bc, rate_row, rate_col, skip_gain, w_out)
    chunks = chunk_count(tokens, rate_row, w_out.shape[0])
    if chunks:
        return per_device_grouped(chunks, *args)
    return per_device_uniform(*args)


def solution(mesh):
    placed = (P(("slides", "cols"), "rows", None), P(), P(), P(), P(), P(), P(), P())
    return jax.shard_map(
        per_device,
        mesh=mesh,
        in_specs=placed,
        out_specs=P(("slides", "cols"), "rows", None),
        check_vma=False,
    )
```

```python
import functools

import jax
import jax.numpy as jnp
from jax import lax
from jax.experimental import pallas as pl
from jax.experimental.pallas import tpu as pltpu
from jax.sharding import PartitionSpec as P

LANES = 128
VMEM_LIMIT = 60 * 1024 * 1024
MESH = pl.DeviceIdType.MESH


def normalise(tokens, gain):
    as_float = tokens.astype(jnp.float32)
    scale_now = lax.rsqrt(jnp.mean(as_float * as_float, axis=-1, keepdims=True) + 1e-05)
    return (as_float * scale_now * gain).astype(jnp.bfloat16)


def transposed_dot(a, b):
    return lax.dot_general(a, b, (((1,), (1,)), ((), ())), preferred_element_type=jnp.float32)


def spread_channels(ref, value, tiles):
    rows = value.shape[0]
    for t in range(tiles):
        ref[pl.ds(t, rows, stride=tiles), :] = value[:, t * LANES : (t + 1) * LANES]


def spread_vectors(ref, value, first, states, base):
    rows = value.shape[0]
    for n in range(states):
        ref[n, pl.ds(base, rows), :] = jnp.broadcast_to(
            value[:, first + n : first + n + 1], (rows, LANES)
        )


def scan_step(carried, decay, value, inject_ref, readout_ref, patch, start, tiles):
    new = []
    totals = [start, None]
    for n, state in enumerate(carried):
        inject = inject_ref[n, pl.ds(patch, tiles, stride=0), :]
        readout = readout_ref[n, pl.ds(patch, tiles, stride=0), :]
        state = decay[n] * state + inject * value
        term = readout * state
        totals[n % 2] = term if totals[n % 2] is None else totals[n % 2] + term
        new.append(state)
    return tuple(new), totals[0] + totals[1]


def layer_kernel(
    states, rows_n, cols_n, share, per_core,
    tok_ref, gain_in, win_in, wbc_in, rrate_in, crate_in, skip_in, wout_in,
    out_ref,
    gain_ref, win_ref, wbc_ref, rrate_ref, crate_ref, skip_ref, wout_ref, tcol, tin, rsend, rrecv, u_ref, rb_ref, rc_ref, cb_ref, cc_ref, z_ref, y_ref, gated_ref,
    rdecay, cdecay, skip_tile, stage, land, state_ref,
    tsend_sem, tin_sem, csend_sem, crecv_sem, rsend_sem, rrecv_sem, osend_sem, orecv_sem, fetch_sem,
):
    group_n = rows_n * cols_n
    pieces = tok_ref.shape[0] // share
    chunks = tin.shape[0]
    columns, width = tok_ref.shape[1:]
    inner = wout_ref.shape[0]
    tiles = inner // LANES
    piece_len = share * per_core
    chunk_len = group_n * piece_len
    blocks = stage.shape[0]
    blocks_home = blocks // cols_n
    block_len = stage.shape[1]
    r, c = lax.axis_index("rows"), lax.axis_index("cols")
    me = r * cols_n + c

    def spot(g):
        return {"rows": g // cols_n, "cols": g % cols_n}

    barrier = pltpu.get_barrier_semaphore()

    def greet(g, _):
        @pl.when(g != me)
        def _():
            pl.semaphore_signal(barrier, inc=1, device_id=spot(g), device_id_type=MESH)
        return 0

    lax.fori_loop(0, group_n, greet, 0)
    fetches = [
        pltpu.make_async_copy(src, dst, fetch_sem.at[k])
        for k, (src, dst) in enumerate((
            (rrate_in, rrate_ref), (crate_in, crate_ref), (skip_in, skip_ref), (gain_in, gain_ref),
            (wbc_in, wbc_ref), (tok_ref, tcol.at[c]), (win_in, win_ref), (wout_in, wout_ref),
        ))
    ]
    for fetch in fetches:
        fetch.start()
    pl.semaphore_wait(barrier, group_n - 1)

    local_chunks = max(1, chunks // cols_n)
    per_chunk = pieces // local_chunks

    def piece_of(k):
        piece = k // per_chunk * per_chunk + (k % per_chunk + me) % per_chunk
        place = c * pieces + piece
        return piece, place // group_n, place % group_n

    def token_copy(k):
        piece, q, g = piece_of(k)
        return g, pltpu.make_async_remote_copy(
            src_ref=tok_ref.at[pl.ds(piece * share, share)], dst_ref=tin.at[q, r],
            send_sem=tsend_sem.at[piece], recv_sem=tin_sem.at[q],
            device_id=spot(g), device_id_type=MESH,
        )

    def send_tokens(k, _):
        piece, q, g = piece_of(k)

        @pl.when(g == me)
        def _():
            pltpu.make_async_copy(tok_ref.at[pl.ds(piece * share, share)], tin.at[q, r], tin_sem.at[q]).start()

        @pl.when(g != me)
        def _():
            token_copy(k)[1].start()
        return 0

    lax.fori_loop(0, pieces, send_tokens, 0)

    def column_copy(step):
        other = (c + step) % cols_n
        return pltpu.make_async_remote_copy(
            src_ref=tok_ref, dst_ref=tcol.at[c],
            send_sem=csend_sem.at[step], recv_sem=crecv_sem.at[step],
            device_id={"cols": other}, device_id_type=MESH,
        )

    for step in range(1, cols_n):
        column_copy(step).start()

    def gate_part(tokens, core):
        tokens = tokens.astype(jnp.float32)
        own = tokens[:, :per_core]
        for k in range(1, cols_n):
            own = jnp.where(c == k, tokens[:, k * per_core : (k + 1) * per_core], own)
        normed = normalise(own.reshape(-1, width), gain_ref[...])
        count = normed.shape[0]
        base = pl.multiple_of(core * count, count)
        mixers = transposed_dot(normed, wbc_ref[...])
        mixers = mixers.astype(jnp.bfloat16).astype(jnp.float32)
        spread_vectors(cb_ref, mixers, 2 * states, states, base)
        spread_vectors(cc_ref, mixers, 3 * states, states, base)
        for k in range(0, inner, 2 * LANES):
            z_ref[pl.ds(base, count), k : k + 2 * LANES] = jnp.dot(
                normed, win_ref[:, inner + k : inner + k + 2 * LANES],
                preferred_element_type=jnp.float32,
            ).astype(jnp.bfloat16)

    for fetch in fetches:
        fetch.wait()
    spread_channels(rdecay, jnp.exp(-rrate_ref[...]), tiles)
    spread_channels(cdecay, jnp.exp(-crate_ref[...]), tiles)
    spread_channels(skip_tile, skip_ref[...], tiles)
    gate_part(tcol[c], c)

    zero = jnp.zeros((tiles, LANES), jnp.float32)
    lanes = 2 if share % 2 == 0 else 1

    def result_copy(q, k):
        g = (me + k) % group_n
        return pltpu.make_async_remote_copy(
            src_ref=rsend.at[q, pl.ds(g * piece_len, piece_len)],
            dst_ref=rrecv.at[q, pl.ds(me * piece_len, piece_len)],
            send_sem=rsend_sem.at[q, k], recv_sem=rrecv_sem.at[q],
            device_id=spot(g), device_id_type=MESH,
        )

    def row_chunk(q, _):
        pltpu.make_async_copy(tin.at[q], tin.at[q], tin_sem.at[q]).wait()
        normed = normalise(tin[q].astype(jnp.float32).reshape(chunk_len, width), gain_ref[...])
        mixers = transposed_dot(normed, wbc_ref[...])
        mixers = mixers.astype(jnp.bfloat16).astype(jnp.float32)
        spread_vectors(rb_ref, mixers, 0, states, 0)
        spread_vectors(rc_ref, mixers, states, states, 0)
        for k in range(0, tiles, 2):
            part = jnp.dot(normed, win_ref[:, k * LANES : (k + 2) * LANES],
                           preferred_element_type=jnp.float32)
            part = part.astype(jnp.bfloat16).astype(jnp.float32)
            for h in range(2):
                u_ref[pl.ds(k + h, chunk_len, stride=tiles), :] = part[:, h * LANES : (h + 1) * LANES]
        decay = [rdecay[n * tiles : (n + 1) * tiles, :] for n in range(states)]
        skip = skip_tile[...]

        def one_group(first, _):
            def one_step(j, carry):
                carry = list(carry)
                for w in range(columns):
                    for b in range(lanes):
                        row = first * lanes + b
                        patch = (j * share + row) * columns + w
                        owner = j * cols_n + w // per_core
                        value = u_ref[pl.ds(pl.multiple_of(patch * tiles, tiles), tiles), :]
                        carry[b], total = scan_step(carry[b], decay, value, rb_ref, rc_ref,
                                                    patch, skip * value, tiles)
                        rsend[q, (owner * share + row) * per_core + w % per_core] = total.astype(jnp.bfloat16)
                return tuple(carry)

            lax.fori_loop(0, rows_n, one_step, tuple((zero,) * states for _ in range(lanes)))
            return 0

        lax.fori_loop(0, share // lanes, one_group, 0)

        def send_result(k, _):
            result_copy(q, k).start()
            return 0

        pltpu.make_async_copy(
            rsend.at[q, pl.ds(me * piece_len, piece_len)],
            rrecv.at[q, pl.ds(me * piece_len, piece_len)], rrecv_sem.at[q],
        ).start()
        lax.fori_loop(1, group_n, send_result, 0)
        return 0

    lax.fori_loop(0, chunks, row_chunk, 0)

    for step in range(1, cols_n):
        column_copy(step).wait_recv()
        source = (c + cols_n - step) % cols_n
        gate_part(tcol[source], source)

    for g in range(per_core):
        for n in range(states):
            state_ref[g, n] = zero

    def out_copy(o):
        return pltpu.make_async_remote_copy(
            src_ref=stage.at[o], dst_ref=land.at[c, o % blocks_home],
            send_sem=osend_sem.at[o], recv_sem=orecv_sem.at[c, o % blocks_home],
            device_id={"cols": o // blocks_home}, device_id_type=MESH,
        )

    def col_chunk(q, _):
        pltpu.make_async_copy(rrecv.at[q], rrecv.at[q], rrecv_sem.at[q]).wait()
        decay = [cdecay[n * tiles : (n + 1) * tiles, :] for n in range(states)]
        base = q * chunk_len

        def one_step(s, carry):
            result = []
            for g in range(per_core):
                patch = s * per_core + g
                value = rrecv[q, patch].astype(jnp.float32)
                state, total = scan_step(carry[g], decay, value, cb_ref, cc_ref,
                                         base + patch, value, tiles)
                y_ref[pl.ds(pl.multiple_of(patch * tiles, tiles), tiles), :] = total
                result.append(state)
            return tuple(result)

        carry = tuple(tuple(state_ref[g, n] for n in range(states)) for g in range(per_core))
        carry = lax.fori_loop(0, chunk_len // per_core, one_step, carry)
        for g in range(per_core):
            for n in range(states):
                state_ref[g, n] = carry[g][n]
        start = pl.multiple_of(base, chunk_len)
        for t in range(tiles):
            gate = z_ref[pl.ds(start, chunk_len), t * LANES : (t + 1) * LANES].astype(jnp.float32)
            mixed = y_ref[pl.ds(t, chunk_len, stride=tiles), :]
            gated_ref[:, t * LANES : (t + 1) * LANES] = (
                mixed * (gate / (1.0 + jnp.exp(-gate)))
            ).astype(jnp.bfloat16)
        result = jnp.dot(gated_ref[...], wout_ref[...], preferred_element_type=jnp.float32)
        result = result.astype(jnp.bfloat16)
        for k in range(blocks // chunks):
            o = q * (blocks // chunks) + k
            block = result[k * block_len : (k + 1) * block_len]
            stage[o] = block

            @pl.when(o // blocks_home == c)
            def _():
                land[c, o % blocks_home] = block

            @pl.when(o // blocks_home != c)
            def _():
                out_copy(o).start()
        return 0

    lax.fori_loop(0, chunks, col_chunk, 0)

    def drain_tokens(k, _):
        g, copy = token_copy(k)

        @pl.when(g != me)
        def _():
            copy.wait_send()
        return 0

    lax.fori_loop(0, pieces, drain_tokens, 0)
    for step in range(1, cols_n):
        column_copy(step).wait_send()

    def drain_results(q, _):
        def one(k, _):
            result_copy(q, k).wait_send()
            return 0
        return lax.fori_loop(1, group_n, one, 0)

    lax.fori_loop(0, chunks, drain_results, 0)

    def drain_out(o, _):
        @pl.when(o // blocks_home != c)
        def _():
            out_copy(o).wait_send()
        return 0

    lax.fori_loop(0, blocks, drain_out, 0)
    for source in range(cols_n):
        @pl.when(source != c)
        def _():
            for i in range(blocks_home):
                pltpu.make_async_copy(
                    land.at[source, i], land.at[source, i], orecv_sem.at[source, i]
                ).wait()
    for i in range(blocks_home):
        parts = [
            land[s, i].astype(jnp.float32).reshape(block_len // per_core, per_core, -1)
            for s in range(cols_n)
        ]
        rows = block_len // per_core
        out_ref[i * rows : (i + 1) * rows] = jnp.concatenate(parts, axis=1).astype(jnp.bfloat16)


def per_device_uniform(tokens, norm_gain, w_in, w_bc, rate_row, rate_col, skip_gain, w_out):
    inner, width_out = w_out.shape
    states = rate_row.shape[0]
    height, columns, width = tokens.shape
    rows_n, cols_n = lax.axis_size("rows"), lax.axis_size("cols")
    group_n = rows_n * cols_n
    per_core = columns // cols_n
    total = height * cols_n
    share = min(4, total // group_n)
    chunks = total // (group_n * share)
    pieces = height // share
    piece_len = share * per_core
    chunk_len = group_n * piece_len
    tiles = inner // LANES
    blocks = max(chunks, cols_n)
    block_len = total * per_core // blocks
    patches = total * per_core
    f32, bf16 = jnp.float32, jnp.bfloat16
    dma = pltpu.SemaphoreType.DMA
    out = pl.pallas_call(
        functools.partial(layer_kernel, states, rows_n, cols_n, share, per_core),
        in_specs=[pl.BlockSpec(memory_space=pl.ANY)] * 8,
        out_specs=pl.BlockSpec(memory_space=pltpu.VMEM),
        out_shape=jax.ShapeDtypeStruct((height, columns, width_out), bf16),
        scratch_shapes=[
            pltpu.VMEM((1, width), f32),
            pltpu.VMEM(w_in.shape, bf16),
            pltpu.VMEM(w_bc.shape[::-1], bf16),
            pltpu.VMEM(rate_row.shape, f32),
            pltpu.VMEM(rate_col.shape, f32),
            pltpu.VMEM((1, inner), f32),
            pltpu.VMEM(w_out.shape, bf16),
            pltpu.VMEM((cols_n, height, columns, width), bf16),
            pltpu.VMEM((chunks, rows_n, share, columns, width), bf16),
            pltpu.VMEM((chunks, chunk_len, tiles, LANES), bf16),
            pltpu.VMEM((chunks, chunk_len, tiles, LANES), bf16),
            pltpu.VMEM((chunk_len * tiles, LANES), f32),
            pltpu.VMEM((states, chunk_len + 8, LANES), f32),
            pltpu.VMEM((states, chunk_len + 8, LANES), f32),
            pltpu.VMEM((states, patches + 8, LANES), f32),
            pltpu.VMEM((states, patches + 8, LANES), f32),
            pltpu.VMEM((patches, inner), bf16),
            pltpu.VMEM((chunk_len * tiles, LANES), f32),
            pltpu.VMEM((chunk_len, inner), bf16),
            pltpu.VMEM((states * tiles, LANES), f32),
            pltpu.VMEM((states * tiles, LANES), f32),
            pltpu.VMEM((tiles, LANES), f32),
            pltpu.VMEM((blocks, block_len, width_out), bf16),
            pltpu.VMEM((cols_n, blocks // cols_n, block_len, width_out), bf16),
            pltpu.VMEM((per_core, states, tiles, LANES), f32),
            dma((pieces,)), dma((chunks,)), dma((cols_n,)), dma((cols_n,)),
            dma((chunks, group_n)), dma((chunks,)), dma((blocks,)),
            dma((cols_n, blocks // cols_n)), dma((8,)),
        ],
        compiler_params=pltpu.CompilerParams(
            vmem_limit_bytes=VMEM_LIMIT, collective_id=0, has_side_effects=True
        ),
        name="layer",
    )(tokens, norm_gain[None], w_in, w_bc.T, rate_row, rate_col, skip_gain[None], w_out)
    return out


LANE_PAIR = 2 * LANES
SUBLANES = 8


def grouped_kernel(
    states, rows_n, cols_n, chunks, per_core,
    tok_ref, gain_in, win_in, wbc_in, rrate_in, crate_in, skip_in, wout_in,
    out_ref,
    gain_ref, win_ref, wbc_ref, rrate_ref, crate_ref, skip_ref, wout_ref,
    tokv, nown, ncol, tin_a, tin_b, tin_c, table, order_ref, u_ref, b_ref, c_ref, lag_ref,
    rsend, rrecv, vcol, inject_ref, spread_ref, read_ref, hist, z_ref, gated_ref, stage, state_ref,
    own_send_sem, own_sem, early_sem, relay_sem, csend_sem, crecv_sem, rsend_sem, rrecv_sem,
    osend_sem, orecv_sem, fetch_sem, ready_sem,
):
    height, columns, width = tok_ref.shape
    inner = wout_ref.shape[0]
    tiles = inner // LANES
    pairs = inner // LANE_PAIR
    quarter = rows_n // 4
    total = height * cols_n
    chunk_rows = total // chunks
    local_chunks = chunks // cols_n
    lines = quarter * cols_n
    rows = chunk_rows // lines
    run = LANE_PAIR // states
    parts = 2 if pairs % 2 == 0 else 1
    share = inner // parts
    r, c = lax.axis_index("rows"), lax.axis_index("cols")

    groups = ((0, quarter), (quarter, quarter), (2 * quarter, 2 * quarter))
    inside = (r < quarter, (r >= quarter) & (r < 2 * quarter), r >= 2 * quarter)
    tins = (tin_a, tin_b, tin_c)
    early = (0, quarter, 2 * quarter)
    line = r % quarter * cols_n + c

    def half_of(q):
        return (q + 1) % 2

    def chip_of(group, q, p):
        chip = groups[group][0] + p // cols_n
        return chip + half_of(q) * quarter if group == 2 else chip

    def slot(group, q):
        return q // 2 if group == 2 else q

    head, rest = pl.ds(0, chunk_rows), pl.ds(chunk_rows, height - chunk_rows)
    fetches = [
        pltpu.make_async_copy(src, dst, fetch_sem.at[k])
        for k, (src, dst) in enumerate((
            (tok_ref.at[head], tokv.at[head]), (gain_in, gain_ref), (tok_ref.at[rest], tokv.at[rest]),
            (rrate_in, rrate_ref), (wbc_in, wbc_ref), (win_in, win_ref),
            (crate_in, crate_ref), (skip_in, skip_ref), (wout_in, wout_ref),
        ))
    ]
    for fetch in fetches:
        fetch.start()

    barrier = pltpu.get_barrier_semaphore()

    def greet(chip, core):
        pl.semaphore_signal(barrier, inc=1, device_id={"rows": chip, "cols": core}, device_id_type=MESH)

    for group, (first, chips) in enumerate(groups):
        @pl.when(inside[group])
        def _():
            me = (r - first) * cols_n + c

            def one(k, _):
                @pl.when(k != me)
                def _():
                    greet(first + k // cols_n, k % cols_n)
                return 0

            lax.fori_loop(0, chips * cols_n, one, 0)
            if group < 2:
                for k in range(group + 1):
                    greet(r + (k + 1) * quarter, c)

    def normalise_part(part):
        first = part * chunk_rows
        flat = normalise(tokv[first : first + chunk_rows].astype(jnp.float32).reshape(-1, width), gain_ref[...])
        flat = flat.astype(jnp.float32)
        for t in range(width // LANES):
            order_ref[t, first * columns : (first + chunk_rows) * columns] = flat[:, t * LANES : (t + 1) * LANES]
        for w in range(columns):
            nown[w, first : first + chunk_rows] = jnp.concatenate([
                order_ref[t, pl.ds(first * columns + w, chunk_rows, stride=columns), :] for t in range(width // LANES)
            ], axis=1).astype(jnp.bfloat16)

    for fetch in fetches[:2]:
        fetch.wait()
    normalise_part(0)

    for group, (first, chips) in enumerate(groups):
        @pl.when(inside[group])
        def _():
            pl.semaphore_wait(barrier, chips * cols_n - 1 + (group > 0))
            if group:
                pl.semaphore_signal(
                    ready_sem, inc=1, device_id={"rows": first - quarter + (r - first) % quarter}, device_id_type=MESH
                )

    def token_copy(group, n):
        part, p = n // lines, (n + line) % lines
        q = c * local_chunks + part
        chip, core = chip_of(group, q, p), p % cols_n
        src = nown.at[:, pl.ds(pl.multiple_of(part * chunk_rows + p * rows, rows), rows)]
        dst = tins[group].at[slot(group, q), early[group] + r - groups[group][0]]
        remote = pltpu.make_async_remote_copy(
            src_ref=src, dst_ref=dst, send_sem=own_send_sem.at[0], recv_sem=own_sem.at[q],
            device_id={"rows": chip, "cols": core}, device_id_type=MESH,
        )
        away = (chip != r) | (core != c)
        return away, remote, lambda: pltpu.make_async_copy(src, dst, own_sem.at[q])

    def send_own(low, high):
        for group in range(3):
            @pl.when(inside[group])
            def _():
                def one(n, _):
                    away, remote, local = token_copy(group, n)

                    @pl.when(away)
                    def _():
                        remote.start()

                    @pl.when(jnp.logical_not(away))
                    def _():
                        local().start()
                    return 0

                lax.fori_loop(low * lines, high * lines, one, 0)

    @pl.when(c == 0)
    def _():
        send_own(0, 1)

    fetches[2].wait()
    for part in range(1, local_chunks):
        normalise_part(part)

    def column_copy(step):
        other = (c + step) % cols_n
        return pltpu.make_async_remote_copy(
            src_ref=nown.at[pl.ds(other * per_core, per_core)], dst_ref=ncol.at[c],
            send_sem=csend_sem.at[step], recv_sem=crecv_sem.at[step],
            device_id={"cols": other}, device_id_type=MESH,
        )

    for step in range(1, cols_n):
        column_copy(step).start()

    def drain_own(group):
        count = local_chunks * (lines - 1) if group < 2 else local_chunks * lines - local_chunks // 2
        sent = nown.at[:, pl.ds(0, count * rows)]
        pltpu.make_async_copy(sent, sent, own_send_sem.at[0]).wait()

    def own_wait(group, q):
        part = tins[group].at[slot(group, q), pl.ds(early[group], groups[group][1])]
        pltpu.make_async_copy(part, part, own_sem.at[q]).wait()

    def early_wait(group, q):
        part = tins[group].at[slot(group, q), pl.ds(0, early[group])]
        pltpu.make_async_copy(part, part, early_sem.at[q]).wait()

    def relay_copy(group, q, which):
        if group == 0:
            src, dst, chip = tin_a.at[q], tin_b.at[q, pl.ds(0, quarter)], r + quarter
        else:
            src = tin_b.at[q, pl.ds(which * quarter, quarter)]
            dst = tin_c.at[q // 2, pl.ds(which * quarter, quarter)]
            chip = r + quarter + half_of(q) * quarter
        return pltpu.make_async_remote_copy(
            src_ref=src, dst_ref=dst, send_sem=relay_sem.at[q, which], recv_sem=early_sem.at[q],
            device_id={"rows": chip}, device_id_type=MESH,
        )

    def relay_own(group, q):
        own_wait(group, q)
        relay_copy(group, q, 1).start()

    def relay_early(group, q):
        early_wait(group, q)
        relay_copy(group, q, 0).start()

    def gate_part(core, normed_of):
        for w in range(per_core):
            normed = normed_of(w)
            base = pl.multiple_of(w * total + core * height, height)
            inject = transposed_dot(normed, wbc_ref[2 * states : 3 * states])
            inject = inject.astype(jnp.bfloat16).astype(jnp.float32)
            for n in range(states):
                inject_ref[pl.ds(base * states + n, height, stride=states), :] = jnp.broadcast_to(
                    inject[:, n : n + 1], (height, LANES)
                )
            read = transposed_dot(normed, spread_ref[...])
            owner = lax.broadcasted_iota(jnp.int32, read.shape, 1) // states
            here = lax.broadcasted_iota(jnp.int32, read.shape, 0) % run
            read_ref[pl.ds(base, height), :] = jnp.where(owner == here, read, 0.0).astype(jnp.bfloat16)
            for k in range(0, inner, LANE_PAIR):
                z_ref[pl.ds(base, height), k : k + LANE_PAIR] = jnp.dot(
                    normed, win_ref[:, inner + k : inner + k + LANE_PAIR],
                    preferred_element_type=jnp.float32,
                ).astype(jnp.bfloat16)

    for fetch in fetches[3:]:
        fetch.wait()

    for group, (first, chips) in enumerate(groups):
        @pl.when(inside[group])
        def _():
            def fill(d, _):
                for k in range(pairs):
                    rate = rrate_ref[:, k * LANE_PAIR : (k + 1) * LANE_PAIR]
                    table[k, d] = jnp.exp(-rate * d.astype(jnp.float32)).astype(jnp.bfloat16)
                return 0

            lax.fori_loop(0, (early[group] + chips) * columns, fill, 0)

    for i in range(run):
        spread_ref[i * states : (i + 1) * states] = wbc_ref[3 * states : 4 * states]
    crate_ref[...] = jnp.exp(-crate_ref[...])
    state_ref[...] = jnp.zeros(state_ref.shape, jnp.float32)
    gated_ref[...] = jnp.zeros(gated_ref.shape, jnp.bfloat16)
    @pl.when(c == 0)
    def _():
        send_own(1, 2)

    @pl.when(inside[0])
    def _():
        pl.semaphore_wait(ready_sem, 1)
        relay_own(0, 0)

    gate_part(c, lambda w: nown[c * per_core + w])

    @pl.when(c == 0)
    def _():
        send_own(2, local_chunks)

    @pl.when(inside[0])
    def _():
        relay_own(0, 1)

    @pl.when(inside[1])
    def _():
        pl.semaphore_wait(ready_sem, 2)
        relay_own(1, 0)

    for step in range(1, cols_n):
        column_copy(step).wait_recv()
        source = (c + cols_n - step) % cols_n
        gate_part(source, lambda w: ncol[source, w])

    @pl.when(c > 0)
    def _():
        send_own(0, local_chunks)

    @pl.when(inside[0])
    def _():
        def one(q, _):
            relay_own(0, q)
            return 0

        lax.fori_loop(2, local_chunks, one, 0)

    @pl.when(inside[1])
    def _():
        relay_own(1, 1)
        relay_early(1, 0)

    def result_copy(group, q, part, k):
        first, chips = groups[group]
        g = ((r - first) * cols_n + c + k) % (chips * cols_n)
        some = pl.ds(pl.multiple_of(part * share, share), share)
        src, dst = rsend.at[slot(group, q), g, :, :, some], rrecv.at[q, line, :, :, some]
        remote = pltpu.make_async_remote_copy(
            src_ref=src, dst_ref=dst, send_sem=rsend_sem.at[slot(group, q)], recv_sem=rrecv_sem.at[q],
            device_id={"rows": first + g // cols_n, "cols": g % cols_n}, device_id_type=MESH,
        )
        return remote, lambda: pltpu.make_async_copy(src, dst, rrecv_sem.at[q])

    def row_chunk(group, q):
        chips = groups[group][1]
        before = early[group]
        at = slot(group, q)
        tin = tins[group]
        if group == 2:
            early_wait(group, q)
            own_wait(group, q)
        out_cols, pre_cols = chips * columns, before * columns
        all_cols = out_cols + pre_cols
        normed = tin[at].reshape(all_cols * rows, width)
        b_ref[: all_cols * rows] = transposed_dot(normed, wbc_ref[:states]).astype(jnp.bfloat16).astype(jnp.float32)
        c_ref[: out_cols * rows] = transposed_dot(
            normed[pre_cols * rows :], wbc_ref[states : 2 * states]
        ).astype(jnp.bfloat16).astype(jnp.float32)
        for k in range(pairs):
            u_ref[k, : all_cols * rows] = jnp.dot(
                normed, win_ref[:, k * LANE_PAIR : (k + 1) * LANE_PAIR], preferred_element_type=jnp.float32
            ).astype(jnp.bfloat16).astype(jnp.float32)

        def span(d):
            low = max(0, d - pre_cols)
            return low, out_cols - low, pre_cols + low - d

        for d in range(all_cols):
            low, count, source = span(d)
            lag_ref[d, : count * rows] = (
                c_ref[low * rows : out_cols * rows] * b_ref[source * rows : (source + count) * rows]
            ).astype(jnp.bfloat16)

        def one_pair(k):
            skip = skip_ref[k]
            sums = [
                skip * u_ref[k, (pre_cols + o) * rows : (pre_cols + o + 1) * rows] for o in range(out_cols)
            ]
            for d in range(all_cols):
                low, count, source = span(d)
                weight = jnp.dot(lag_ref[d, : count * rows], table[k, d], preferred_element_type=jnp.float32)
                for i in range(count):
                    sums[low + i] += weight[i * rows : (i + 1) * rows] * u_ref[
                        k, (source + i) * rows : (source + i + 1) * rows
                    ]
            some = pl.ds(pl.multiple_of(k * LANE_PAIR, LANE_PAIR), LANE_PAIR)
            for o in range(out_cols):
                rsend[at, o // per_core, o % per_core, :, some] = sums[o].astype(jnp.bfloat16)

        def one_part(part, _):
            for k in range(pairs // parts):
                one_pair(part * (pairs // parts) + k)
            result_copy(group, q, part, 0)[1]().start()

            def send_result(k, _):
                result_copy(group, q, part, k)[0].start()
                return 0

            lax.fori_loop(1, chips * cols_n, send_result, 0)
            return 0

        lax.fori_loop(0, parts, one_part, 0)

    def out_part(core, i):
        first = pl.multiple_of(i * chunk_rows, chunk_rows)
        return out_ref.at[pl.ds(core * per_core, per_core), pl.ds(first, chunk_rows)]

    def out_copy(q):
        return pltpu.make_async_remote_copy(
            src_ref=stage.at[q], dst_ref=out_part(c, q % local_chunks),
            send_sem=osend_sem.at[q], recv_sem=orecv_sem.at[c, q % local_chunks],
            device_id={"cols": q // local_chunks}, device_id_type=MESH,
        )

    def col_chunk(q):
        pltpu.make_async_copy(rrecv.at[q], rrecv.at[q], rrecv_sem.at[q]).wait()
        for p in range(lines):
            for w in range(per_core):
                value = rrecv[q, p, w].astype(jnp.float32)
                for t in range(tiles):
                    vcol[t, w * chunk_rows + p * rows : w * chunk_rows + (p + 1) * rows] = (
                        value[:, t * LANES : (t + 1) * LANES]
                    )
        project((q + chunks - 1) % chunks)
        halves = range(0, states, SUBLANES)

        def one_run(i):
            for w in range(per_core):
                here = w * chunk_rows + i * run
                patch = pl.multiple_of(w * total + q * chunk_rows + i * run, run)
                decay = [[crate_ref[h : h + SUBLANES, t * LANES : (t + 1) * LANES] for t in range(tiles)] for h in halves]
                state = [[state_ref[w, h : h + SUBLANES, t * LANES : (t + 1) * LANES] for t in range(tiles)] for h in halves]
                for s in range(run):
                    inject = [
                        inject_ref[pl.ds(pl.multiple_of((patch + s) * states + h, SUBLANES), SUBLANES), :] for h in halves
                    ]
                    for t in range(tiles):
                        value = vcol[t, pl.ds(here + s, SUBLANES, stride=0), :]
                        for j in range(len(inject)):
                            state[j][t] = decay[j][t] * state[j][t] + inject[j] * value
                        hist[i * per_core + w, t, s * states : (s + 1) * states, :] = jnp.concatenate(
                            [state[j][t] for j in range(len(inject))], axis=0
                        ).astype(jnp.bfloat16)
                for j, h in enumerate(halves):
                    for t in range(tiles):
                        state_ref[w, h : h + SUBLANES, t * LANES : (t + 1) * LANES] = state[j][t]
                for t in range(tiles):
                    if t % 2 == 0:
                        both_tiles = jnp.concatenate([hist[i * per_core + w, t], hist[i * per_core + w, t + 1]], axis=1)
                        mixed = jnp.dot(
                            read_ref[pl.ds(patch, run), :], both_tiles, preferred_element_type=jnp.float32
                        )
                    gate = z_ref[pl.ds(patch, run), t * LANES : (t + 1) * LANES].astype(jnp.float32)
                    both = mixed[:, t % 2 * LANES : (t % 2 + 1) * LANES] + vcol[t, pl.ds(here, run), :]
                    gated_ref[q % 2, pl.ds(here, run), t * LANES : (t + 1) * LANES] = (
                        both * (gate / (1.0 + jnp.exp(-gate)))
                    ).astype(jnp.bfloat16)

        for i in range(chunk_rows // run):
            one_run(i)

        @pl.when(q > 0)
        def _():
            send_out(q - 1)

    def project(q):
        result = jnp.dot(gated_ref[q % 2], wout_ref[...], preferred_element_type=jnp.float32).astype(jnp.bfloat16)
        stage[q] = result.reshape(per_core, chunk_rows, -1)

    def send_out(q):
        home = q // local_chunks

        @pl.when(home == c)
        def _():
            pltpu.make_async_copy(stage.at[q], out_part(c, q % local_chunks), orecv_sem.at[c, q % local_chunks]).start()

        @pl.when(home != c)
        def _():
            out_copy(q).start()

    def one_chunk(q, _):
        for group in range(3):
            mine = inside[group] & (q < chunks)
            if group == 2:
                mine = mine & (half_of(q) == (r - 2 * quarter) // quarter)

            @pl.when(mine)
            def _():
                row_chunk(group, q)

            if group == 0:
                @pl.when(inside[group] & (q + local_chunks < chunks))
                def _():
                    relay_own(group, q + local_chunks)
            if group == 1:
                @pl.when(inside[group] & (q + 1 < chunks))
                def _():
                    relay_early(group, q + 1)

                @pl.when(inside[group] & (q + 2 < chunks))
                def _():
                    relay_own(group, q + 2)

        @pl.when(q >= lag)
        def _():
            col_chunk(q - lag)
        return 0

    @pl.when(inside[2])
    def _():
        drain_own(2)

    lag = 3
    lax.fori_loop(0, chunks + lag, one_chunk, 0)
    project(chunks - 1)
    send_out(chunks - 1)

    for group, (first, chips) in enumerate(groups):
        @pl.when(inside[group])
        def _():
            if group < 2:
                drain_own(group)

            def drain_chunk(q, _):
                if group < 2:
                    relay_copy(group, q, 1).wait_send()
                if group == 1:
                    relay_copy(group, q, 0).wait_send()
                return 0

            if group < 2:
                lax.fori_loop(0, chunks, drain_chunk, 0)
            for at in range(chunks // (1 + group // 2)):
                sent = rsend.at[at, pl.ds(0, chips * cols_n - 1)]
                pltpu.make_async_copy(sent, sent, rsend_sem.at[at]).wait()

    for step in range(1, cols_n):
        column_copy(step).wait_send()

    def drain_out(q, _):
        @pl.when(q // local_chunks != c)
        def _():
            out_copy(q).wait_send()
        return 0

    lax.fori_loop(0, chunks, drain_out, 0)
    for source in range(cols_n):
        for i in range(local_chunks):
            part = out_part(source, i)
            pltpu.make_async_copy(part, part, orecv_sem.at[source, i]).wait()


def per_device_grouped(chunks, tokens, norm_gain, w_in, w_bc, rate_row, rate_col, skip_gain, w_out):
    inner, width_out = w_out.shape
    states = rate_row.shape[0]
    height, columns, width = tokens.shape
    rows_n, cols_n = lax.axis_size("rows"), lax.axis_size("cols")
    quarter = rows_n // 4
    per_core = columns // cols_n
    total = height * cols_n
    chunk_rows = total // chunks
    lines = quarter * cols_n
    rows = chunk_rows // lines
    tiles = inner // LANES
    pairs = inner // LANE_PAIR
    patches = total * per_core
    local_chunks = chunks // cols_n
    lags = rows_n * columns
    held = lags * rows
    outs = 2 * quarter * columns * rows
    f32, bf16 = jnp.float32, jnp.bfloat16
    dma = pltpu.SemaphoreType.DMA
    out = pl.pallas_call(
        functools.partial(grouped_kernel, states, rows_n, cols_n, chunks, per_core),
        in_specs=[pl.BlockSpec(memory_space=pl.ANY)] * 8,
        out_specs=pl.BlockSpec(memory_space=pl.ANY),
        out_shape=pltpu.VMEM((columns, height, width_out), bf16),
        scratch_shapes=[
            pltpu.VMEM((1, width), f32),
            pltpu.VMEM(w_in.shape, bf16),
            pltpu.VMEM(w_bc.shape[::-1], bf16),
            pltpu.VMEM(rate_row.shape, f32),
            pltpu.VMEM(rate_col.shape, f32),
            pltpu.VMEM((pairs, 1, LANE_PAIR), f32),
            pltpu.VMEM(w_out.shape, bf16),
            pltpu.VMEM((height, columns, width), bf16),
            pltpu.VMEM((columns, height, width), bf16),
            pltpu.VMEM((cols_n, per_core, height, width), bf16),
            pltpu.VMEM((chunks, quarter, columns, rows, width), bf16),
            pltpu.VMEM((chunks, 2 * quarter, columns, rows, width), bf16),
            pltpu.VMEM((chunks // 2, 4 * quarter, columns, rows, width), bf16),
            pltpu.VMEM((pairs, lags, states, LANE_PAIR), bf16),
            pltpu.VMEM((width // LANES, height * columns, LANES), f32),
            pltpu.VMEM((pairs, held, LANE_PAIR), f32),
            pltpu.VMEM((held, states), f32),
            pltpu.VMEM((outs, states), f32),
            pltpu.VMEM((lags, outs, states), bf16),
            pltpu.VMEM((chunks, 2 * lines, per_core, rows, inner), bf16),
            pltpu.VMEM((chunks, lines, per_core, rows, inner), bf16),
            pltpu.VMEM((tiles, per_core * chunk_rows + SUBLANES, LANES), f32),
            pltpu.VMEM((patches * states, LANES), f32),
            pltpu.VMEM((LANE_PAIR, width), bf16),
            pltpu.VMEM((patches, LANE_PAIR), bf16),
            pltpu.VMEM((per_core * chunk_rows * states // LANE_PAIR, tiles, LANE_PAIR, LANES), bf16),
            pltpu.VMEM((patches, inner), bf16),
            pltpu.VMEM((2, per_core * chunk_rows, inner), bf16),
            pltpu.VMEM((chunks, per_core, chunk_rows, width_out), bf16),
            pltpu.VMEM((per_core, states, inner), f32),
            dma((1,)), dma((chunks,)), dma((chunks,)), dma((chunks, 2)),
            dma((cols_n,)), dma((cols_n,)),
            dma((chunks,)), dma((chunks,)), dma((chunks,)),
            dma((cols_n, local_chunks)), dma((9,)), pltpu.SemaphoreType.REGULAR,
        ],
        compiler_params=pltpu.CompilerParams(
            vmem_limit_bytes=VMEM_LIMIT, collective_id=0, has_side_effects=True
        ),
        name="layer",
    )(
        tokens, norm_gain[None], w_in, w_bc.T, rate_row, rate_col,
        skip_gain.reshape(pairs, 1, LANE_PAIR), w_out,
    )
    return out.transpose(1, 0, 2)


def chunk_count(tokens, rate_row, inner):
    height, columns, _ = tokens.shape
    states = rate_row.shape[0]
    rows_n, cols_n = lax.axis_size("rows"), lax.axis_size("cols")
    total = height * cols_n
    if rows_n % 4 or columns % cols_n or inner % LANE_PAIR or states % SUBLANES or LANE_PAIR % states:
        return 0
    step = rows_n // 4 * cols_n * SUBLANES
    run = LANE_PAIR // states
    if total % step or step % run or total // step % (2 * cols_n):
        return 0
    return total // step


def per_device(tokens, norm_gain, w_in, w_bc, rate_row, rate_col, skip_gain, w_out):
    args = (tokens, norm_gain, w_in, w_bc, rate_row, rate_col, skip_gain, w_out)
    chunks = chunk_count(tokens, rate_row, w_out.shape[0])
    if chunks:
        return per_device_grouped(chunks, *args)
    return per_device_uniform(*args)


def solution(mesh):
    placed = (P(("slides", "cols"), "rows", None), P(), P(), P(), P(), P(), P(), P())
    return jax.shard_map(
        per_device,
        mesh=mesh,
        in_specs=placed,
        out_specs=P(("slides", "cols"), "rows", None),
        check_vma=False,
    )
```

```python
import functools

import jax
import jax.numpy as jnp
from jax import lax
from jax.experimental import pallas as pl
from jax.experimental.pallas import tpu as pltpu
from jax.sharding import PartitionSpec as P

LANES = 128
VMEM_LIMIT = 60 * 1024 * 1024
MESH = pl.DeviceIdType.MESH


def normalise(tokens, gain):
    as_float = tokens.astype(jnp.float32)
    scale_now = lax.rsqrt(jnp.mean(as_float * as_float, axis=-1, keepdims=True) + 1e-05)
    return (as_float * scale_now * gain).astype(jnp.bfloat16)


def transposed_dot(a, b):
    return lax.dot_general(a, b, (((1,), (1,)), ((), ())), preferred_element_type=jnp.float32)


def spread_channels(ref, value, tiles):
    rows = value.shape[0]
    for t in range(tiles):
        ref[pl.ds(t, rows, stride=tiles), :] = value[:, t * LANES : (t + 1) * LANES]


def spread_vectors(ref, value, first, states, base):
    rows = value.shape[0]
    for n in range(states):
        ref[n, pl.ds(base, rows), :] = jnp.broadcast_to(
            value[:, first + n : first + n + 1], (rows, LANES)
        )


def scan_step(carried, decay, value, inject_ref, readout_ref, patch, start, tiles):
    new = []
    totals = [start, None]
    for n, state in enumerate(carried):
        inject = inject_ref[n, pl.ds(patch, tiles, stride=0), :]
        readout = readout_ref[n, pl.ds(patch, tiles, stride=0), :]
        state = decay[n] * state + inject * value
        term = readout * state
        totals[n % 2] = term if totals[n % 2] is None else totals[n % 2] + term
        new.append(state)
    return tuple(new), totals[0] + totals[1]


def layer_kernel(
    states, rows_n, cols_n, share, per_core,
    tok_ref, gain_in, win_in, wbc_in, rrate_in, crate_in, skip_in, wout_in,
    out_ref,
    gain_ref, win_ref, wbc_ref, rrate_ref, crate_ref, skip_ref, wout_ref, tcol, tin, rsend, rrecv, u_ref, rb_ref, rc_ref, cb_ref, cc_ref, z_ref, y_ref, gated_ref,
    rdecay, cdecay, skip_tile, stage, land, state_ref,
    tsend_sem, tin_sem, csend_sem, crecv_sem, rsend_sem, rrecv_sem, osend_sem, orecv_sem, fetch_sem,
):
    group_n = rows_n * cols_n
    pieces = tok_ref.shape[0] // share
    chunks = tin.shape[0]
    columns, width = tok_ref.shape[1:]
    inner = wout_ref.shape[0]
    tiles = inner // LANES
    piece_len = share * per_core
    chunk_len = group_n * piece_len
    blocks = stage.shape[0]
    blocks_home = blocks // cols_n
    block_len = stage.shape[1]
    r, c = lax.axis_index("rows"), lax.axis_index("cols")
    me = r * cols_n + c

    def spot(g):
        return {"rows": g // cols_n, "cols": g % cols_n}

    barrier = pltpu.get_barrier_semaphore()

    def greet(g, _):
        @pl.when(g != me)
        def _():
            pl.semaphore_signal(barrier, inc=1, device_id=spot(g), device_id_type=MESH)
        return 0

    lax.fori_loop(0, group_n, greet, 0)
    fetches = [
        pltpu.make_async_copy(src, dst, fetch_sem.at[k])
        for k, (src, dst) in enumerate((
            (rrate_in, rrate_ref), (crate_in, crate_ref), (skip_in, skip_ref), (gain_in, gain_ref),
            (wbc_in, wbc_ref), (tok_ref, tcol.at[c]), (win_in, win_ref), (wout_in, wout_ref),
        ))
    ]
    for fetch in fetches:
        fetch.start()
    pl.semaphore_wait(barrier, group_n - 1)

    local_chunks = max(1, chunks // cols_n)
    per_chunk = pieces // local_chunks

    def piece_of(k):
        piece = k // per_chunk * per_chunk + (k % per_chunk + me) % per_chunk
        place = c * pieces + piece
        return piece, place // group_n, place % group_n

    def token_copy(k):
        piece, q, g = piece_of(k)
        return g, pltpu.make_async_remote_copy(
            src_ref=tok_ref.at[pl.ds(piece * share, share)], dst_ref=tin.at[q, r],
            send_sem=tsend_sem.at[piece], recv_sem=tin_sem.at[q],
            device_id=spot(g), device_id_type=MESH,
        )

    def send_tokens(k, _):
        piece, q, g = piece_of(k)

        @pl.when(g == me)
        def _():
            pltpu.make_async_copy(tok_ref.at[pl.ds(piece * share, share)], tin.at[q, r], tin_sem.at[q]).start()

        @pl.when(g != me)
        def _():
            token_copy(k)[1].start()
        return 0

    lax.fori_loop(0, pieces, send_tokens, 0)

    def column_copy(step):
        other = (c + step) % cols_n
        return pltpu.make_async_remote_copy(
            src_ref=tok_ref, dst_ref=tcol.at[c],
            send_sem=csend_sem.at[step], recv_sem=crecv_sem.at[step],
            device_id={"cols": other}, device_id_type=MESH,
        )

    for step in range(1, cols_n):
        column_copy(step).start()

    def gate_part(tokens, core):
        tokens = tokens.astype(jnp.float32)
        own = tokens[:, :per_core]
        for k in range(1, cols_n):
            own = jnp.where(c == k, tokens[:, k * per_core : (k + 1) * per_core], own)
        normed = normalise(own.reshape(-1, width), gain_ref[...])
        count = normed.shape[0]
        base = pl.multiple_of(core * count, count)
        mixers = transposed_dot(normed, wbc_ref[...])
        mixers = mixers.astype(jnp.bfloat16).astype(jnp.float32)
        spread_vectors(cb_ref, mixers, 2 * states, states, base)
        spread_vectors(cc_ref, mixers, 3 * states, states, base)
        for k in range(0, inner, 2 * LANES):
            z_ref[pl.ds(base, count), k : k + 2 * LANES] = jnp.dot(
                normed, win_ref[:, inner + k : inner + k + 2 * LANES],
                preferred_element_type=jnp.float32,
            ).astype(jnp.bfloat16)

    for fetch in fetches:
        fetch.wait()
    spread_channels(rdecay, jnp.exp(-rrate_ref[...]), tiles)
    spread_channels(cdecay, jnp.exp(-crate_ref[...]), tiles)
    spread_channels(skip_tile, skip_ref[...], tiles)
    gate_part(tcol[c], c)

    zero = jnp.zeros((tiles, LANES), jnp.float32)
    lanes = 2 if share % 2 == 0 else 1

    def result_copy(q, k):
        g = (me + k) % group_n
        return pltpu.make_async_remote_copy(
            src_ref=rsend.at[q, pl.ds(g * piece_len, piece_len)],
            dst_ref=rrecv.at[q, pl.ds(me * piece_len, piece_len)],
            send_sem=rsend_sem.at[q, k], recv_sem=rrecv_sem.at[q],
            device_id=spot(g), device_id_type=MESH,
        )

    def row_chunk(q, _):
        pltpu.make_async_copy(tin.at[q], tin.at[q], tin_sem.at[q]).wait()
        normed = normalise(tin[q].astype(jnp.float32).reshape(chunk_len, width), gain_ref[...])
        mixers = transposed_dot(normed, wbc_ref[...])
        mixers = mixers.astype(jnp.bfloat16).astype(jnp.float32)
        spread_vectors(rb_ref, mixers, 0, states, 0)
        spread_vectors(rc_ref, mixers, states, states, 0)
        for k in range(0, tiles, 2):
            part = jnp.dot(normed, win_ref[:, k * LANES : (k + 2) * LANES],
                           preferred_element_type=jnp.float32)
            part = part.astype(jnp.bfloat16).astype(jnp.float32)
            for h in range(2):
                u_ref[pl.ds(k + h, chunk_len, stride=tiles), :] = part[:, h * LANES : (h + 1) * LANES]
        decay = [rdecay[n * tiles : (n + 1) * tiles, :] for n in range(states)]
        skip = skip_tile[...]

        def one_group(first, _):
            def one_step(j, carry):
                carry = list(carry)
                for w in range(columns):
                    for b in range(lanes):
                        row = first * lanes + b
                        patch = (j * share + row) * columns + w
                        owner = j * cols_n + w // per_core
                        value = u_ref[pl.ds(pl.multiple_of(patch * tiles, tiles), tiles), :]
                        carry[b], total = scan_step(carry[b], decay, value, rb_ref, rc_ref,
                                                    patch, skip * value, tiles)
                        rsend[q, (owner * share + row) * per_core + w % per_core] = total.astype(jnp.bfloat16)
                return tuple(carry)

            lax.fori_loop(0, rows_n, one_step, tuple((zero,) * states for _ in range(lanes)))
            return 0

        lax.fori_loop(0, share // lanes, one_group, 0)

        def send_result(k, _):
            result_copy(q, k).start()
            return 0

        pltpu.make_async_copy(
            rsend.at[q, pl.ds(me * piece_len, piece_len)],
            rrecv.at[q, pl.ds(me * piece_len, piece_len)], rrecv_sem.at[q],
        ).start()
        lax.fori_loop(1, group_n, send_result, 0)
        return 0

    lax.fori_loop(0, chunks, row_chunk, 0)

    for step in range(1, cols_n):
        column_copy(step).wait_recv()
        source = (c + cols_n - step) % cols_n
        gate_part(tcol[source], source)

    for g in range(per_core):
        for n in range(states):
            state_ref[g, n] = zero

    def out_copy(o):
        return pltpu.make_async_remote_copy(
            src_ref=stage.at[o], dst_ref=land.at[c, o % blocks_home],
            send_sem=osend_sem.at[o], recv_sem=orecv_sem.at[c, o % blocks_home],
            device_id={"cols": o // blocks_home}, device_id_type=MESH,
        )

    def col_chunk(q, _):
        pltpu.make_async_copy(rrecv.at[q], rrecv.at[q], rrecv_sem.at[q]).wait()
        decay = [cdecay[n * tiles : (n + 1) * tiles, :] for n in range(states)]
        base = q * chunk_len

        def one_step(s, carry):
            result = []
            for g in range(per_core):
                patch = s * per_core + g
                value = rrecv[q, patch].astype(jnp.float32)
                state, total = scan_step(carry[g], decay, value, cb_ref, cc_ref,
                                         base + patch, value, tiles)
                y_ref[pl.ds(pl.multiple_of(patch * tiles, tiles), tiles), :] = total
                result.append(state)
            return tuple(result)

        carry = tuple(tuple(state_ref[g, n] for n in range(states)) for g in range(per_core))
        carry = lax.fori_loop(0, chunk_len // per_core, one_step, carry)
        for g in range(per_core):
            for n in range(states):
                state_ref[g, n] = carry[g][n]
        start = pl.multiple_of(base, chunk_len)
        for t in range(tiles):
            gate = z_ref[pl.ds(start, chunk_len), t * LANES : (t + 1) * LANES].astype(jnp.float32)
            mixed = y_ref[pl.ds(t, chunk_len, stride=tiles), :]
            gated_ref[:, t * LANES : (t + 1) * LANES] = (
                mixed * (gate / (1.0 + jnp.exp(-gate)))
            ).astype(jnp.bfloat16)
        result = jnp.dot(gated_ref[...], wout_ref[...], preferred_element_type=jnp.float32)
        result = result.astype(jnp.bfloat16)
        for k in range(blocks // chunks):
            o = q * (blocks // chunks) + k
            block = result[k * block_len : (k + 1) * block_len]
            stage[o] = block

            @pl.when(o // blocks_home == c)
            def _():
                land[c, o % blocks_home] = block

            @pl.when(o // blocks_home != c)
            def _():
                out_copy(o).start()
        return 0

    lax.fori_loop(0, chunks, col_chunk, 0)

    def drain_tokens(k, _):
        g, copy = token_copy(k)

        @pl.when(g != me)
        def _():
            copy.wait_send()
        return 0

    lax.fori_loop(0, pieces, drain_tokens, 0)
    for step in range(1, cols_n):
        column_copy(step).wait_send()

    def drain_results(q, _):
        def one(k, _):
            result_copy(q, k).wait_send()
            return 0
        return lax.fori_loop(1, group_n, one, 0)

    lax.fori_loop(0, chunks, drain_results, 0)

    def drain_out(o, _):
        @pl.when(o // blocks_home != c)
        def _():
            out_copy(o).wait_send()
        return 0

    lax.fori_loop(0, blocks, drain_out, 0)
    for source in range(cols_n):
        @pl.when(source != c)
        def _():
            for i in range(blocks_home):
                pltpu.make_async_copy(
                    land.at[source, i], land.at[source, i], orecv_sem.at[source, i]
                ).wait()
    for i in range(blocks_home):
        parts = [
            land[s, i].astype(jnp.float32).reshape(block_len // per_core, per_core, -1)
            for s in range(cols_n)
        ]
        rows = block_len // per_core
        out_ref[i * rows : (i + 1) * rows] = jnp.concatenate(parts, axis=1).astype(jnp.bfloat16)


def per_device_uniform(tokens, norm_gain, w_in, w_bc, rate_row, rate_col, skip_gain, w_out):
    inner, width_out = w_out.shape
    states = rate_row.shape[0]
    height, columns, width = tokens.shape
    rows_n, cols_n = lax.axis_size("rows"), lax.axis_size("cols")
    group_n = rows_n * cols_n
    per_core = columns // cols_n
    total = height * cols_n
    share = min(4, total // group_n)
    chunks = total // (group_n * share)
    pieces = height // share
    piece_len = share * per_core
    chunk_len = group_n * piece_len
    tiles = inner // LANES
    blocks = max(chunks, cols_n)
    block_len = total * per_core // blocks
    patches = total * per_core
    f32, bf16 = jnp.float32, jnp.bfloat16
    dma = pltpu.SemaphoreType.DMA
    out = pl.pallas_call(
        functools.partial(layer_kernel, states, rows_n, cols_n, share, per_core),
        in_specs=[pl.BlockSpec(memory_space=pl.ANY)] * 8,
        out_specs=pl.BlockSpec(memory_space=pltpu.VMEM),
        out_shape=jax.ShapeDtypeStruct((height, columns, width_out), bf16),
        scratch_shapes=[
            pltpu.VMEM((1, width), f32),
            pltpu.VMEM(w_in.shape, bf16),
            pltpu.VMEM(w_bc.shape[::-1], bf16),
            pltpu.VMEM(rate_row.shape, f32),
            pltpu.VMEM(rate_col.shape, f32),
            pltpu.VMEM((1, inner), f32),
            pltpu.VMEM(w_out.shape, bf16),
            pltpu.VMEM((cols_n, height, columns, width), bf16),
            pltpu.VMEM((chunks, rows_n, share, columns, width), bf16),
            pltpu.VMEM((chunks, chunk_len, tiles, LANES), bf16),
            pltpu.VMEM((chunks, chunk_len, tiles, LANES), bf16),
            pltpu.VMEM((chunk_len * tiles, LANES), f32),
            pltpu.VMEM((states, chunk_len + 8, LANES), f32),
            pltpu.VMEM((states, chunk_len + 8, LANES), f32),
            pltpu.VMEM((states, patches + 8, LANES), f32),
            pltpu.VMEM((states, patches + 8, LANES), f32),
            pltpu.VMEM((patches, inner), bf16),
            pltpu.VMEM((chunk_len * tiles, LANES), f32),
            pltpu.VMEM((chunk_len, inner), bf16),
            pltpu.VMEM((states * tiles, LANES), f32),
            pltpu.VMEM((states * tiles, LANES), f32),
            pltpu.VMEM((tiles, LANES), f32),
            pltpu.VMEM((blocks, block_len, width_out), bf16),
            pltpu.VMEM((cols_n, blocks // cols_n, block_len, width_out), bf16),
            pltpu.VMEM((per_core, states, tiles, LANES), f32),
            dma((pieces,)), dma((chunks,)), dma((cols_n,)), dma((cols_n,)),
            dma((chunks, group_n)), dma((chunks,)), dma((blocks,)),
            dma((cols_n, blocks // cols_n)), dma((8,)),
        ],
        compiler_params=pltpu.CompilerParams(
            vmem_limit_bytes=VMEM_LIMIT, collective_id=0, has_side_effects=True
        ),
        name="layer",
    )(tokens, norm_gain[None], w_in, w_bc.T, rate_row, rate_col, skip_gain[None], w_out)
    return out


LANE_PAIR = 2 * LANES
SUBLANES = 8


def grouped_kernel(
    states, rows_n, cols_n, chunks, per_core,
    tok_ref, gain_in, win_in, wbc_in, rrate_in, crate_in, skip_in, wout_in,
    out_ref,
    gain_ref, win_ref, wbc_ref, rrate_ref, crate_ref, skip_ref, wout_ref,
    tokv, nown, ncol, tin_a, tin_b, tin_c, table, order_ref, u_ref, b_ref, uown_ref, bown_ref, cown_ref, lag_ref,
    rsend, rrecv, vcol, inject_ref, spread_ref, read_ref, hist, z_ref, gated_ref, stage, state_ref,
    own_send_sem, next_send_sem, own_sem, early_sem, relay_sem, csend_sem, crecv_sem, rsend_sem, rrecv_sem,
    osend_sem, orecv_sem, fetch_sem, ready_sem,
):
    height, columns, width = tok_ref.shape
    inner = wout_ref.shape[0]
    tiles = inner // LANES
    pairs = inner // LANE_PAIR
    quarter = rows_n // 4
    total = height * cols_n
    chunk_rows = total // chunks
    local_chunks = chunks // cols_n
    lines = quarter * cols_n
    rows = chunk_rows // lines
    run = LANE_PAIR // states
    parts = 1
    share = inner // parts
    r, c = lax.axis_index("rows"), lax.axis_index("cols")

    groups = ((0, quarter), (quarter, quarter), (2 * quarter, 2 * quarter))
    inside = (r < quarter, (r >= quarter) & (r < 2 * quarter), r >= 2 * quarter)
    tins = (tin_a, tin_b, tin_c)
    early = (0, quarter, 2 * quarter)
    line = r % quarter * cols_n + c

    def half_of(q):
        return (q + 1) % 2

    def chip_of(group, q, p):
        chip = groups[group][0] + p // cols_n
        return chip + half_of(q) * quarter if group == 2 else chip

    def slot(group, q):
        return q // 2 if group == 2 else q

    head, rest = pl.ds(0, chunk_rows), pl.ds(chunk_rows, height - chunk_rows)
    fetches = [
        pltpu.make_async_copy(src, dst, fetch_sem.at[k])
        for k, (src, dst) in enumerate((
            (tok_ref.at[head], tokv.at[head]), (gain_in, gain_ref), (tok_ref.at[rest], tokv.at[rest]),
            (rrate_in, rrate_ref), (wbc_in, wbc_ref), (win_in, win_ref),
            (crate_in, crate_ref), (skip_in, skip_ref), (wout_in, wout_ref),
        ))
    ]
    for fetch in fetches:
        fetch.start()

    barrier = pltpu.get_barrier_semaphore()

    def greet(chip, core):
        pl.semaphore_signal(barrier, inc=1, device_id={"rows": chip, "cols": core}, device_id_type=MESH)

    for group, (first, chips) in enumerate(groups):
        @pl.when(inside[group])
        def _():
            me = (r - first) * cols_n + c

            def one(k, _):
                @pl.when(k != me)
                def _():
                    greet(first + k // cols_n, k % cols_n)
                return 0

            lax.fori_loop(0, chips * cols_n, one, 0)
            if group == 1:
                for k in range(2):
                    greet(r + (k + 1) * quarter, c)

                def back(k, _):
                    greet(k // cols_n, k % cols_n)
                    return 0

                lax.fori_loop(0, lines, back, 0)

    def normalise_part(part):
        first = part * chunk_rows
        flat = normalise(tokv[first : first + chunk_rows].astype(jnp.float32).reshape(-1, width), gain_ref[...])
        flat = flat.astype(jnp.float32)
        for t in range(width // LANES):
            order_ref[t, first * columns : (first + chunk_rows) * columns] = flat[:, t * LANES : (t + 1) * LANES]
        for w in range(columns):
            nown[w, first : first + chunk_rows] = jnp.concatenate([
                order_ref[t, pl.ds(first * columns + w, chunk_rows, stride=columns), :] for t in range(width // LANES)
            ], axis=1).astype(jnp.bfloat16)

    for fetch in fetches[:2]:
        fetch.wait()
    normalise_part(0)

    for group, (first, chips) in enumerate(groups):
        @pl.when(inside[group])
        def _():
            pl.semaphore_wait(barrier, chips * cols_n - 1 + (lines, 0, 1)[group])
            if group == 2:
                pl.semaphore_signal(
                    ready_sem, inc=1, device_id={"rows": first - quarter + (r - first) % quarter}, device_id_type=MESH
                )

    def token_copy(group, n):
        part, p = n // lines, (n + line) % lines
        q = c * local_chunks + part
        chip, core = chip_of(group, q, p), p % cols_n
        src = nown.at[:, pl.ds(pl.multiple_of(part * chunk_rows + p * rows, rows), rows)]
        dst = tins[group].at[slot(group, q), early[group] + r - groups[group][0]]
        remote = pltpu.make_async_remote_copy(
            src_ref=src, dst_ref=dst, send_sem=own_send_sem.at[0], recv_sem=own_sem.at[q],
            device_id={"rows": chip, "cols": core}, device_id_type=MESH,
        )
        away = (chip != r) | (core != c)
        return away, remote, lambda: pltpu.make_async_copy(src, dst, own_sem.at[q])

    def send_own(low, high):
        for group in range(3):
            @pl.when(inside[group])
            def _():
                def one(n, _):
                    away, remote, local = token_copy(group, n)

                    @pl.when(away)
                    def _():
                        remote.start()

                    @pl.when(jnp.logical_not(away))
                    def _():
                        local().start()
                    return 0

                lax.fori_loop(low * lines, high * lines, one, 0)

    def next_copy(part, p):
        p = (p + line) % lines
        return pltpu.make_async_remote_copy(
            src_ref=nown.at[:, pl.ds(pl.multiple_of(part * chunk_rows + p * rows, rows), rows)],
            dst_ref=tin_b.at[part, r], send_sem=next_send_sem.at[0], recv_sem=early_sem.at[part],
            device_id={"rows": quarter + p // cols_n, "cols": p % cols_n}, device_id_type=MESH,
        )

    def send_first(part):
        @pl.when(c == 0)
        def _():
            send_own(part, part + 1)

        @pl.when(inside[0] & (c == 0))
        def _():
            def one(p, _):
                next_copy(part, p).start()
                return 0

            lax.fori_loop(0, lines, one, 0)

    direct = 2
    send_first(0)
    fetches[2].wait()
    for part in range(1, local_chunks):
        normalise_part(part)

    def column_copy(step):
        other = (c + step) % cols_n
        return pltpu.make_async_remote_copy(
            src_ref=nown.at[pl.ds(other * per_core, per_core)], dst_ref=ncol.at[c],
            send_sem=csend_sem.at[step], recv_sem=crecv_sem.at[step],
            device_id={"cols": other}, device_id_type=MESH,
        )

    for step in range(1, cols_n):
        column_copy(step).start()

    def drain_own(group):
        count = local_chunks * (lines - 1) if group < 2 else local_chunks * lines - local_chunks // 2
        sent = nown.at[:, pl.ds(0, count * rows)]
        pltpu.make_async_copy(sent, sent, own_send_sem.at[0]).wait()

    def own_wait(group, q):
        part = tins[group].at[slot(group, q), pl.ds(early[group], groups[group][1])]
        pltpu.make_async_copy(part, part, own_sem.at[q]).wait()

    def early_wait(group, q):
        part = tins[group].at[slot(group, q), pl.ds(0, early[group])]
        pltpu.make_async_copy(part, part, early_sem.at[q]).wait()

    def relay_copy(group, q, which):
        if group == 0:
            src, dst, chip = tin_a.at[q], tin_b.at[q, pl.ds(0, quarter)], r + quarter
        else:
            src = tin_b.at[q, pl.ds(which * quarter, quarter)]
            dst = tin_c.at[q // 2, pl.ds(which * quarter, quarter)]
            chip = r + quarter + half_of(q) * quarter
        return pltpu.make_async_remote_copy(
            src_ref=src, dst_ref=dst, send_sem=relay_sem.at[q, which], recv_sem=early_sem.at[q],
            device_id={"rows": chip}, device_id_type=MESH,
        )

    def relay_own(group, q):
        own_wait(group, q)
        relay_copy(group, q, 1).start()

    def relay_early(group, q):
        early_wait(group, q)
        relay_copy(group, q, 0).start()

    def gate_part(core, normed_of):
        for w in range(per_core):
            normed = normed_of(w)
            base = pl.multiple_of(w * total + core * height, height)
            inject = transposed_dot(normed, wbc_ref[2 * states : 3 * states])
            inject = inject.astype(jnp.bfloat16).astype(jnp.float32)
            for n in range(states):
                inject_ref[pl.ds(base * states + n, height, stride=states), :] = jnp.broadcast_to(
                    inject[:, n : n + 1], (height, LANES)
                )
            read = transposed_dot(normed, spread_ref[...])
            owner = lax.broadcasted_iota(jnp.int32, read.shape, 1) // states
            here = lax.broadcasted_iota(jnp.int32, read.shape, 0) % run
            read_ref[pl.ds(base, height), :] = jnp.where(owner == here, read, 0.0).astype(jnp.bfloat16)
            for k in range(0, inner, LANE_PAIR):
                z_ref[pl.ds(base, height), k : k + LANE_PAIR] = jnp.dot(
                    normed, win_ref[:, inner + k : inner + k + LANE_PAIR],
                    preferred_element_type=jnp.float32,
                ).astype(jnp.bfloat16)

    for fetch in fetches[3:]:
        fetch.wait()

    for group, (first, chips) in enumerate(groups):
        @pl.when(inside[group])
        def _():
            def fill(d, _):
                for k in range(pairs):
                    rate = rrate_ref[:, k * LANE_PAIR : (k + 1) * LANE_PAIR]
                    table[k, d] = jnp.exp(-rate * d.astype(jnp.float32)).astype(jnp.bfloat16)
                return 0

            lax.fori_loop(0, (early[group] + chips) * columns, fill, 0)

    for i in range(run):
        spread_ref[i * states : (i + 1) * states] = wbc_ref[3 * states : 4 * states]
    crate_ref[...] = jnp.exp(-crate_ref[...])
    state_ref[...] = jnp.zeros(state_ref.shape, jnp.float32)
    gated_ref[...] = jnp.zeros(gated_ref.shape, jnp.bfloat16)
    send_first(1)
    gate_part(c, lambda w: nown[c * per_core + w])

    @pl.when(c == 0)
    def _():
        send_own(direct, local_chunks)

    @pl.when(inside[1])
    def _():
        pl.semaphore_wait(ready_sem, 2)
        relay_own(1, 0)

    for step in range(1, cols_n):
        column_copy(step).wait_recv()
        source = (c + cols_n - step) % cols_n
        gate_part(source, lambda w: ncol[source, w])

    @pl.when(c > 0)
    def _():
        send_own(0, local_chunks)

    @pl.when(inside[0])
    def _():
        def one(q, _):
            relay_own(0, q)
            return 0

        for q in range(direct):
            own_wait(0, q)
        lax.fori_loop(direct, local_chunks, one, 0)

    @pl.when(inside[1])
    def _():
        relay_early(1, 0)
        relay_own(1, 1)

    def result_copy(group, q, part, k):
        first, chips = groups[group]
        g = ((r - first) * cols_n + c + k) % (chips * cols_n)
        some = pl.ds(pl.multiple_of(part * share, share), share)
        src, dst = rsend.at[slot(group, q), g, :, :, some], rrecv.at[q, line, :, :, some]
        remote = pltpu.make_async_remote_copy(
            src_ref=src, dst_ref=dst, send_sem=rsend_sem.at[slot(group, q)], recv_sem=rrecv_sem.at[q],
            device_id={"rows": first + g // cols_n, "cols": g % cols_n}, device_id_type=MESH,
        )
        return remote, lambda: pltpu.make_async_copy(src, dst, rrecv_sem.at[q])

    def rounded(value):
        return value.astype(jnp.bfloat16).astype(jnp.float32)

    def project_in(normed, k):
        return rounded(jnp.dot(
            normed, win_ref[:, k * LANE_PAIR : (k + 1) * LANE_PAIR], preferred_element_type=jnp.float32
        ))

    def own_part(group, q):
        chips = groups[group][1]
        before = early[group]
        count = chips * columns * rows
        ready = slot(group, q) if group == 2 else 0
        if group == 2:
            own_wait(group, q)
        normed = tins[group][slot(group, q), before : before + chips].reshape(count, width)
        bown_ref[ready, :count] = rounded(transposed_dot(normed, wbc_ref[:states]))
        cown_ref[ready, :count] = rounded(transposed_dot(normed, wbc_ref[states : 2 * states]))
        for k in range(pairs):
            uown_ref[ready, k, :count] = project_in(normed, k)

    def row_chunk(group, q):
        chips = groups[group][1]
        before = early[group]
        at = slot(group, q)
        tin = tins[group]
        out_cols, pre_cols = chips * columns, before * columns
        all_cols = out_cols + pre_cols
        if group < 2:
            own_part(group, q)
        else:
            early_wait(group, q)
        ready = at if group == 2 else 0
        if before:
            normed = tin[at, :before].reshape(pre_cols * rows, width)
            b_ref[: pre_cols * rows] = rounded(transposed_dot(normed, wbc_ref[:states]))
            for k in range(pairs):
                u_ref[k, : pre_cols * rows] = project_in(normed, k)
        b_ref[pre_cols * rows : all_cols * rows] = bown_ref[ready, : out_cols * rows]

        def value_of(k, col):
            if col < pre_cols:
                return u_ref[k, col * rows : (col + 1) * rows]
            return uown_ref[ready, k, (col - pre_cols) * rows : (col - pre_cols + 1) * rows]

        def span(d):
            low = max(0, d - pre_cols)
            return low, out_cols - low, pre_cols + low - d

        for d in range(all_cols):
            low, count, source = span(d)
            lag_ref[d, : count * rows] = (
                cown_ref[ready, low * rows : out_cols * rows] * b_ref[source * rows : (source + count) * rows]
            ).astype(jnp.bfloat16)

        def one_pair(k):
            skip = skip_ref[k]
            sums = [
                skip * value_of(k, pre_cols + o) for o in range(out_cols)
            ]
            for d in range(all_cols):
                low, count, source = span(d)
                weight = jnp.dot(lag_ref[d, : count * rows], table[k, d], preferred_element_type=jnp.float32)
                for i in range(count):
                    sums[low + i] += weight[i * rows : (i + 1) * rows] * value_of(k, source + i)
            some = pl.ds(pl.multiple_of(k * LANE_PAIR, LANE_PAIR), LANE_PAIR)
            for o in range(out_cols):
                rsend[at, o // per_core, o % per_core, :, some] = sums[o].astype(jnp.bfloat16)

        def one_part(part, _):
            for k in range(pairs // parts):
                one_pair(part * (pairs // parts) + k)
            result_copy(group, q, part, 0)[1]().start()

            def send_result(k, _):
                result_copy(group, q, part, k)[0].start()
                return 0

            lax.fori_loop(1, chips * cols_n, send_result, 0)
            return 0

        lax.fori_loop(0, parts, one_part, 0)

    def out_part(core, i):
        first = pl.multiple_of(i * chunk_rows, chunk_rows)
        return out_ref.at[pl.ds(core * per_core, per_core), pl.ds(first, chunk_rows)]

    def out_copy(q):
        return pltpu.make_async_remote_copy(
            src_ref=stage.at[q], dst_ref=out_part(c, q % local_chunks),
            send_sem=osend_sem.at[q], recv_sem=orecv_sem.at[c, q % local_chunks],
            device_id={"cols": q // local_chunks}, device_id_type=MESH,
        )

    def col_chunk(q):
        pltpu.make_async_copy(rrecv.at[q], rrecv.at[q], rrecv_sem.at[q]).wait()
        for p in range(lines):
            for w in range(per_core):
                value = rrecv[q, p, w].astype(jnp.float32)
                for t in range(tiles):
                    vcol[t, w * chunk_rows + p * rows : w * chunk_rows + (p + 1) * rows] = (
                        value[:, t * LANES : (t + 1) * LANES]
                    )
        project((q + chunks - 1) % chunks)
        halves = range(0, states, SUBLANES)

        def one_run(i):
            for w in range(per_core):
                here = w * chunk_rows + i * run
                patch = pl.multiple_of(w * total + q * chunk_rows + i * run, run)
                decay = [[crate_ref[h : h + SUBLANES, t * LANES : (t + 1) * LANES] for t in range(tiles)] for h in halves]
                state = [[state_ref[w, h : h + SUBLANES, t * LANES : (t + 1) * LANES] for t in range(tiles)] for h in halves]
                for s in range(run):
                    inject = [
                        inject_ref[pl.ds(pl.multiple_of((patch + s) * states + h, SUBLANES), SUBLANES), :] for h in halves
                    ]
                    for t in range(tiles):
                        value = vcol[t, pl.ds(here + s, SUBLANES, stride=0), :]
                        for j in range(len(inject)):
                            state[j][t] = decay[j][t] * state[j][t] + inject[j] * value
                        hist[i * per_core + w, t, s * states : (s + 1) * states, :] = jnp.concatenate(
                            [state[j][t] for j in range(len(inject))], axis=0
                        ).astype(jnp.bfloat16)
                for j, h in enumerate(halves):
                    for t in range(tiles):
                        state_ref[w, h : h + SUBLANES, t * LANES : (t + 1) * LANES] = state[j][t]
                for t in range(tiles):
                    if t % 2 == 0:
                        both_tiles = jnp.concatenate([hist[i * per_core + w, t], hist[i * per_core + w, t + 1]], axis=1)
                        mixed = jnp.dot(
                            read_ref[pl.ds(patch, run), :], both_tiles, preferred_element_type=jnp.float32
                        )
                    gate = z_ref[pl.ds(patch, run), t * LANES : (t + 1) * LANES].astype(jnp.float32)
                    both = mixed[:, t % 2 * LANES : (t % 2 + 1) * LANES] + vcol[t, pl.ds(here, run), :]
                    gated_ref[q % 2, pl.ds(here, run), t * LANES : (t + 1) * LANES] = (
                        both * (gate / (1.0 + jnp.exp(-gate)))
                    ).astype(jnp.bfloat16)

        for i in range(chunk_rows // run):
            one_run(i)

        @pl.when(q > 0)
        def _():
            send_out(q - 1)

    def project(q):
        result = jnp.dot(gated_ref[q % 2], wout_ref[...], preferred_element_type=jnp.float32).astype(jnp.bfloat16)
        stage[q] = result.reshape(per_core, chunk_rows, -1)

    def send_out(q):
        home = q // local_chunks

        @pl.when(home == c)
        def _():
            pltpu.make_async_copy(stage.at[q], out_part(c, q % local_chunks), orecv_sem.at[c, q % local_chunks]).start()

        @pl.when(home != c)
        def _():
            out_copy(q).start()

    def one_chunk(q, _):
        for group in range(3):
            mine = inside[group] & (q < chunks)
            if group == 2:
                mine = mine & (half_of(q) == (r - 2 * quarter) // quarter)

            @pl.when(mine)
            def _():
                row_chunk(group, q)
                if group == 2:
                    @pl.when(q + 2 < chunks)
                    def _():
                        own_part(group, q + 2)

            if group == 0:
                @pl.when(inside[group] & (q + local_chunks < chunks))
                def _():
                    relay_own(group, q + local_chunks)
            if group == 1:
                @pl.when(inside[group] & (q + 1 < chunks))
                def _():
                    relay_early(group, q + 1)

                @pl.when(inside[group] & (q + 2 < chunks))
                def _():
                    relay_own(group, q + 2)

        @pl.when(q >= lag)
        def _():
            col_chunk(q - lag)
        return 0

    @pl.when(inside[2])
    def _():
        own_part(2, 1 - (r - 2 * quarter) // quarter)

    lag = 3
    lax.fori_loop(0, chunks + lag, one_chunk, 0)
    project(chunks - 1)
    send_out(chunks - 1)

    for group, (first, chips) in enumerate(groups):
        @pl.when(inside[group])
        def _():
            drain_own(group)

            def drain_chunk(q, _):
                relay_copy(group, q, 1).wait_send()
                if group == 1:
                    relay_copy(group, q, 0).wait_send()
                return 0

            if group == 0:
                @pl.when(c == 0)
                def _():
                    sent = nown.at[:, pl.ds(0, direct * lines * rows)]
                    pltpu.make_async_copy(sent, sent, next_send_sem.at[0]).wait()
            if group < 2:
                lax.fori_loop((direct, 0)[group], chunks, drain_chunk, 0)
            for at in range(chunks // (1 + group // 2)):
                sent = rsend.at[at, pl.ds(0, chips * cols_n - 1)]
                pltpu.make_async_copy(sent, sent, rsend_sem.at[at]).wait()

    for step in range(1, cols_n):
        column_copy(step).wait_send()

    def drain_out(q, _):
        @pl.when(q // local_chunks != c)
        def _():
            out_copy(q).wait_send()
        return 0

    lax.fori_loop(0, chunks, drain_out, 0)
    for source in range(cols_n):
        for i in range(local_chunks):
            part = out_part(source, i)
            pltpu.make_async_copy(part, part, orecv_sem.at[source, i]).wait()


def per_device_grouped(chunks, tokens, norm_gain, w_in, w_bc, rate_row, rate_col, skip_gain, w_out):
    inner, width_out = w_out.shape
    states = rate_row.shape[0]
    height, columns, width = tokens.shape
    rows_n, cols_n = lax.axis_size("rows"), lax.axis_size("cols")
    quarter = rows_n // 4
    per_core = columns // cols_n
    total = height * cols_n
    chunk_rows = total // chunks
    lines = quarter * cols_n
    rows = chunk_rows // lines
    tiles = inner // LANES
    pairs = inner // LANE_PAIR
    patches = total * per_core
    local_chunks = chunks // cols_n
    lags = rows_n * columns
    held = lags * rows
    outs = 2 * quarter * columns * rows
    f32, bf16 = jnp.float32, jnp.bfloat16
    dma = pltpu.SemaphoreType.DMA
    out = pl.pallas_call(
        functools.partial(grouped_kernel, states, rows_n, cols_n, chunks, per_core),
        in_specs=[pl.BlockSpec(memory_space=pl.ANY)] * 8,
        out_specs=pl.BlockSpec(memory_space=pl.ANY),
        out_shape=pltpu.VMEM((columns, height, width_out), bf16),
        scratch_shapes=[
            pltpu.VMEM((1, width), f32),
            pltpu.VMEM(w_in.shape, bf16),
            pltpu.VMEM(w_bc.shape[::-1], bf16),
            pltpu.VMEM(rate_row.shape, f32),
            pltpu.VMEM(rate_col.shape, f32),
            pltpu.VMEM((pairs, 1, LANE_PAIR), f32),
            pltpu.VMEM(w_out.shape, bf16),
            pltpu.VMEM((height, columns, width), bf16),
            pltpu.VMEM((columns, height, width), bf16),
            pltpu.VMEM((cols_n, per_core, height, width), bf16),
            pltpu.VMEM((chunks, quarter, columns, rows, width), bf16),
            pltpu.VMEM((chunks, 2 * quarter, columns, rows, width), bf16),
            pltpu.VMEM((chunks // 2, 4 * quarter, columns, rows, width), bf16),
            pltpu.VMEM((pairs, lags, states, LANE_PAIR), bf16),
            pltpu.VMEM((width // LANES, height * columns, LANES), f32),
            pltpu.VMEM((pairs, held, LANE_PAIR), f32),
            pltpu.VMEM((held, states), f32),
            pltpu.VMEM((chunks // 2, pairs, outs, LANE_PAIR), f32),
            pltpu.VMEM((chunks // 2, outs, states), f32),
            pltpu.VMEM((chunks // 2, outs, states), f32),
            pltpu.VMEM((lags, outs, states), bf16),
            pltpu.VMEM((chunks, 2 * lines, per_core, rows, inner), bf16),
            pltpu.VMEM((chunks, lines, per_core, rows, inner), bf16),
            pltpu.VMEM((tiles, per_core * chunk_rows + SUBLANES, LANES), f32),
            pltpu.VMEM((patches * states, LANES), f32),
            pltpu.VMEM((LANE_PAIR, width), bf16),
            pltpu.VMEM((patches, LANE_PAIR), bf16),
            pltpu.VMEM((per_core * chunk_rows * states // LANE_PAIR, tiles, LANE_PAIR, LANES), bf16),
            pltpu.VMEM((patches, inner), bf16),
            pltpu.VMEM((2, per_core * chunk_rows, inner), bf16),
            pltpu.VMEM((chunks, per_core, chunk_rows, width_out), bf16),
            pltpu.VMEM((per_core, states, inner), f32),
            dma((1,)), dma((1,)), dma((chunks,)), dma((chunks,)), dma((chunks, 2)),
            dma((cols_n,)), dma((cols_n,)),
            dma((chunks,)), dma((chunks,)), dma((chunks,)),
            dma((cols_n, local_chunks)), dma((9,)), pltpu.SemaphoreType.REGULAR,
        ],
        compiler_params=pltpu.CompilerParams(
            vmem_limit_bytes=VMEM_LIMIT, collective_id=0, has_side_effects=True
        ),
        name="layer",
    )(
        tokens, norm_gain[None], w_in, w_bc.T, rate_row, rate_col,
        skip_gain.reshape(pairs, 1, LANE_PAIR), w_out,
    )
    return out.transpose(1, 0, 2)


def chunk_count(tokens, rate_row, inner):
    height, columns, _ = tokens.shape
    states = rate_row.shape[0]
    rows_n, cols_n = lax.axis_size("rows"), lax.axis_size("cols")
    total = height * cols_n
    if rows_n % 4 or columns % cols_n or inner % LANE_PAIR or states % SUBLANES or LANE_PAIR % states:
        return 0
    step = rows_n // 4 * cols_n * SUBLANES
    run = LANE_PAIR // states
    if total % step or step % run or total // step % (2 * cols_n):
        return 0
    return total // step


def per_device(tokens, norm_gain, w_in, w_bc, rate_row, rate_col, skip_gain, w_out):
    args = (tokens, norm_gain, w_in, w_bc, rate_row, rate_col, skip_gain, w_out)
    chunks = chunk_count(tokens, rate_row, w_out.shape[0])
    if chunks:
        return per_device_grouped(chunks, *args)
    return per_device_uniform(*args)


def solution(mesh):
    placed = (P(("slides", "cols"), "rows", None), P(), P(), P(), P(), P(), P(), P())
    return jax.shard_map(
        per_device,
        mesh=mesh,
        in_specs=placed,
        out_specs=P(("slides", "cols"), "rows", None),
        check_vma=False,
    )
```

```python
import functools

import jax
import jax.numpy as jnp
from jax import lax
from jax.experimental import pallas as pl
from jax.experimental.pallas import tpu as pltpu
from jax.sharding import PartitionSpec as P

LANES = 128
VMEM_LIMIT = 60 * 1024 * 1024
MESH = pl.DeviceIdType.MESH


def normalise(tokens, gain):
    as_float = tokens.astype(jnp.float32)
    scale_now = lax.rsqrt(jnp.mean(as_float * as_float, axis=-1, keepdims=True) + 1e-05)
    return (as_float * scale_now * gain).astype(jnp.bfloat16)


def transposed_dot(a, b):
    return lax.dot_general(a, b, (((1,), (1,)), ((), ())), preferred_element_type=jnp.float32)


def spread_channels(ref, value, tiles):
    rows = value.shape[0]
    for t in range(tiles):
        ref[pl.ds(t, rows, stride=tiles), :] = value[:, t * LANES : (t + 1) * LANES]


def spread_vectors(ref, value, first, states, base):
    rows = value.shape[0]
    for n in range(states):
        ref[n, pl.ds(base, rows), :] = jnp.broadcast_to(
            value[:, first + n : first + n + 1], (rows, LANES)
        )


def scan_step(carried, decay, value, inject_ref, readout_ref, patch, start, tiles):
    new = []
    totals = [start, None]
    for n, state in enumerate(carried):
        inject = inject_ref[n, pl.ds(patch, tiles, stride=0), :]
        readout = readout_ref[n, pl.ds(patch, tiles, stride=0), :]
        state = decay[n] * state + inject * value
        term = readout * state
        totals[n % 2] = term if totals[n % 2] is None else totals[n % 2] + term
        new.append(state)
    return tuple(new), totals[0] + totals[1]


def layer_kernel(
    states, rows_n, cols_n, share, per_core,
    tok_ref, gain_in, win_in, wbc_in, rrate_in, crate_in, skip_in, wout_in,
    out_ref,
    gain_ref, win_ref, wbc_ref, rrate_ref, crate_ref, skip_ref, wout_ref, tcol, tin, rsend, rrecv, u_ref, rb_ref, rc_ref, cb_ref, cc_ref, z_ref, y_ref, gated_ref,
    rdecay, cdecay, skip_tile, stage, land, state_ref,
    tsend_sem, tin_sem, csend_sem, crecv_sem, rsend_sem, rrecv_sem, osend_sem, orecv_sem, fetch_sem,
):
    group_n = rows_n * cols_n
    pieces = tok_ref.shape[0] // share
    chunks = tin.shape[0]
    columns, width = tok_ref.shape[1:]
    inner = wout_ref.shape[0]
    tiles = inner // LANES
    piece_len = share * per_core
    chunk_len = group_n * piece_len
    blocks = stage.shape[0]
    blocks_home = blocks // cols_n
    block_len = stage.shape[1]
    r, c = lax.axis_index("rows"), lax.axis_index("cols")
    me = r * cols_n + c

    def spot(g):
        return {"rows": g // cols_n, "cols": g % cols_n}

    barrier = pltpu.get_barrier_semaphore()

    def greet(g, _):
        @pl.when(g != me)
        def _():
            pl.semaphore_signal(barrier, inc=1, device_id=spot(g), device_id_type=MESH)
        return 0

    lax.fori_loop(0, group_n, greet, 0)
    fetches = [
        pltpu.make_async_copy(src, dst, fetch_sem.at[k])
        for k, (src, dst) in enumerate((
            (rrate_in, rrate_ref), (crate_in, crate_ref), (skip_in, skip_ref), (gain_in, gain_ref),
            (wbc_in, wbc_ref), (tok_ref, tcol.at[c]), (win_in, win_ref), (wout_in, wout_ref),
        ))
    ]
    for fetch in fetches:
        fetch.start()
    pl.semaphore_wait(barrier, group_n - 1)

    local_chunks = max(1, chunks // cols_n)
    per_chunk = pieces // local_chunks

    def piece_of(k):
        piece = k // per_chunk * per_chunk + (k % per_chunk + me) % per_chunk
        place = c * pieces + piece
        return piece, place // group_n, place % group_n

    def token_copy(k):
        piece, q, g = piece_of(k)
        return g, pltpu.make_async_remote_copy(
            src_ref=tok_ref.at[pl.ds(piece * share, share)], dst_ref=tin.at[q, r],
            send_sem=tsend_sem.at[piece], recv_sem=tin_sem.at[q],
            device_id=spot(g), device_id_type=MESH,
        )

    def send_tokens(k, _):
        piece, q, g = piece_of(k)

        @pl.when(g == me)
        def _():
            pltpu.make_async_copy(tok_ref.at[pl.ds(piece * share, share)], tin.at[q, r], tin_sem.at[q]).start()

        @pl.when(g != me)
        def _():
            token_copy(k)[1].start()
        return 0

    lax.fori_loop(0, pieces, send_tokens, 0)

    def column_copy(step):
        other = (c + step) % cols_n
        return pltpu.make_async_remote_copy(
            src_ref=tok_ref, dst_ref=tcol.at[c],
            send_sem=csend_sem.at[step], recv_sem=crecv_sem.at[step],
            device_id={"cols": other}, device_id_type=MESH,
        )

    for step in range(1, cols_n):
        column_copy(step).start()

    def gate_part(tokens, core):
        tokens = tokens.astype(jnp.float32)
        own = tokens[:, :per_core]
        for k in range(1, cols_n):
            own = jnp.where(c == k, tokens[:, k * per_core : (k + 1) * per_core], own)
        normed = normalise(own.reshape(-1, width), gain_ref[...])
        count = normed.shape[0]
        base = pl.multiple_of(core * count, count)
        mixers = transposed_dot(normed, wbc_ref[...])
        mixers = mixers.astype(jnp.bfloat16).astype(jnp.float32)
        spread_vectors(cb_ref, mixers, 2 * states, states, base)
        spread_vectors(cc_ref, mixers, 3 * states, states, base)
        for k in range(0, inner, 2 * LANES):
            z_ref[pl.ds(base, count), k : k + 2 * LANES] = jnp.dot(
                normed, win_ref[:, inner + k : inner + k + 2 * LANES],
                preferred_element_type=jnp.float32,
            ).astype(jnp.bfloat16)

    for fetch in fetches:
        fetch.wait()
    spread_channels(rdecay, jnp.exp(-rrate_ref[...]), tiles)
    spread_channels(cdecay, jnp.exp(-crate_ref[...]), tiles)
    spread_channels(skip_tile, skip_ref[...], tiles)
    gate_part(tcol[c], c)

    zero = jnp.zeros((tiles, LANES), jnp.float32)
    lanes = 2 if share % 2 == 0 else 1

    def result_copy(q, k):
        g = (me + k) % group_n
        return pltpu.make_async_remote_copy(
            src_ref=rsend.at[q, pl.ds(g * piece_len, piece_len)],
            dst_ref=rrecv.at[q, pl.ds(me * piece_len, piece_len)],
            send_sem=rsend_sem.at[q, k], recv_sem=rrecv_sem.at[q],
            device_id=spot(g), device_id_type=MESH,
        )

    def row_chunk(q, _):
        pltpu.make_async_copy(tin.at[q], tin.at[q], tin_sem.at[q]).wait()
        normed = normalise(tin[q].astype(jnp.float32).reshape(chunk_len, width), gain_ref[...])
        mixers = transposed_dot(normed, wbc_ref[...])
        mixers = mixers.astype(jnp.bfloat16).astype(jnp.float32)
        spread_vectors(rb_ref, mixers, 0, states, 0)
        spread_vectors(rc_ref, mixers, states, states, 0)
        for k in range(0, tiles, 2):
            part = jnp.dot(normed, win_ref[:, k * LANES : (k + 2) * LANES],
                           preferred_element_type=jnp.float32)
            part = part.astype(jnp.bfloat16).astype(jnp.float32)
            for h in range(2):
                u_ref[pl.ds(k + h, chunk_len, stride=tiles), :] = part[:, h * LANES : (h + 1) * LANES]
        decay = [rdecay[n * tiles : (n + 1) * tiles, :] for n in range(states)]
        skip = skip_tile[...]

        def one_group(first, _):
            def one_step(j, carry):
                carry = list(carry)
                for w in range(columns):
                    for b in range(lanes):
                        row = first * lanes + b
                        patch = (j * share + row) * columns + w
                        owner = j * cols_n + w // per_core
                        value = u_ref[pl.ds(pl.multiple_of(patch * tiles, tiles), tiles), :]
                        carry[b], total = scan_step(carry[b], decay, value, rb_ref, rc_ref,
                                                    patch, skip * value, tiles)
                        rsend[q, (owner * share + row) * per_core + w % per_core] = total.astype(jnp.bfloat16)
                return tuple(carry)

            lax.fori_loop(0, rows_n, one_step, tuple((zero,) * states for _ in range(lanes)))
            return 0

        lax.fori_loop(0, share // lanes, one_group, 0)

        def send_result(k, _):
            result_copy(q, k).start()
            return 0

        pltpu.make_async_copy(
            rsend.at[q, pl.ds(me * piece_len, piece_len)],
            rrecv.at[q, pl.ds(me * piece_len, piece_len)], rrecv_sem.at[q],
        ).start()
        lax.fori_loop(1, group_n, send_result, 0)
        return 0

    lax.fori_loop(0, chunks, row_chunk, 0)

    for step in range(1, cols_n):
        column_copy(step).wait_recv()
        source = (c + cols_n - step) % cols_n
        gate_part(tcol[source], source)

    for g in range(per_core):
        for n in range(states):
            state_ref[g, n] = zero

    def out_copy(o):
        return pltpu.make_async_remote_copy(
            src_ref=stage.at[o], dst_ref=land.at[c, o % blocks_home],
            send_sem=osend_sem.at[o], recv_sem=orecv_sem.at[c, o % blocks_home],
            device_id={"cols": o // blocks_home}, device_id_type=MESH,
        )

    def col_chunk(q, _):
        pltpu.make_async_copy(rrecv.at[q], rrecv.at[q], rrecv_sem.at[q]).wait()
        decay = [cdecay[n * tiles : (n + 1) * tiles, :] for n in range(states)]
        base = q * chunk_len

        def one_step(s, carry):
            result = []
            for g in range(per_core):
                patch = s * per_core + g
                value = rrecv[q, patch].astype(jnp.float32)
                state, total = scan_step(carry[g], decay, value, cb_ref, cc_ref,
                                         base + patch, value, tiles)
                y_ref[pl.ds(pl.multiple_of(patch * tiles, tiles), tiles), :] = total
                result.append(state)
            return tuple(result)

        carry = tuple(tuple(state_ref[g, n] for n in range(states)) for g in range(per_core))
        carry = lax.fori_loop(0, chunk_len // per_core, one_step, carry)
        for g in range(per_core):
            for n in range(states):
                state_ref[g, n] = carry[g][n]
        start = pl.multiple_of(base, chunk_len)
        for t in range(tiles):
            gate = z_ref[pl.ds(start, chunk_len), t * LANES : (t + 1) * LANES].astype(jnp.float32)
            mixed = y_ref[pl.ds(t, chunk_len, stride=tiles), :]
            gated_ref[:, t * LANES : (t + 1) * LANES] = (
                mixed * (gate / (1.0 + jnp.exp(-gate)))
            ).astype(jnp.bfloat16)
        result = jnp.dot(gated_ref[...], wout_ref[...], preferred_element_type=jnp.float32)
        result = result.astype(jnp.bfloat16)
        for k in range(blocks // chunks):
            o = q * (blocks // chunks) + k
            block = result[k * block_len : (k + 1) * block_len]
            stage[o] = block

            @pl.when(o // blocks_home == c)
            def _():
                land[c, o % blocks_home] = block

            @pl.when(o // blocks_home != c)
            def _():
                out_copy(o).start()
        return 0

    lax.fori_loop(0, chunks, col_chunk, 0)

    def drain_tokens(k, _):
        g, copy = token_copy(k)

        @pl.when(g != me)
        def _():
            copy.wait_send()
        return 0

    lax.fori_loop(0, pieces, drain_tokens, 0)
    for step in range(1, cols_n):
        column_copy(step).wait_send()

    def drain_results(q, _):
        def one(k, _):
            result_copy(q, k).wait_send()
            return 0
        return lax.fori_loop(1, group_n, one, 0)

    lax.fori_loop(0, chunks, drain_results, 0)

    def drain_out(o, _):
        @pl.when(o // blocks_home != c)
        def _():
            out_copy(o).wait_send()
        return 0

    lax.fori_loop(0, blocks, drain_out, 0)
    for source in range(cols_n):
        @pl.when(source != c)
        def _():
            for i in range(blocks_home):
                pltpu.make_async_copy(
                    land.at[source, i], land.at[source, i], orecv_sem.at[source, i]
                ).wait()
    for i in range(blocks_home):
        parts = [
            land[s, i].astype(jnp.float32).reshape(block_len // per_core, per_core, -1)
            for s in range(cols_n)
        ]
        rows = block_len // per_core
        out_ref[i * rows : (i + 1) * rows] = jnp.concatenate(parts, axis=1).astype(jnp.bfloat16)


def per_device_uniform(tokens, norm_gain, w_in, w_bc, rate_row, rate_col, skip_gain, w_out):
    inner, width_out = w_out.shape
    states = rate_row.shape[0]
    height, columns, width = tokens.shape
    rows_n, cols_n = lax.axis_size("rows"), lax.axis_size("cols")
    group_n = rows_n * cols_n
    per_core = columns // cols_n
    total = height * cols_n
    share = min(4, total // group_n)
    chunks = total // (group_n * share)
    pieces = height // share
    piece_len = share * per_core
    chunk_len = group_n * piece_len
    tiles = inner // LANES
    blocks = max(chunks, cols_n)
    block_len = total * per_core // blocks
    patches = total * per_core
    f32, bf16 = jnp.float32, jnp.bfloat16
    dma = pltpu.SemaphoreType.DMA
    out = pl.pallas_call(
        functools.partial(layer_kernel, states, rows_n, cols_n, share, per_core),
        in_specs=[pl.BlockSpec(memory_space=pl.ANY)] * 8,
        out_specs=pl.BlockSpec(memory_space=pltpu.VMEM),
        out_shape=jax.ShapeDtypeStruct((height, columns, width_out), bf16),
        scratch_shapes=[
            pltpu.VMEM((1, width), f32),
            pltpu.VMEM(w_in.shape, bf16),
            pltpu.VMEM(w_bc.shape[::-1], bf16),
            pltpu.VMEM(rate_row.shape, f32),
            pltpu.VMEM(rate_col.shape, f32),
            pltpu.VMEM((1, inner), f32),
            pltpu.VMEM(w_out.shape, bf16),
            pltpu.VMEM((cols_n, height, columns, width), bf16),
            pltpu.VMEM((chunks, rows_n, share, columns, width), bf16),
            pltpu.VMEM((chunks, chunk_len, tiles, LANES), bf16),
            pltpu.VMEM((chunks, chunk_len, tiles, LANES), bf16),
            pltpu.VMEM((chunk_len * tiles, LANES), f32),
            pltpu.VMEM((states, chunk_len + 8, LANES), f32),
            pltpu.VMEM((states, chunk_len + 8, LANES), f32),
            pltpu.VMEM((states, patches + 8, LANES), f32),
            pltpu.VMEM((states, patches + 8, LANES), f32),
            pltpu.VMEM((patches, inner), bf16),
            pltpu.VMEM((chunk_len * tiles, LANES), f32),
            pltpu.VMEM((chunk_len, inner), bf16),
            pltpu.VMEM((states * tiles, LANES), f32),
            pltpu.VMEM((states * tiles, LANES), f32),
            pltpu.VMEM((tiles, LANES), f32),
            pltpu.VMEM((blocks, block_len, width_out), bf16),
            pltpu.VMEM((cols_n, blocks // cols_n, block_len, width_out), bf16),
            pltpu.VMEM((per_core, states, tiles, LANES), f32),
            dma((pieces,)), dma((chunks,)), dma((cols_n,)), dma((cols_n,)),
            dma((chunks, group_n)), dma((chunks,)), dma((blocks,)),
            dma((cols_n, blocks // cols_n)), dma((8,)),
        ],
        compiler_params=pltpu.CompilerParams(
            vmem_limit_bytes=VMEM_LIMIT, collective_id=0, has_side_effects=True
        ),
        name="layer",
    )(tokens, norm_gain[None], w_in, w_bc.T, rate_row, rate_col, skip_gain[None], w_out)
    return out


LANE_PAIR = 2 * LANES
SUBLANES = 8


def grouped_kernel(
    states, rows_n, cols_n, chunks, per_core,
    tok_ref, gain_in, win_in, wbc_in, rrate_in, crate_in, skip_in, wout_in,
    out_ref,
    gain_ref, win_ref, wbc_ref, rrate_ref, crate_ref, skip_ref, wout_ref,
    tokv, nown, ncol, tin_a, tin_b, tin_c, table, order_ref, u_ref, b_ref, uown_ref, bown_ref, cown_ref, lag_ref,
    rsend, rrecv, vcol, inject_ref, spread_ref, read_ref, hist, z_ref, gated_ref, stage, state_ref,
    own_send_sem, next_send_sem, own_sem, early_sem, relay_sem, csend_sem, crecv_sem, rsend_sem, rrecv_sem,
    osend_sem, orecv_sem, fetch_sem, ready_sem,
):
    height, columns, width = tok_ref.shape
    inner = wout_ref.shape[0]
    tiles = inner // LANES
    pairs = inner // LANE_PAIR
    quarter = rows_n // 4
    total = height * cols_n
    chunk_rows = total // chunks
    local_chunks = chunks // cols_n
    lines = quarter * cols_n
    rows = chunk_rows // lines
    run = LANE_PAIR // states
    parts = 1
    share = inner // parts
    r, c = lax.axis_index("rows"), lax.axis_index("cols")

    groups = ((0, quarter), (quarter, quarter), (2 * quarter, 2 * quarter))
    inside = (r < quarter, (r >= quarter) & (r < 2 * quarter), r >= 2 * quarter)
    tins = (tin_a, tin_b, tin_c)
    early = (0, quarter, 2 * quarter)
    line = r % quarter * cols_n + c

    def half_of(q):
        return (q + 1) % 2

    def chip_of(group, q, p):
        chip = groups[group][0] + p // cols_n
        return chip + half_of(q) * quarter if group == 2 else chip

    def slot(group, q):
        return q // 2 if group == 2 else q

    head, rest = pl.ds(0, chunk_rows), pl.ds(chunk_rows, height - chunk_rows)
    fetches = [
        pltpu.make_async_copy(src, dst, fetch_sem.at[k])
        for k, (src, dst) in enumerate((
            (tok_ref.at[head], tokv.at[head]), (gain_in, gain_ref), (tok_ref.at[rest], tokv.at[rest]),
            (rrate_in, rrate_ref), (wbc_in, wbc_ref), (win_in, win_ref),
            (crate_in, crate_ref), (skip_in, skip_ref), (wout_in, wout_ref),
        ))
    ]
    for fetch in fetches:
        fetch.start()

    barrier = pltpu.get_barrier_semaphore()

    def greet(chip, core):
        pl.semaphore_signal(barrier, inc=1, device_id={"rows": chip, "cols": core}, device_id_type=MESH)

    for group, (first, chips) in enumerate(groups):
        @pl.when(inside[group])
        def _():
            me = (r - first) * cols_n + c

            def one(k, _):
                @pl.when(k != me)
                def _():
                    greet(first + k // cols_n, k % cols_n)
                return 0

            lax.fori_loop(0, chips * cols_n, one, 0)
            if group == 1:
                for k in range(2):
                    greet(r + (k + 1) * quarter, c)

                def back(k, _):
                    greet(k // cols_n, k % cols_n)
                    return 0

                lax.fori_loop(0, lines, back, 0)

    def normalise_part(part):
        first = part * chunk_rows
        flat = normalise(tokv[first : first + chunk_rows].astype(jnp.float32).reshape(-1, width), gain_ref[...])
        flat = flat.astype(jnp.float32)
        for t in range(width // LANES):
            order_ref[t, first * columns : (first + chunk_rows) * columns] = flat[:, t * LANES : (t + 1) * LANES]
        for w in range(columns):
            nown[w, first : first + chunk_rows] = jnp.concatenate([
                order_ref[t, pl.ds(first * columns + w, chunk_rows, stride=columns), :] for t in range(width // LANES)
            ], axis=1).astype(jnp.bfloat16)

    for fetch in fetches[:2]:
        fetch.wait()
    normalise_part(0)

    for group, (first, chips) in enumerate(groups):
        @pl.when(inside[group])
        def _():
            pl.semaphore_wait(barrier, chips * cols_n - 1 + (lines, 0, 1)[group])
            if group == 2:
                pl.semaphore_signal(
                    ready_sem, inc=1, device_id={"rows": first - quarter + (r - first) % quarter}, device_id_type=MESH
                )

    def token_copy(group, n):
        part, p = n // lines, (n + line) % lines
        q = c * local_chunks + part
        chip, core = chip_of(group, q, p), p % cols_n
        src = nown.at[:, pl.ds(pl.multiple_of(part * chunk_rows + p * rows, rows), rows)]
        dst = tins[group].at[slot(group, q), early[group] + r - groups[group][0]]
        remote = pltpu.make_async_remote_copy(
            src_ref=src, dst_ref=dst, send_sem=own_send_sem.at[0], recv_sem=own_sem.at[q],
            device_id={"rows": chip, "cols": core}, device_id_type=MESH,
        )
        away = (chip != r) | (core != c)
        return away, remote, lambda: pltpu.make_async_copy(src, dst, own_sem.at[q])

    def send_own(low, high):
        for group in range(3):
            @pl.when(inside[group])
            def _():
                def one(n, _):
                    away, remote, local = token_copy(group, n)

                    @pl.when(away)
                    def _():
                        remote.start()

                    @pl.when(jnp.logical_not(away))
                    def _():
                        local().start()
                    return 0

                lax.fori_loop(low * lines, high * lines, one, 0)

    def next_copy(part, p):
        p = (p + line) % lines
        return pltpu.make_async_remote_copy(
            src_ref=nown.at[:, pl.ds(pl.multiple_of(part * chunk_rows + p * rows, rows), rows)],
            dst_ref=tin_b.at[part, r], send_sem=next_send_sem.at[0], recv_sem=early_sem.at[part],
            device_id={"rows": quarter + p // cols_n, "cols": p % cols_n}, device_id_type=MESH,
        )

    def send_first(part):
        @pl.when(c == 0)
        def _():
            send_own(part, part + 1)

        @pl.when(inside[0] & (c == 0))
        def _():
            def one(p, _):
                next_copy(part, p).start()
                return 0

            lax.fori_loop(0, lines, one, 0)

    direct = 2
    send_first(0)
    fetches[2].wait()
    for part in range(1, local_chunks):
        normalise_part(part)

    def column_copy(step):
        other = (c + step) % cols_n
        return pltpu.make_async_remote_copy(
            src_ref=nown.at[pl.ds(other * per_core, per_core)], dst_ref=ncol.at[c],
            send_sem=csend_sem.at[step], recv_sem=crecv_sem.at[step],
            device_id={"cols": other}, device_id_type=MESH,
        )

    for step in range(1, cols_n):
        column_copy(step).start()

    def drain_own(group):
        count = local_chunks * (lines - 1) if group < 2 else local_chunks * lines - local_chunks // 2
        sent = nown.at[:, pl.ds(0, count * rows)]
        pltpu.make_async_copy(sent, sent, own_send_sem.at[0]).wait()

    def own_wait(group, q):
        part = tins[group].at[slot(group, q), pl.ds(early[group], groups[group][1])]
        pltpu.make_async_copy(part, part, own_sem.at[q]).wait()

    def early_wait(group, q):
        part = tins[group].at[slot(group, q), pl.ds(0, early[group])]
        pltpu.make_async_copy(part, part, early_sem.at[q]).wait()

    def relay_copy(group, q, which):
        if group == 0:
            src, dst, chip = tin_a.at[q], tin_b.at[q, pl.ds(0, quarter)], r + quarter
        else:
            src = tin_b.at[q, pl.ds(which * quarter, quarter)]
            dst = tin_c.at[q // 2, pl.ds(which * quarter, quarter)]
            chip = r + quarter + half_of(q) * quarter
        return pltpu.make_async_remote_copy(
            src_ref=src, dst_ref=dst, send_sem=relay_sem.at[q, which], recv_sem=early_sem.at[q],
            device_id={"rows": chip}, device_id_type=MESH,
        )

    def relay_own(group, q):
        own_wait(group, q)
        relay_copy(group, q, 1).start()

    def relay_early(group, q):
        early_wait(group, q)
        relay_copy(group, q, 0).start()

    def gate_part(core, normed_of):
        for w in range(per_core):
            normed = normed_of(w)
            base = pl.multiple_of(w * total + core * height, height)
            inject = transposed_dot(normed, wbc_ref[2 * states : 3 * states])
            inject = inject.astype(jnp.bfloat16).astype(jnp.float32)
            for n in range(states):
                inject_ref[pl.ds(base * states + n, height, stride=states), :] = jnp.broadcast_to(
                    inject[:, n : n + 1], (height, LANES)
                )
            read = transposed_dot(normed, spread_ref[...])
            owner = lax.broadcasted_iota(jnp.int32, read.shape, 1) // states
            here = lax.broadcasted_iota(jnp.int32, read.shape, 0) % run
            read_ref[pl.ds(base, height), :] = jnp.where(owner == here, read, 0.0).astype(jnp.bfloat16)
            for k in range(0, inner, LANE_PAIR):
                z_ref[pl.ds(base, height), k : k + LANE_PAIR] = jnp.dot(
                    normed, win_ref[:, inner + k : inner + k + LANE_PAIR],
                    preferred_element_type=jnp.float32,
                ).astype(jnp.bfloat16)

    for fetch in fetches[3:]:
        fetch.wait()

    for group, (first, chips) in enumerate(groups):
        @pl.when(inside[group])
        def _():
            def fill(d, _):
                for k in range(pairs):
                    rate = rrate_ref[:, k * LANE_PAIR : (k + 1) * LANE_PAIR]
                    table[k, d] = jnp.exp(-rate * d.astype(jnp.float32)).astype(jnp.bfloat16)
                return 0

            lax.fori_loop(0, (early[group] + chips) * columns, fill, 0)

    for i in range(run):
        spread_ref[i * states : (i + 1) * states] = wbc_ref[3 * states : 4 * states]
    crate_ref[...] = jnp.exp(-crate_ref[...])
    state_ref[...] = jnp.zeros(state_ref.shape, jnp.float32)
    gated_ref[...] = jnp.zeros(gated_ref.shape, jnp.bfloat16)
    send_first(1)
    gate_part(c, lambda w: nown[c * per_core + w])

    @pl.when(c == 0)
    def _():
        send_own(direct, local_chunks)

    @pl.when(inside[1])
    def _():
        pl.semaphore_wait(ready_sem, 2)
        relay_own(1, 0)

    for step in range(1, cols_n):
        column_copy(step).wait_recv()
        source = (c + cols_n - step) % cols_n
        gate_part(source, lambda w: ncol[source, w])

    @pl.when(c > 0)
    def _():
        send_own(0, local_chunks)

    @pl.when(inside[0])
    def _():
        def one(q, _):
            relay_own(0, q)
            return 0

        for q in range(direct):
            own_wait(0, q)
        lax.fori_loop(direct, local_chunks, one, 0)

    @pl.when(inside[1])
    def _():
        relay_early(1, 0)
        relay_own(1, 1)

    def result_copy(group, q, part, k):
        first, chips = groups[group]
        g = ((r - first) * cols_n + c + k) % (chips * cols_n)
        some = pl.ds(pl.multiple_of(part * share, share), share)
        src, dst = rsend.at[slot(group, q), g, :, :, some], rrecv.at[q, line, :, :, some]
        remote = pltpu.make_async_remote_copy(
            src_ref=src, dst_ref=dst, send_sem=rsend_sem.at[slot(group, q)], recv_sem=rrecv_sem.at[q],
            device_id={"rows": first + g // cols_n, "cols": g % cols_n}, device_id_type=MESH,
        )
        return remote, lambda: pltpu.make_async_copy(src, dst, rrecv_sem.at[q])

    def rounded(value):
        return value.astype(jnp.bfloat16).astype(jnp.float32)

    def project_in(normed, k):
        return rounded(jnp.dot(
            normed, win_ref[:, k * LANE_PAIR : (k + 1) * LANE_PAIR], preferred_element_type=jnp.float32
        ))

    def own_part(group, q):
        chips = groups[group][1]
        before = early[group]
        count = chips * columns * rows
        ready = slot(group, q) if group == 2 else 0
        if group == 2:
            own_wait(group, q)
        normed = tins[group][slot(group, q), before : before + chips].reshape(count, width)
        bown_ref[ready, :count] = rounded(transposed_dot(normed, wbc_ref[:states]))
        cown_ref[ready, :count] = rounded(transposed_dot(normed, wbc_ref[states : 2 * states]))
        for k in range(pairs):
            uown_ref[ready, k, :count] = project_in(normed, k)

    def row_chunk(group, q):
        chips = groups[group][1]
        before = early[group]
        at = slot(group, q)
        tin = tins[group]
        out_cols, pre_cols = chips * columns, before * columns
        all_cols = out_cols + pre_cols
        if group < 2:
            own_part(group, q)
        else:
            early_wait(group, q)
        ready = at if group == 2 else 0
        if before:
            normed = tin[at, :before].reshape(pre_cols * rows, width)
            b_ref[: pre_cols * rows] = rounded(transposed_dot(normed, wbc_ref[:states]))
            for k in range(pairs):
                u_ref[k, : pre_cols * rows] = project_in(normed, k)
        b_ref[pre_cols * rows : all_cols * rows] = bown_ref[ready, : out_cols * rows]

        def value_of(k, col):
            if col < pre_cols:
                return u_ref[k, col * rows : (col + 1) * rows]
            return uown_ref[ready, k, (col - pre_cols) * rows : (col - pre_cols + 1) * rows]

        def span(d):
            low = max(0, d - pre_cols)
            return low, out_cols - low, pre_cols + low - d

        for d in range(1, all_cols):
            low, count, source = span(d)
            lag_ref[d, : count * rows] = (
                cown_ref[ready, low * rows : out_cols * rows] * b_ref[source * rows : (source + count) * rows]
            ).astype(jnp.bfloat16)

        here = jnp.sum(
            cown_ref[ready, : out_cols * rows] * b_ref[pre_cols * rows : all_cols * rows], axis=1, keepdims=True
        )

        def one_pair(k):
            skip = skip_ref[k]
            sums = [
                (skip + here[o * rows : (o + 1) * rows]) * value_of(k, pre_cols + o) for o in range(out_cols)
            ]
            for d in range(1, all_cols):
                low, count, source = span(d)
                weight = jnp.dot(lag_ref[d, : count * rows], table[k, d], preferred_element_type=jnp.float32)
                for i in range(count):
                    sums[low + i] += weight[i * rows : (i + 1) * rows] * value_of(k, source + i)
            some = pl.ds(pl.multiple_of(k * LANE_PAIR, LANE_PAIR), LANE_PAIR)
            for o in range(out_cols):
                rsend[at, o // per_core, o % per_core, :, some] = sums[o].astype(jnp.bfloat16)

        def one_part(part, _):
            for k in range(pairs // parts):
                one_pair(part * (pairs // parts) + k)
            result_copy(group, q, part, 0)[1]().start()

            def send_result(k, _):
                result_copy(group, q, part, k)[0].start()
                return 0

            lax.fori_loop(1, chips * cols_n, send_result, 0)
            return 0

        lax.fori_loop(0, parts, one_part, 0)

    def out_part(core, i):
        first = pl.multiple_of(i * chunk_rows, chunk_rows)
        return out_ref.at[pl.ds(core * per_core, per_core), pl.ds(first, chunk_rows)]

    def out_copy(q):
        return pltpu.make_async_remote_copy(
            src_ref=stage.at[q], dst_ref=out_part(c, q % local_chunks),
            send_sem=osend_sem.at[q], recv_sem=orecv_sem.at[c, q % local_chunks],
            device_id={"cols": q // local_chunks}, device_id_type=MESH,
        )

    def col_chunk(q):
        pltpu.make_async_copy(rrecv.at[q], rrecv.at[q], rrecv_sem.at[q]).wait()
        for p in range(lines):
            for w in range(per_core):
                value = rrecv[q, p, w].astype(jnp.float32)
                for t in range(tiles):
                    vcol[t, w * chunk_rows + p * rows : w * chunk_rows + (p + 1) * rows] = (
                        value[:, t * LANES : (t + 1) * LANES]
                    )
        project((q + chunks - 1) % chunks)
        halves = range(0, states, SUBLANES)

        def one_run(i):
            for w in range(per_core):
                here = w * chunk_rows + i * run
                patch = pl.multiple_of(w * total + q * chunk_rows + i * run, run)
                decay = [[crate_ref[h : h + SUBLANES, t * LANES : (t + 1) * LANES] for t in range(tiles)] for h in halves]
                state = [[state_ref[w, h : h + SUBLANES, t * LANES : (t + 1) * LANES] for t in range(tiles)] for h in halves]
                for s in range(run):
                    inject = [
                        inject_ref[pl.ds(pl.multiple_of((patch + s) * states + h, SUBLANES), SUBLANES), :] for h in halves
                    ]
                    for t in range(tiles):
                        value = vcol[t, pl.ds(here + s, SUBLANES, stride=0), :]
                        for j in range(len(inject)):
                            state[j][t] = decay[j][t] * state[j][t] + inject[j] * value
                        hist[i * per_core + w, t, s * states : (s + 1) * states, :] = jnp.concatenate(
                            [state[j][t] for j in range(len(inject))], axis=0
                        ).astype(jnp.bfloat16)
                for j, h in enumerate(halves):
                    for t in range(tiles):
                        state_ref[w, h : h + SUBLANES, t * LANES : (t + 1) * LANES] = state[j][t]
                for t in range(tiles):
                    if t % 2 == 0:
                        both_tiles = jnp.concatenate([hist[i * per_core + w, t], hist[i * per_core + w, t + 1]], axis=1)
                        mixed = jnp.dot(
                            read_ref[pl.ds(patch, run), :], both_tiles, preferred_element_type=jnp.float32
                        )
                    gate = z_ref[pl.ds(patch, run), t * LANES : (t + 1) * LANES].astype(jnp.float32)
                    both = mixed[:, t % 2 * LANES : (t % 2 + 1) * LANES] + vcol[t, pl.ds(here, run), :]
                    gated_ref[q % 2, pl.ds(here, run), t * LANES : (t + 1) * LANES] = (
                        both * (gate / (1.0 + jnp.exp(-gate)))
                    ).astype(jnp.bfloat16)

        for i in range(chunk_rows // run):
            one_run(i)

        @pl.when(q > 0)
        def _():
            send_out(q - 1)

    def project(q):
        result = jnp.dot(gated_ref[q % 2], wout_ref[...], preferred_element_type=jnp.float32).astype(jnp.bfloat16)
        stage[q] = result.reshape(per_core, chunk_rows, -1)

    def send_out(q):
        home = q // local_chunks

        @pl.when(home == c)
        def _():
            pltpu.make_async_copy(stage.at[q], out_part(c, q % local_chunks), orecv_sem.at[c, q % local_chunks]).start()

        @pl.when(home != c)
        def _():
            out_copy(q).start()

    def one_chunk(q, _):
        for group in range(3):
            mine = inside[group] & (q < chunks)
            if group == 2:
                mine = mine & (half_of(q) == (r - 2 * quarter) // quarter)

            @pl.when(mine)
            def _():
                row_chunk(group, q)
                if group == 2:
                    @pl.when(q + 2 < chunks)
                    def _():
                        own_part(group, q + 2)

            if group == 0:
                @pl.when(inside[group] & (q + local_chunks < chunks))
                def _():
                    relay_own(group, q + local_chunks)
            if group == 1:
                @pl.when(inside[group] & (q + 1 < chunks))
                def _():
                    relay_early(group, q + 1)

                @pl.when(inside[group] & (q + 2 < chunks))
                def _():
                    relay_own(group, q + 2)

        @pl.when(q >= lag)
        def _():
            col_chunk(q - lag)
        return 0

    @pl.when(inside[2])
    def _():
        own_part(2, 1 - (r - 2 * quarter) // quarter)

    lag = 3
    lax.fori_loop(0, chunks + lag, one_chunk, 0)
    project(chunks - 1)
    send_out(chunks - 1)

    for group, (first, chips) in enumerate(groups):
        @pl.when(inside[group])
        def _():
            drain_own(group)

            def drain_chunk(q, _):
                relay_copy(group, q, 1).wait_send()
                if group == 1:
                    relay_copy(group, q, 0).wait_send()
                return 0

            if group == 0:
                @pl.when(c == 0)
                def _():
                    sent = nown.at[:, pl.ds(0, direct * lines * rows)]
                    pltpu.make_async_copy(sent, sent, next_send_sem.at[0]).wait()
            if group < 2:
                lax.fori_loop((direct, 0)[group], chunks, drain_chunk, 0)
            for at in range(chunks // (1 + group // 2)):
                sent = rsend.at[at, pl.ds(0, chips * cols_n - 1)]
                pltpu.make_async_copy(sent, sent, rsend_sem.at[at]).wait()

    for step in range(1, cols_n):
        column_copy(step).wait_send()

    def drain_out(q, _):
        @pl.when(q // local_chunks != c)
        def _():
            out_copy(q).wait_send()
        return 0

    lax.fori_loop(0, chunks, drain_out, 0)
    for source in range(cols_n):
        for i in range(local_chunks):
            part = out_part(source, i)
            pltpu.make_async_copy(part, part, orecv_sem.at[source, i]).wait()


def per_device_grouped(chunks, tokens, norm_gain, w_in, w_bc, rate_row, rate_col, skip_gain, w_out):
    inner, width_out = w_out.shape
    states = rate_row.shape[0]
    height, columns, width = tokens.shape
    rows_n, cols_n = lax.axis_size("rows"), lax.axis_size("cols")
    quarter = rows_n // 4
    per_core = columns // cols_n
    total = height * cols_n
    chunk_rows = total // chunks
    lines = quarter * cols_n
    rows = chunk_rows // lines
    tiles = inner // LANES
    pairs = inner // LANE_PAIR
    patches = total * per_core
    local_chunks = chunks // cols_n
    lags = rows_n * columns
    held = lags * rows
    outs = 2 * quarter * columns * rows
    f32, bf16 = jnp.float32, jnp.bfloat16
    dma = pltpu.SemaphoreType.DMA
    out = pl.pallas_call(
        functools.partial(grouped_kernel, states, rows_n, cols_n, chunks, per_core),
        in_specs=[pl.BlockSpec(memory_space=pl.ANY)] * 8,
        out_specs=pl.BlockSpec(memory_space=pl.ANY),
        out_shape=pltpu.VMEM((columns, height, width_out), bf16),
        scratch_shapes=[
            pltpu.VMEM((1, width), f32),
            pltpu.VMEM(w_in.shape, bf16),
            pltpu.VMEM(w_bc.shape[::-1], bf16),
            pltpu.VMEM(rate_row.shape, f32),
            pltpu.VMEM(rate_col.shape, f32),
            pltpu.VMEM((pairs, 1, LANE_PAIR), f32),
            pltpu.VMEM(w_out.shape, bf16),
            pltpu.VMEM((height, columns, width), bf16),
            pltpu.VMEM((columns, height, width), bf16),
            pltpu.VMEM((cols_n, per_core, height, width), bf16),
            pltpu.VMEM((chunks, quarter, columns, rows, width), bf16),
            pltpu.VMEM((chunks, 2 * quarter, columns, rows, width), bf16),
            pltpu.VMEM((chunks // 2, 4 * quarter, columns, rows, width), bf16),
            pltpu.VMEM((pairs, lags, states, LANE_PAIR), bf16),
            pltpu.VMEM((width // LANES, height * columns, LANES), f32),
            pltpu.VMEM((pairs, held, LANE_PAIR), f32),
            pltpu.VMEM((held, states), f32),
            pltpu.VMEM((chunks // 2, pairs, outs, LANE_PAIR), f32),
            pltpu.VMEM((chunks // 2, outs, states), f32),
            pltpu.VMEM((chunks // 2, outs, states), f32),
            pltpu.VMEM((lags, outs, states), bf16),
            pltpu.VMEM((chunks, 2 * lines, per_core, rows, inner), bf16),
            pltpu.VMEM((chunks, lines, per_core, rows, inner), bf16),
            pltpu.VMEM((tiles, per_core * chunk_rows + SUBLANES, LANES), f32),
            pltpu.VMEM((patches * states, LANES), f32),
            pltpu.VMEM((LANE_PAIR, width), bf16),
            pltpu.VMEM((patches, LANE_PAIR), bf16),
            pltpu.VMEM((per_core * chunk_rows * states // LANE_PAIR, tiles, LANE_PAIR, LANES), bf16),
            pltpu.VMEM((patches, inner), bf16),
            pltpu.VMEM((2, per_core * chunk_rows, inner), bf16),
            pltpu.VMEM((chunks, per_core, chunk_rows, width_out), bf16),
            pltpu.VMEM((per_core, states, inner), f32),
            dma((1,)), dma((1,)), dma((chunks,)), dma((chunks,)), dma((chunks, 2)),
            dma((cols_n,)), dma((cols_n,)),
            dma((chunks,)), dma((chunks,)), dma((chunks,)),
            dma((cols_n, local_chunks)), dma((9,)), pltpu.SemaphoreType.REGULAR,
        ],
        compiler_params=pltpu.CompilerParams(
            vmem_limit_bytes=VMEM_LIMIT, collective_id=0, has_side_effects=True
        ),
        name="layer",
    )(
        tokens, norm_gain[None], w_in, w_bc.T, rate_row, rate_col,
        skip_gain.reshape(pairs, 1, LANE_PAIR), w_out,
    )
    return out.transpose(1, 0, 2)


def chunk_count(tokens, rate_row, inner):
    height, columns, _ = tokens.shape
    states = rate_row.shape[0]
    rows_n, cols_n = lax.axis_size("rows"), lax.axis_size("cols")
    total = height * cols_n
    if rows_n % 4 or columns % cols_n or inner % LANE_PAIR or states % SUBLANES or LANE_PAIR % states:
        return 0
    step = rows_n // 4 * cols_n * SUBLANES
    run = LANE_PAIR // states
    if total % step or step % run or total // step % (2 * cols_n):
        return 0
    return total // step


def per_device(tokens, norm_gain, w_in, w_bc, rate_row, rate_col, skip_gain, w_out):
    args = (tokens, norm_gain, w_in, w_bc, rate_row, rate_col, skip_gain, w_out)
    chunks = chunk_count(tokens, rate_row, w_out.shape[0])
    if chunks:
        return per_device_grouped(chunks, *args)
    return per_device_uniform(*args)


def solution(mesh):
    placed = (P(("slides", "cols"), "rows", None), P(), P(), P(), P(), P(), P(), P())
    return jax.shard_map(
        per_device,
        mesh=mesh,
        in_specs=placed,
        out_specs=P(("slides", "cols"), "rows", None),
        check_vma=False,
    )
```

```python
import functools

import jax
import jax.numpy as jnp
from jax import lax
from jax.experimental import pallas as pl
from jax.experimental.pallas import tpu as pltpu
from jax.sharding import PartitionSpec as P

LANES = 128
VMEM_LIMIT = 60 * 1024 * 1024
MESH = pl.DeviceIdType.MESH


def normalise(tokens, gain):
    as_float = tokens.astype(jnp.float32)
    scale_now = lax.rsqrt(jnp.mean(as_float * as_float, axis=-1, keepdims=True) + 1e-05)
    return (as_float * scale_now * gain).astype(jnp.bfloat16)


def transposed_dot(a, b):
    return lax.dot_general(a, b, (((1,), (1,)), ((), ())), preferred_element_type=jnp.float32)


def spread_channels(ref, value, tiles):
    rows = value.shape[0]
    for t in range(tiles):
        ref[pl.ds(t, rows, stride=tiles), :] = value[:, t * LANES : (t + 1) * LANES]


def spread_vectors(ref, value, first, states, base):
    rows = value.shape[0]
    for n in range(states):
        ref[n, pl.ds(base, rows), :] = jnp.broadcast_to(
            value[:, first + n : first + n + 1], (rows, LANES)
        )


def scan_step(carried, decay, value, inject_ref, readout_ref, patch, start, tiles):
    new = []
    totals = [start, None]
    for n, state in enumerate(carried):
        inject = inject_ref[n, pl.ds(patch, tiles, stride=0), :]
        readout = readout_ref[n, pl.ds(patch, tiles, stride=0), :]
        state = decay[n] * state + inject * value
        term = readout * state
        totals[n % 2] = term if totals[n % 2] is None else totals[n % 2] + term
        new.append(state)
    return tuple(new), totals[0] + totals[1]


def layer_kernel(
    states, rows_n, cols_n, share, per_core,
    tok_ref, gain_in, win_in, wbc_in, rrate_in, crate_in, skip_in, wout_in,
    out_ref,
    gain_ref, win_ref, wbc_ref, rrate_ref, crate_ref, skip_ref, wout_ref, tcol, tin, rsend, rrecv, u_ref, rb_ref, rc_ref, cb_ref, cc_ref, z_ref, y_ref, gated_ref,
    rdecay, cdecay, skip_tile, stage, land, state_ref,
    tsend_sem, tin_sem, csend_sem, crecv_sem, rsend_sem, rrecv_sem, osend_sem, orecv_sem, fetch_sem,
):
    group_n = rows_n * cols_n
    pieces = tok_ref.shape[0] // share
    chunks = tin.shape[0]
    columns, width = tok_ref.shape[1:]
    inner = wout_ref.shape[0]
    tiles = inner // LANES
    piece_len = share * per_core
    chunk_len = group_n * piece_len
    blocks = stage.shape[0]
    blocks_home = blocks // cols_n
    block_len = stage.shape[1]
    r, c = lax.axis_index("rows"), lax.axis_index("cols")
    me = r * cols_n + c

    def spot(g):
        return {"rows": g // cols_n, "cols": g % cols_n}

    barrier = pltpu.get_barrier_semaphore()

    def greet(g, _):
        @pl.when(g != me)
        def _():
            pl.semaphore_signal(barrier, inc=1, device_id=spot(g), device_id_type=MESH)
        return 0

    lax.fori_loop(0, group_n, greet, 0)
    fetches = [
        pltpu.make_async_copy(src, dst, fetch_sem.at[k])
        for k, (src, dst) in enumerate((
            (rrate_in, rrate_ref), (crate_in, crate_ref), (skip_in, skip_ref), (gain_in, gain_ref),
            (wbc_in, wbc_ref), (tok_ref, tcol.at[c]), (win_in, win_ref), (wout_in, wout_ref),
        ))
    ]
    for fetch in fetches:
        fetch.start()
    pl.semaphore_wait(barrier, group_n - 1)

    local_chunks = max(1, chunks // cols_n)
    per_chunk = pieces // local_chunks

    def piece_of(k):
        piece = k // per_chunk * per_chunk + (k % per_chunk + me) % per_chunk
        place = c * pieces + piece
        return piece, place // group_n, place % group_n

    def token_copy(k):
        piece, q, g = piece_of(k)
        return g, pltpu.make_async_remote_copy(
            src_ref=tok_ref.at[pl.ds(piece * share, share)], dst_ref=tin.at[q, r],
            send_sem=tsend_sem.at[piece], recv_sem=tin_sem.at[q],
            device_id=spot(g), device_id_type=MESH,
        )

    def send_tokens(k, _):
        piece, q, g = piece_of(k)

        @pl.when(g == me)
        def _():
            pltpu.make_async_copy(tok_ref.at[pl.ds(piece * share, share)], tin.at[q, r], tin_sem.at[q]).start()

        @pl.when(g != me)
        def _():
            token_copy(k)[1].start()
        return 0

    lax.fori_loop(0, pieces, send_tokens, 0)

    def column_copy(step):
        other = (c + step) % cols_n
        return pltpu.make_async_remote_copy(
            src_ref=tok_ref, dst_ref=tcol.at[c],
            send_sem=csend_sem.at[step], recv_sem=crecv_sem.at[step],
            device_id={"cols": other}, device_id_type=MESH,
        )

    for step in range(1, cols_n):
        column_copy(step).start()

    def gate_part(tokens, core):
        tokens = tokens.astype(jnp.float32)
        own = tokens[:, :per_core]
        for k in range(1, cols_n):
            own = jnp.where(c == k, tokens[:, k * per_core : (k + 1) * per_core], own)
        normed = normalise(own.reshape(-1, width), gain_ref[...])
        count = normed.shape[0]
        base = pl.multiple_of(core * count, count)
        mixers = transposed_dot(normed, wbc_ref[...])
        mixers = mixers.astype(jnp.bfloat16).astype(jnp.float32)
        spread_vectors(cb_ref, mixers, 2 * states, states, base)
        spread_vectors(cc_ref, mixers, 3 * states, states, base)
        for k in range(0, inner, 2 * LANES):
            z_ref[pl.ds(base, count), k : k + 2 * LANES] = jnp.dot(
                normed, win_ref[:, inner + k : inner + k + 2 * LANES],
                preferred_element_type=jnp.float32,
            ).astype(jnp.bfloat16)

    for fetch in fetches:
        fetch.wait()
    spread_channels(rdecay, jnp.exp(-rrate_ref[...]), tiles)
    spread_channels(cdecay, jnp.exp(-crate_ref[...]), tiles)
    spread_channels(skip_tile, skip_ref[...], tiles)
    gate_part(tcol[c], c)

    zero = jnp.zeros((tiles, LANES), jnp.float32)
    lanes = 2 if share % 2 == 0 else 1

    def result_copy(q, k):
        g = (me + k) % group_n
        return pltpu.make_async_remote_copy(
            src_ref=rsend.at[q, pl.ds(g * piece_len, piece_len)],
            dst_ref=rrecv.at[q, pl.ds(me * piece_len, piece_len)],
            send_sem=rsend_sem.at[q, k], recv_sem=rrecv_sem.at[q],
            device_id=spot(g), device_id_type=MESH,
        )

    def row_chunk(q, _):
        pltpu.make_async_copy(tin.at[q], tin.at[q], tin_sem.at[q]).wait()
        normed = normalise(tin[q].astype(jnp.float32).reshape(chunk_len, width), gain_ref[...])
        mixers = transposed_dot(normed, wbc_ref[...])
        mixers = mixers.astype(jnp.bfloat16).astype(jnp.float32)
        spread_vectors(rb_ref, mixers, 0, states, 0)
        spread_vectors(rc_ref, mixers, states, states, 0)
        for k in range(0, tiles, 2):
            part = jnp.dot(normed, win_ref[:, k * LANES : (k + 2) * LANES],
                           preferred_element_type=jnp.float32)
            part = part.astype(jnp.bfloat16).astype(jnp.float32)
            for h in range(2):
                u_ref[pl.ds(k + h, chunk_len, stride=tiles), :] = part[:, h * LANES : (h + 1) * LANES]
        decay = [rdecay[n * tiles : (n + 1) * tiles, :] for n in range(states)]
        skip = skip_tile[...]

        def one_group(first, _):
            def one_step(j, carry):
                carry = list(carry)
                for w in range(columns):
                    for b in range(lanes):
                        row = first * lanes + b
                        patch = (j * share + row) * columns + w
                        owner = j * cols_n + w // per_core
                        value = u_ref[pl.ds(pl.multiple_of(patch * tiles, tiles), tiles), :]
                        carry[b], total = scan_step(carry[b], decay, value, rb_ref, rc_ref,
                                                    patch, skip * value, tiles)
                        rsend[q, (owner * share + row) * per_core + w % per_core] = total.astype(jnp.bfloat16)
                return tuple(carry)

            lax.fori_loop(0, rows_n, one_step, tuple((zero,) * states for _ in range(lanes)))
            return 0

        lax.fori_loop(0, share // lanes, one_group, 0)

        def send_result(k, _):
            result_copy(q, k).start()
            return 0

        pltpu.make_async_copy(
            rsend.at[q, pl.ds(me * piece_len, piece_len)],
            rrecv.at[q, pl.ds(me * piece_len, piece_len)], rrecv_sem.at[q],
        ).start()
        lax.fori_loop(1, group_n, send_result, 0)
        return 0

    lax.fori_loop(0, chunks, row_chunk, 0)

    for step in range(1, cols_n):
        column_copy(step).wait_recv()
        source = (c + cols_n - step) % cols_n
        gate_part(tcol[source], source)

    for g in range(per_core):
        for n in range(states):
            state_ref[g, n] = zero

    def out_copy(o):
        return pltpu.make_async_remote_copy(
            src_ref=stage.at[o], dst_ref=land.at[c, o % blocks_home],
            send_sem=osend_sem.at[o], recv_sem=orecv_sem.at[c, o % blocks_home],
            device_id={"cols": o // blocks_home}, device_id_type=MESH,
        )

    def col_chunk(q, _):
        pltpu.make_async_copy(rrecv.at[q], rrecv.at[q], rrecv_sem.at[q]).wait()
        decay = [cdecay[n * tiles : (n + 1) * tiles, :] for n in range(states)]
        base = q * chunk_len

        def one_step(s, carry):
            result = []
            for g in range(per_core):
                patch = s * per_core + g
                value = rrecv[q, patch].astype(jnp.float32)
                state, total = scan_step(carry[g], decay, value, cb_ref, cc_ref,
                                         base + patch, value, tiles)
                y_ref[pl.ds(pl.multiple_of(patch * tiles, tiles), tiles), :] = total
                result.append(state)
            return tuple(result)

        carry = tuple(tuple(state_ref[g, n] for n in range(states)) for g in range(per_core))
        carry = lax.fori_loop(0, chunk_len // per_core, one_step, carry)
        for g in range(per_core):
            for n in range(states):
                state_ref[g, n] = carry[g][n]
        start = pl.multiple_of(base, chunk_len)
        for t in range(tiles):
            gate = z_ref[pl.ds(start, chunk_len), t * LANES : (t + 1) * LANES].astype(jnp.float32)
            mixed = y_ref[pl.ds(t, chunk_len, stride=tiles), :]
            gated_ref[:, t * LANES : (t + 1) * LANES] = (
                mixed * (gate / (1.0 + jnp.exp(-gate)))
            ).astype(jnp.bfloat16)
        result = jnp.dot(gated_ref[...], wout_ref[...], preferred_element_type=jnp.float32)
        result = result.astype(jnp.bfloat16)
        for k in range(blocks // chunks):
            o = q * (blocks // chunks) + k
            block = result[k * block_len : (k + 1) * block_len]
            stage[o] = block

            @pl.when(o // blocks_home == c)
            def _():
                land[c, o % blocks_home] = block

            @pl.when(o // blocks_home != c)
            def _():
                out_copy(o).start()
        return 0

    lax.fori_loop(0, chunks, col_chunk, 0)

    def drain_tokens(k, _):
        g, copy = token_copy(k)

        @pl.when(g != me)
        def _():
            copy.wait_send()
        return 0

    lax.fori_loop(0, pieces, drain_tokens, 0)
    for step in range(1, cols_n):
        column_copy(step).wait_send()

    def drain_results(q, _):
        def one(k, _):
            result_copy(q, k).wait_send()
            return 0
        return lax.fori_loop(1, group_n, one, 0)

    lax.fori_loop(0, chunks, drain_results, 0)

    def drain_out(o, _):
        @pl.when(o // blocks_home != c)
        def _():
            out_copy(o).wait_send()
        return 0

    lax.fori_loop(0, blocks, drain_out, 0)
    for source in range(cols_n):
        @pl.when(source != c)
        def _():
            for i in range(blocks_home):
                pltpu.make_async_copy(
                    land.at[source, i], land.at[source, i], orecv_sem.at[source, i]
                ).wait()
    for i in range(blocks_home):
        parts = [
            land[s, i].astype(jnp.float32).reshape(block_len // per_core, per_core, -1)
            for s in range(cols_n)
        ]
        rows = block_len // per_core
        out_ref[i * rows : (i + 1) * rows] = jnp.concatenate(parts, axis=1).astype(jnp.bfloat16)


def per_device_uniform(tokens, norm_gain, w_in, w_bc, rate_row, rate_col, skip_gain, w_out):
    inner, width_out = w_out.shape
    states = rate_row.shape[0]
    height, columns, width = tokens.shape
    rows_n, cols_n = lax.axis_size("rows"), lax.axis_size("cols")
    group_n = rows_n * cols_n
    per_core = columns // cols_n
    total = height * cols_n
    share = min(4, total // group_n)
    chunks = total // (group_n * share)
    pieces = height // share
    piece_len = share * per_core
    chunk_len = group_n * piece_len
    tiles = inner // LANES
    blocks = max(chunks, cols_n)
    block_len = total * per_core // blocks
    patches = total * per_core
    f32, bf16 = jnp.float32, jnp.bfloat16
    dma = pltpu.SemaphoreType.DMA
    out = pl.pallas_call(
        functools.partial(layer_kernel, states, rows_n, cols_n, share, per_core),
        in_specs=[pl.BlockSpec(memory_space=pl.ANY)] * 8,
        out_specs=pl.BlockSpec(memory_space=pltpu.VMEM),
        out_shape=jax.ShapeDtypeStruct((height, columns, width_out), bf16),
        scratch_shapes=[
            pltpu.VMEM((1, width), f32),
            pltpu.VMEM(w_in.shape, bf16),
            pltpu.VMEM(w_bc.shape[::-1], bf16),
            pltpu.VMEM(rate_row.shape, f32),
            pltpu.VMEM(rate_col.shape, f32),
            pltpu.VMEM((1, inner), f32),
            pltpu.VMEM(w_out.shape, bf16),
            pltpu.VMEM((cols_n, height, columns, width), bf16),
            pltpu.VMEM((chunks, rows_n, share, columns, width), bf16),
            pltpu.VMEM((chunks, chunk_len, tiles, LANES), bf16),
            pltpu.VMEM((chunks, chunk_len, tiles, LANES), bf16),
            pltpu.VMEM((chunk_len * tiles, LANES), f32),
            pltpu.VMEM((states, chunk_len + 8, LANES), f32),
            pltpu.VMEM((states, chunk_len + 8, LANES), f32),
            pltpu.VMEM((states, patches + 8, LANES), f32),
            pltpu.VMEM((states, patches + 8, LANES), f32),
            pltpu.VMEM((patches, inner), bf16),
            pltpu.VMEM((chunk_len * tiles, LANES), f32),
            pltpu.VMEM((chunk_len, inner), bf16),
            pltpu.VMEM((states * tiles, LANES), f32),
            pltpu.VMEM((states * tiles, LANES), f32),
            pltpu.VMEM((tiles, LANES), f32),
            pltpu.VMEM((blocks, block_len, width_out), bf16),
            pltpu.VMEM((cols_n, blocks // cols_n, block_len, width_out), bf16),
            pltpu.VMEM((per_core, states, tiles, LANES), f32),
            dma((pieces,)), dma((chunks,)), dma((cols_n,)), dma((cols_n,)),
            dma((chunks, group_n)), dma((chunks,)), dma((blocks,)),
            dma((cols_n, blocks // cols_n)), dma((8,)),
        ],
        compiler_params=pltpu.CompilerParams(
            vmem_limit_bytes=VMEM_LIMIT, collective_id=0, has_side_effects=True
        ),
        name="layer",
    )(tokens, norm_gain[None], w_in, w_bc.T, rate_row, rate_col, skip_gain[None], w_out)
    return out


LANE_PAIR = 2 * LANES
SUBLANES = 8


def grouped_kernel(
    states, rows_n, cols_n, chunks, per_core,
    tok_ref, gain_in, win_in, wbc_in, rrate_in, crate_in, skip_in, wout_in,
    out_ref,
    gain_ref, win_ref, wbc_ref, rrate_ref, crate_ref, skip_ref, wout_ref,
    tokv, nown, ncol, tin_a, tin_b, tin_c, table, order_ref, u_ref, b_ref, uown_ref, bown_ref, cown_ref, lag_ref,
    rsend, rrecv, vcol, inject_ref, spread_ref, read_ref, hist, z_ref, gated_ref, stage, state_ref,
    own_send_sem, next_send_sem, own_sem, early_sem, relay_sem, csend_sem, crecv_sem, rsend_sem, rrecv_sem,
    osend_sem, orecv_sem, fetch_sem, ready_sem,
):
    height, columns, width = tok_ref.shape
    inner = wout_ref.shape[0]
    tiles = inner // LANES
    pairs = inner // LANE_PAIR
    quarter = rows_n // 4
    total = height * cols_n
    chunk_rows = total // chunks
    local_chunks = chunks // cols_n
    lines = quarter * cols_n
    rows = chunk_rows // lines
    run = LANE_PAIR // states
    parts = 1
    share = inner // parts
    r, c = lax.axis_index("rows"), lax.axis_index("cols")

    groups = ((0, quarter), (quarter, quarter), (2 * quarter, 2 * quarter))
    inside = (r < quarter, (r >= quarter) & (r < 2 * quarter), r >= 2 * quarter)
    tins = (tin_a, tin_b, tin_c)
    early = (0, quarter, 2 * quarter)
    line = r % quarter * cols_n + c

    def half_of(q):
        return (q + 1) % 2

    def chip_of(group, q, p):
        chip = groups[group][0] + p // cols_n
        return chip + half_of(q) * quarter if group == 2 else chip

    def slot(group, q):
        return q // 2 if group == 2 else q

    head, rest = pl.ds(0, chunk_rows), pl.ds(chunk_rows, height - chunk_rows)
    fetches = [
        pltpu.make_async_copy(src, dst, fetch_sem.at[k])
        for k, (src, dst) in enumerate((
            (tok_ref.at[head], tokv.at[head]), (gain_in, gain_ref), (tok_ref.at[rest], tokv.at[rest]),
            (rrate_in, rrate_ref), (wbc_in, wbc_ref), (win_in, win_ref),
            (crate_in, crate_ref), (skip_in, skip_ref), (wout_in, wout_ref),
        ))
    ]
    for fetch in fetches:
        fetch.start()

    barrier = pltpu.get_barrier_semaphore()

    def greet(chip, core):
        pl.semaphore_signal(barrier, inc=1, device_id={"rows": chip, "cols": core}, device_id_type=MESH)

    for group, (first, chips) in enumerate(groups):
        @pl.when(inside[group])
        def _():
            me = (r - first) * cols_n + c

            def one(k, _):
                @pl.when(k != me)
                def _():
                    greet(first + k // cols_n, k % cols_n)
                return 0

            lax.fori_loop(0, chips * cols_n, one, 0)
            if group == 1:
                for k in range(2):
                    greet(r + (k + 1) * quarter, c)

                def back(k, _):
                    greet(k // cols_n, k % cols_n)
                    return 0

                lax.fori_loop(0, lines, back, 0)

    def normalise_part(part):
        first = part * chunk_rows
        flat = normalise(tokv[first : first + chunk_rows].astype(jnp.float32).reshape(-1, width), gain_ref[...])
        flat = flat.astype(jnp.float32)
        for t in range(width // LANES):
            order_ref[t, first * columns : (first + chunk_rows) * columns] = flat[:, t * LANES : (t + 1) * LANES]
        for w in range(columns):
            nown[w, first : first + chunk_rows] = jnp.concatenate([
                order_ref[t, pl.ds(first * columns + w, chunk_rows, stride=columns), :] for t in range(width // LANES)
            ], axis=1).astype(jnp.bfloat16)

    for fetch in fetches[:2]:
        fetch.wait()
    normalise_part(0)

    for group, (first, chips) in enumerate(groups):
        @pl.when(inside[group])
        def _():
            pl.semaphore_wait(barrier, chips * cols_n - 1 + (lines, 0, 1)[group])
            if group == 2:
                pl.semaphore_signal(
                    ready_sem, inc=1, device_id={"rows": first - quarter + (r - first) % quarter}, device_id_type=MESH
                )

    def token_copy(group, n):
        part, p = n // lines, (n + line) % lines
        q = c * local_chunks + part
        chip, core = chip_of(group, q, p), p % cols_n
        src = nown.at[:, pl.ds(pl.multiple_of(part * chunk_rows + p * rows, rows), rows)]
        dst = tins[group].at[slot(group, q), early[group] + r - groups[group][0]]
        remote = pltpu.make_async_remote_copy(
            src_ref=src, dst_ref=dst, send_sem=own_send_sem.at[0], recv_sem=own_sem.at[q],
            device_id={"rows": chip, "cols": core}, device_id_type=MESH,
        )
        away = (chip != r) | (core != c)
        return away, remote, lambda: pltpu.make_async_copy(src, dst, own_sem.at[q])

    def send_own(low, high):
        for group in range(3):
            @pl.when(inside[group])
            def _():
                def one(n, _):
                    away, remote, local = token_copy(group, n)

                    @pl.when(away)
                    def _():
                        remote.start()

                    @pl.when(jnp.logical_not(away))
                    def _():
                        local().start()
                    return 0

                lax.fori_loop(low * lines, high * lines, one, 0)

    def next_copy(part, p):
        p = (p + line) % lines
        return pltpu.make_async_remote_copy(
            src_ref=nown.at[:, pl.ds(pl.multiple_of(part * chunk_rows + p * rows, rows), rows)],
            dst_ref=tin_b.at[part, r], send_sem=next_send_sem.at[0], recv_sem=early_sem.at[part],
            device_id={"rows": quarter + p // cols_n, "cols": p % cols_n}, device_id_type=MESH,
        )

    def send_first(part):
        @pl.when(c == 0)
        def _():
            send_own(part, part + 1)

        @pl.when(inside[0] & (c == 0))
        def _():
            def one(p, _):
                next_copy(part, p).start()
                return 0

            lax.fori_loop(0, lines, one, 0)

    direct = 2
    send_first(0)
    fetches[2].wait()
    for part in range(1, local_chunks):
        normalise_part(part)

    def column_copy(step):
        other = (c + step) % cols_n
        return pltpu.make_async_remote_copy(
            src_ref=nown.at[pl.ds(other * per_core, per_core)], dst_ref=ncol.at[c],
            send_sem=csend_sem.at[step], recv_sem=crecv_sem.at[step],
            device_id={"cols": other}, device_id_type=MESH,
        )

    for step in range(1, cols_n):
        column_copy(step).start()

    def drain_own(group):
        count = local_chunks * (lines - 1) if group < 2 else local_chunks * lines - local_chunks // 2
        sent = nown.at[:, pl.ds(0, count * rows)]
        pltpu.make_async_copy(sent, sent, own_send_sem.at[0]).wait()

    def own_wait(group, q):
        part = tins[group].at[slot(group, q), pl.ds(early[group], groups[group][1])]
        pltpu.make_async_copy(part, part, own_sem.at[q]).wait()

    def early_wait(group, q):
        part = tins[group].at[slot(group, q), pl.ds(0, early[group])]
        pltpu.make_async_copy(part, part, early_sem.at[q]).wait()

    def relay_copy(group, q, which):
        if group == 0:
            src, dst, chip = tin_a.at[q], tin_b.at[q, pl.ds(0, quarter)], r + quarter
        else:
            src = tin_b.at[q, pl.ds(which * quarter, quarter)]
            dst = tin_c.at[q // 2, pl.ds(which * quarter, quarter)]
            chip = r + quarter + half_of(q) * quarter
        return pltpu.make_async_remote_copy(
            src_ref=src, dst_ref=dst, send_sem=relay_sem.at[q, which], recv_sem=early_sem.at[q],
            device_id={"rows": chip}, device_id_type=MESH,
        )

    def relay_own(group, q):
        own_wait(group, q)
        relay_copy(group, q, 1).start()

    def relay_early(group, q):
        early_wait(group, q)
        relay_copy(group, q, 0).start()

    def gate_part(core, normed_of):
        for w in range(per_core):
            normed = normed_of(w)
            base = pl.multiple_of(w * total + core * height, height)
            inject = transposed_dot(normed, wbc_ref[2 * states : 3 * states])
            inject = inject.astype(jnp.bfloat16).astype(jnp.float32)
            for n in range(states):
                inject_ref[pl.ds(base * states + n, height, stride=states), :] = jnp.broadcast_to(
                    inject[:, n : n + 1], (height, LANES)
                )
            read = transposed_dot(normed, spread_ref[...])
            owner = lax.broadcasted_iota(jnp.int32, read.shape, 1) // states
            here = lax.broadcasted_iota(jnp.int32, read.shape, 0) % run
            read_ref[pl.ds(base, height), :] = jnp.where(owner == here, read, 0.0).astype(jnp.bfloat16)
            for k in range(0, inner, LANE_PAIR):
                z_ref[pl.ds(base, height), k : k + LANE_PAIR] = jnp.dot(
                    normed, win_ref[:, inner + k : inner + k + LANE_PAIR],
                    preferred_element_type=jnp.float32,
                ).astype(jnp.bfloat16)

    for fetch in fetches[3:]:
        fetch.wait()

    for group, (first, chips) in enumerate(groups):
        @pl.when(inside[group])
        def _():
            def fill(d, _):
                for k in range(pairs):
                    rate = rrate_ref[:, k * LANE_PAIR : (k + 1) * LANE_PAIR]
                    table[k, d] = jnp.exp(-rate * d.astype(jnp.float32)).astype(jnp.bfloat16)
                return 0

            lax.fori_loop(0, (early[group] + chips) * columns, fill, 0)

    for i in range(run):
        spread_ref[i * states : (i + 1) * states] = wbc_ref[3 * states : 4 * states]
    crate_ref[...] = jnp.exp(-crate_ref[...])
    state_ref[...] = jnp.zeros(state_ref.shape, jnp.float32)
    gated_ref[...] = jnp.zeros(gated_ref.shape, jnp.bfloat16)
    send_first(1)
    gate_part(c, lambda w: nown[c * per_core + w])

    @pl.when(c == 0)
    def _():
        send_own(direct, local_chunks)

    @pl.when(inside[1])
    def _():
        pl.semaphore_wait(ready_sem, 2)
        relay_own(1, 0)

    for step in range(1, cols_n):
        column_copy(step).wait_recv()
        source = (c + cols_n - step) % cols_n
        gate_part(source, lambda w: ncol[source, w])

    @pl.when(c > 0)
    def _():
        send_own(0, local_chunks)

    @pl.when(inside[0])
    def _():
        def one(q, _):
            relay_own(0, q)
            return 0

        for q in range(direct):
            own_wait(0, q)
        lax.fori_loop(direct, local_chunks, one, 0)

    @pl.when(inside[1])
    def _():
        relay_early(1, 0)
        relay_own(1, 1)

    def result_copy(group, q, part, k):
        first, chips = groups[group]
        count = chips * cols_n
        k = jnp.where(k == 0, 0, (k + count // 2 - 2) % (count - 1) + 1)
        g = ((r - first) * cols_n + c + k) % count
        some = pl.ds(pl.multiple_of(part * share, share), share)
        src, dst = rsend.at[slot(group, q), g, :, :, some], rrecv.at[q, line, :, :, some]
        remote = pltpu.make_async_remote_copy(
            src_ref=src, dst_ref=dst, send_sem=rsend_sem.at[slot(group, q)], recv_sem=rrecv_sem.at[q],
            device_id={"rows": first + g // cols_n, "cols": g % cols_n}, device_id_type=MESH,
        )
        return remote, lambda: pltpu.make_async_copy(src, dst, rrecv_sem.at[q])

    def rounded(value):
        return value.astype(jnp.bfloat16).astype(jnp.float32)

    def project_in(normed, k):
        return rounded(jnp.dot(
            normed, win_ref[:, k * LANE_PAIR : (k + 1) * LANE_PAIR], preferred_element_type=jnp.float32
        ))

    def own_part(group, q):
        chips = groups[group][1]
        before = early[group]
        count = chips * columns * rows
        ready = slot(group, q) if group == 2 else 0
        if group == 2:
            own_wait(group, q)
        normed = tins[group][slot(group, q), before : before + chips].reshape(count, width)
        bown_ref[ready, :count] = rounded(transposed_dot(normed, wbc_ref[:states]))
        cown_ref[ready, :count] = rounded(transposed_dot(normed, wbc_ref[states : 2 * states]))
        for k in range(pairs):
            uown_ref[ready, k, :count] = project_in(normed, k)

    def row_chunk(group, q):
        chips = groups[group][1]
        before = early[group]
        at = slot(group, q)
        tin = tins[group]
        out_cols, pre_cols = chips * columns, before * columns
        all_cols = out_cols + pre_cols
        if group < 2:
            own_part(group, q)
        else:
            early_wait(group, q)
        ready = at if group == 2 else 0
        if before:
            normed = tin[at, :before].reshape(pre_cols * rows, width)
            b_ref[: pre_cols * rows] = rounded(transposed_dot(normed, wbc_ref[:states]))
            for k in range(pairs):
                u_ref[k, : pre_cols * rows] = project_in(normed, k)
        b_ref[pre_cols * rows : all_cols * rows] = bown_ref[ready, : out_cols * rows]

        def value_of(k, col):
            if col < pre_cols:
                return u_ref[k, col * rows : (col + 1) * rows]
            return uown_ref[ready, k, (col - pre_cols) * rows : (col - pre_cols + 1) * rows]

        def span(d):
            low = max(0, d - pre_cols)
            return low, out_cols - low, pre_cols + low - d

        for d in range(1, all_cols):
            low, count, source = span(d)
            lag_ref[d, : count * rows] = (
                cown_ref[ready, low * rows : out_cols * rows] * b_ref[source * rows : (source + count) * rows]
            ).astype(jnp.bfloat16)

        here = jnp.sum(
            cown_ref[ready, : out_cols * rows] * b_ref[pre_cols * rows : all_cols * rows], axis=1, keepdims=True
        )

        def one_pair(k):
            skip = skip_ref[k]
            sums = [
                (skip + here[o * rows : (o + 1) * rows]) * value_of(k, pre_cols + o) for o in range(out_cols)
            ]
            for d in range(1, all_cols):
                low, count, source = span(d)
                weight = jnp.dot(lag_ref[d, : count * rows], table[k, d], preferred_element_type=jnp.float32)
                for i in range(count):
                    sums[low + i] += weight[i * rows : (i + 1) * rows] * value_of(k, source + i)
            some = pl.ds(pl.multiple_of(k * LANE_PAIR, LANE_PAIR), LANE_PAIR)
            for o in range(out_cols):
                rsend[at, o // per_core, o % per_core, :, some] = sums[o].astype(jnp.bfloat16)

        def one_part(part, _):
            for k in range(pairs // parts):
                one_pair(part * (pairs // parts) + k)

            def send_result(k, _):
                result_copy(group, q, part, k)[0].start()
                return 0

            lax.fori_loop(1, chips * cols_n, send_result, 0)
            result_copy(group, q, part, 0)[1]().start()
            return 0

        lax.fori_loop(0, parts, one_part, 0)

    def out_part(core, i):
        first = pl.multiple_of(i * chunk_rows, chunk_rows)
        return out_ref.at[pl.ds(core * per_core, per_core), pl.ds(first, chunk_rows)]

    def out_copy(q):
        return pltpu.make_async_remote_copy(
            src_ref=stage.at[q], dst_ref=out_part(c, q % local_chunks),
            send_sem=osend_sem.at[q], recv_sem=orecv_sem.at[c, q % local_chunks],
            device_id={"cols": q // local_chunks}, device_id_type=MESH,
        )

    def col_chunk(q):
        pltpu.make_async_copy(rrecv.at[q], rrecv.at[q], rrecv_sem.at[q]).wait()
        for p in range(lines):
            for w in range(per_core):
                value = rrecv[q, p, w].astype(jnp.float32)
                for t in range(tiles):
                    vcol[t, w * chunk_rows + p * rows : w * chunk_rows + (p + 1) * rows] = (
                        value[:, t * LANES : (t + 1) * LANES]
                    )
        project((q + chunks - 1) % chunks)
        halves = range(0, states, SUBLANES)

        def one_run(i):
            for w in range(per_core):
                here = w * chunk_rows + i * run
                patch = pl.multiple_of(w * total + q * chunk_rows + i * run, run)
                decay = [[crate_ref[h : h + SUBLANES, t * LANES : (t + 1) * LANES] for t in range(tiles)] for h in halves]
                state = [[state_ref[w, h : h + SUBLANES, t * LANES : (t + 1) * LANES] for t in range(tiles)] for h in halves]
                for s in range(run):
                    inject = [
                        inject_ref[pl.ds(pl.multiple_of((patch + s) * states + h, SUBLANES), SUBLANES), :] for h in halves
                    ]
                    for t in range(tiles):
                        value = vcol[t, pl.ds(here + s, SUBLANES, stride=0), :]
                        for j in range(len(inject)):
                            state[j][t] = decay[j][t] * state[j][t] + inject[j] * value
                        hist[i * per_core + w, t, s * states : (s + 1) * states, :] = jnp.concatenate(
                            [state[j][t] for j in range(len(inject))], axis=0
                        ).astype(jnp.bfloat16)
                for j, h in enumerate(halves):
                    for t in range(tiles):
                        state_ref[w, h : h + SUBLANES, t * LANES : (t + 1) * LANES] = state[j][t]
                for t in range(tiles):
                    if t % 2 == 0:
                        both_tiles = jnp.concatenate([hist[i * per_core + w, t], hist[i * per_core + w, t + 1]], axis=1)
                        mixed = jnp.dot(
                            read_ref[pl.ds(patch, run), :], both_tiles, preferred_element_type=jnp.float32
                        )
                    gate = z_ref[pl.ds(patch, run), t * LANES : (t + 1) * LANES].astype(jnp.float32)
                    both = mixed[:, t % 2 * LANES : (t % 2 + 1) * LANES] + vcol[t, pl.ds(here, run), :]
                    gated_ref[q % 2, pl.ds(here, run), t * LANES : (t + 1) * LANES] = (
                        both * (gate / (1.0 + jnp.exp(-gate)))
                    ).astype(jnp.bfloat16)

        for i in range(chunk_rows // run):
            one_run(i)

        @pl.when(q > 0)
        def _():
            send_out(q - 1)

    def project(q):
        result = jnp.dot(gated_ref[q % 2], wout_ref[...], preferred_element_type=jnp.float32).astype(jnp.bfloat16)
        stage[q] = result.reshape(per_core, chunk_rows, -1)

    def send_out(q):
        home = q // local_chunks

        @pl.when(home == c)
        def _():
            pltpu.make_async_copy(stage.at[q], out_part(c, q % local_chunks), orecv_sem.at[c, q % local_chunks]).start()

        @pl.when(home != c)
        def _():
            out_copy(q).start()

    def one_chunk(q, _):
        for group in range(3):
            mine = inside[group] & (q < chunks)
            if group == 2:
                mine = mine & (half_of(q) == (r - 2 * quarter) // quarter)

            @pl.when(mine)
            def _():
                row_chunk(group, q)
                if group == 2:
                    @pl.when(q + 2 < chunks)
                    def _():
                        own_part(group, q + 2)

            if group == 0:
                @pl.when(inside[group] & (q + local_chunks < chunks))
                def _():
                    relay_own(group, q + local_chunks)
            if group == 1:
                @pl.when(inside[group] & (q + 1 < chunks))
                def _():
                    relay_early(group, q + 1)

                @pl.when(inside[group] & (q + 2 < chunks))
                def _():
                    relay_own(group, q + 2)

        @pl.when(q >= lag)
        def _():
            col_chunk(q - lag)
        return 0

    @pl.when(inside[2])
    def _():
        own_part(2, 1 - (r - 2 * quarter) // quarter)

    lag = 3
    lax.fori_loop(0, chunks + lag, one_chunk, 0)
    project(chunks - 1)
    send_out(chunks - 1)

    for group, (first, chips) in enumerate(groups):
        @pl.when(inside[group])
        def _():
            drain_own(group)

            def drain_chunk(q, _):
                relay_copy(group, q, 1).wait_send()
                if group == 1:
                    relay_copy(group, q, 0).wait_send()
                return 0

            if group == 0:
                @pl.when(c == 0)
                def _():
                    sent = nown.at[:, pl.ds(0, direct * lines * rows)]
                    pltpu.make_async_copy(sent, sent, next_send_sem.at[0]).wait()
            if group < 2:
                lax.fori_loop((direct, 0)[group], chunks, drain_chunk, 0)
            for at in range(chunks // (1 + group // 2)):
                sent = rsend.at[at, pl.ds(0, chips * cols_n - 1)]
                pltpu.make_async_copy(sent, sent, rsend_sem.at[at]).wait()

    for step in range(1, cols_n):
        column_copy(step).wait_send()

    def drain_out(q, _):
        @pl.when(q // local_chunks != c)
        def _():
            out_copy(q).wait_send()
        return 0

    lax.fori_loop(0, chunks, drain_out, 0)
    for source in range(cols_n):
        for i in range(local_chunks):
            part = out_part(source, i)
            pltpu.make_async_copy(part, part, orecv_sem.at[source, i]).wait()


def per_device_grouped(chunks, tokens, norm_gain, w_in, w_bc, rate_row, rate_col, skip_gain, w_out):
    inner, width_out = w_out.shape
    states = rate_row.shape[0]
    height, columns, width = tokens.shape
    rows_n, cols_n = lax.axis_size("rows"), lax.axis_size("cols")
    quarter = rows_n // 4
    per_core = columns // cols_n
    total = height * cols_n
    chunk_rows = total // chunks
    lines = quarter * cols_n
    rows = chunk_rows // lines
    tiles = inner // LANES
    pairs = inner // LANE_PAIR
    patches = total * per_core
    local_chunks = chunks // cols_n
    lags = rows_n * columns
    held = lags * rows
    outs = 2 * quarter * columns * rows
    f32, bf16 = jnp.float32, jnp.bfloat16
    dma = pltpu.SemaphoreType.DMA
    out = pl.pallas_call(
        functools.partial(grouped_kernel, states, rows_n, cols_n, chunks, per_core),
        in_specs=[pl.BlockSpec(memory_space=pl.ANY)] * 8,
        out_specs=pl.BlockSpec(memory_space=pl.ANY),
        out_shape=pltpu.VMEM((columns, height, width_out), bf16),
        scratch_shapes=[
            pltpu.VMEM((1, width), f32),
            pltpu.VMEM(w_in.shape, bf16),
            pltpu.VMEM(w_bc.shape[::-1], bf16),
            pltpu.VMEM(rate_row.shape, f32),
            pltpu.VMEM(rate_col.shape, f32),
            pltpu.VMEM((pairs, 1, LANE_PAIR), f32),
            pltpu.VMEM(w_out.shape, bf16),
            pltpu.VMEM((height, columns, width), bf16),
            pltpu.VMEM((columns, height, width), bf16),
            pltpu.VMEM((cols_n, per_core, height, width), bf16),
            pltpu.VMEM((chunks, quarter, columns, rows, width), bf16),
            pltpu.VMEM((chunks, 2 * quarter, columns, rows, width), bf16),
            pltpu.VMEM((chunks // 2, 4 * quarter, columns, rows, width), bf16),
            pltpu.VMEM((pairs, lags, states, LANE_PAIR), bf16),
            pltpu.VMEM((width // LANES, height * columns, LANES), f32),
            pltpu.VMEM((pairs, held, LANE_PAIR), f32),
            pltpu.VMEM((held, states), f32),
            pltpu.VMEM((chunks // 2, pairs, outs, LANE_PAIR), f32),
            pltpu.VMEM((chunks // 2, outs, states), f32),
            pltpu.VMEM((chunks // 2, outs, states), f32),
            pltpu.VMEM((lags, outs, states), bf16),
            pltpu.VMEM((chunks, 2 * lines, per_core, rows, inner), bf16),
            pltpu.VMEM((chunks, lines, per_core, rows, inner), bf16),
            pltpu.VMEM((tiles, per_core * chunk_rows + SUBLANES, LANES), f32),
            pltpu.VMEM((patches * states, LANES), f32),
            pltpu.VMEM((LANE_PAIR, width), bf16),
            pltpu.VMEM((patches, LANE_PAIR), bf16),
            pltpu.VMEM((per_core * chunk_rows * states // LANE_PAIR, tiles, LANE_PAIR, LANES), bf16),
            pltpu.VMEM((patches, inner), bf16),
            pltpu.VMEM((2, per_core * chunk_rows, inner), bf16),
            pltpu.VMEM((chunks, per_core, chunk_rows, width_out), bf16),
            pltpu.VMEM((per_core, states, inner), f32),
            dma((1,)), dma((1,)), dma((chunks,)), dma((chunks,)), dma((chunks, 2)),
            dma((cols_n,)), dma((cols_n,)),
            dma((chunks,)), dma((chunks,)), dma((chunks,)),
            dma((cols_n, local_chunks)), dma((9,)), pltpu.SemaphoreType.REGULAR,
        ],
        compiler_params=pltpu.CompilerParams(
            vmem_limit_bytes=VMEM_LIMIT, collective_id=0, has_side_effects=True
        ),
        name="layer",
    )(
        tokens, norm_gain[None], w_in, w_bc.T, rate_row, rate_col,
        skip_gain.reshape(pairs, 1, LANE_PAIR), w_out,
    )
    return out.transpose(1, 0, 2)


def chunk_count(tokens, rate_row, inner):
    height, columns, _ = tokens.shape
    states = rate_row.shape[0]
    rows_n, cols_n = lax.axis_size("rows"), lax.axis_size("cols")
    total = height * cols_n
    if rows_n % 4 or columns % cols_n or inner % LANE_PAIR or states % SUBLANES or LANE_PAIR % states:
        return 0
    step = rows_n // 4 * cols_n * SUBLANES
    run = LANE_PAIR // states
    if total % step or step % run or total // step % (2 * cols_n):
        return 0
    return total // step


def per_device(tokens, norm_gain, w_in, w_bc, rate_row, rate_col, skip_gain, w_out):
    args = (tokens, norm_gain, w_in, w_bc, rate_row, rate_col, skip_gain, w_out)
    chunks = chunk_count(tokens, rate_row, w_out.shape[0])
    if chunks:
        return per_device_grouped(chunks, *args)
    return per_device_uniform(*args)


def solution(mesh):
    placed = (P(("slides", "cols"), "rows", None), P(), P(), P(), P(), P(), P(), P())
    return jax.shard_map(
        per_device,
        mesh=mesh,
        in_specs=placed,
        out_specs=P(("slides", "cols"), "rows", None),
        check_vma=False,
    )
```
